32 devices in a mesh: wide: 16 (over z, y, x), narrow: 2 (over core).
Axes of the slice: x: 2, y: 2, z: 4, core: 2. Of those that a mesh axis runs over, the one named last changes fastest.
Arguments:
- inputs: bfloat16 [16384, 768], P(('wide', 'narrow')), may hold values from -6 to 6
- memory: bfloat16 [4096, 768], P(('wide', 'narrow')), may hold values from -6 to 6
- cotangent: bfloat16 [16384, 768], P(('wide', 'narrow')), may hold values from -6 to 6
- answer_lengths: int32 [16, 8], replicated, may hold values from 1 to 256, 1024 in all within a row
- answer_groups: int32 [16, 8], replicated, may hold values from 0 to 15
- memory_lengths: int32 [16, 16], replicated, may hold values from 1 to 64, 256 in all within a row
- gain_attn: bfloat16 [768], replicated, may hold values from 0.5 to 1.5
- self_query: bfloat16 [768, 768], replicated, may hold values from -0.109375 to 0.109375
- self_key: bfloat16 [768, 768], replicated, may hold values from -0.109375 to 0.109375
- self_value: bfloat16 [768, 768], replicated, may hold values from -0.21875 to 0.21875
- self_out: bfloat16 [768, 768], replicated, may hold values from -0.875 to 0.875
- bucket_bias_table: bfloat16 [32, 12], replicated, may hold values from -4 to 4
- gain_cross: bfloat16 [768], replicated, may hold values from 0.5 to 1.5
- cross_query: bfloat16 [768, 768], replicated, may hold values from -0.109375 to 0.109375
- cross_key_matrix: bfloat16 [768, 768], replicated, may hold values from -0.109375 to 0.109375
- cross_value: bfloat16 [768, 768], replicated, may hold values from -0.21875 to 0.21875
- cross_out: bfloat16 [768, 768], replicated, may hold values from -0.875 to 0.875
- gain_ffn: bfloat16 [768], replicated, may hold values from 0.5 to 1.5
- hidden_gate: bfloat16 [768, 2048], replicated, may hold values from -0.21875 to 0.21875
- hidden_up: bfloat16 [768, 2048], replicated, may hold values from -0.21875 to 0.21875
- hidden_down: bfloat16 [2048, 768], replicated, may hold values from -0.125 to 0.125
Outputs:
- layer_out: bfloat16 [16384, 768], P(('wide', 'narrow'))
- input_grad: float32 [16384, 768], P(('wide', 'narrow'))
- memory_grad: float32 [4096, 768], P(('wide', 'narrow'))
- grad_gain_attn: float32 [768], P('wide')
- grad_self_query: float32 [768, 768], P('wide')
- grad_self_key: float32 [768, 768], P('wide')
- grad_self_value: float32 [768, 768], P('wide')
- grad_self_out: float32 [768, 768], P('wide')
- grad_position_table: float32 [32, 12], P('wide')
- grad_gain_cross: float32 [768], P('wide')
- grad_cross_query: float32 [768, 768], P('wide')
- grad_cross_key: float32 [768, 768], P('wide')
- grad_cross_value: float32 [768, 768], P('wide')
- grad_cross_out: float32 [768, 768], P('wide')
- grad_gain_ffn: float32 [768], P('wide')
- grad_hidden_gate: float32 [768, 2048], P('wide')
- grad_hidden_up: float32 [768, 2048], P('wide')
- down_hidden_gradient: float32 [2048, 768], P('wide')
The draws below stay inside these ranges and needn't reach their ends.
Inputs may be any that keep to these rules, and one draw needn't show every extreme that they name: `answer_lengths`: in each row the 8 answer lengths sum to 1024. `memory_lengths`: in each memory the 16 group lengths sum to 256.
All inputs are finite; a program needn't handle non-finite values.
Results may differ from the reference program's by a relative error of at most 0.029.
Values may be sent and summed in bfloat16 or wider, within the bound.
No kernel may reach another device: no remote copies, remote signals or barrier semaphores. Data moves between devices by JAX's collectives and lax.ppermute only.
A program may use at most 192 MiB of HBM per device.

```python
import math
import jax
import jax.numpy as jnp
import numpy as np
from jax import lax

D = 768
HEADS = 12
HEAD_DIM = 64
FF = 2048
BUCKETS = 32
MAX_DIST = 128
SEQ_LEN = 1024
ANSWERS = 8
GROUPS = 16
INNER = 768
PER_MEMORY = 1
MEMORIES = 16
MEM = 256
ROWS = 16
TOKENS = 16384


def touch_ends(array, own_key, smallest, high):
    dims = array.shape
    index_at = [jax.random.randint(jax.random.fold_in(own_key, axis), (), 0, dims[axis]) for axis in range(len(dims))]
    array = array.at[tuple(index_at)].set(smallest)
    longest = dims.index(max(dims))
    index_at[longest] = (index_at[longest] + 1) % dims[longest]
    return array.at[tuple(index_at)].set(high)


def raised(drawn, rng, source, target, parts, factor):
    owner, partner = [(jnp.arange(drawn.shape[axis_at]) // (drawn.shape[axis_at] // parts)).reshape([-1 if axis == axis_at else 1 for axis in range(drawn.ndim)]) for axis_at in (source, target)]
    chosen = jax.random.permutation(rng, parts)[partner]
    strong = (owner == chosen) | (owner == (partner + parts // 2) % parts)
    return jnp.where(strong, factor * drawn, drawn)


def block_scale(stream_key, extent, pieces, least, largest):
    factor_of, own = 1.0, jax.random.fold_in(stream_key, 6)
    for axis_at, shards_of in pieces:
        draws = jnp.exp(jax.random.uniform(jax.random.fold_in(own, axis_at), (shards_of,), jnp.float32, least / len(pieces), largest / len(pieces)))
        factor_of = factor_of * jnp.repeat(draws, extent[axis_at] // shards_of).reshape([-1 if axis == axis_at else 1 for axis in range(len(extent))])
    return factor_of


def split_up(amount, total, bound, skew):
    loads = [(1 << 20) // math.isqrt(grade ** skew) + 1 for grade in range(2, amount + 1)]
    spare, counts = total - bound - (amount - 1), [1] * (amount - 1)
    while spare > 0:
        free = [i for i in range(amount - 1) if counts[i] < bound]
        mass, budget = sum([loads[i] for i in free]), spare
        for i in free:
            more = min(bound - counts[i], max(1, budget * loads[i] // mass), spare)
            counts[i] = counts[i] + more
            spare = spare - more
    return np.array([bound] + counts)


def ragged_sizes(stream_key, count, total, most, lean):
    if count == 2:
        one = jax.random.randint(stream_key, (), max(1, total - most), min(most, total - 1) + 1)
        return jnp.stack([one, total - one])
    tallies = jnp.asarray(split_up(count, total, most, lean), jnp.int32)
    twos = (count - 1) // 2
    giver, sink = tallies[1:1 + 2 * twos:2], tallies[2:2 + 2 * twos:2]
    margin = jnp.minimum(giver - 1, most - sink)
    moved = jax.random.randint(jax.random.fold_in(stream_key, 1), (twos,), 0, 1 << 20) % (margin + 1)
    tallies = tallies.at[1:1 + 2 * twos:2].set(giver - moved).at[2:2 + 2 * twos:2].set(sink + moved)
    return tallies[jax.random.permutation(jax.random.fold_in(stream_key, 2), count)]


def normal_values(key, extent, spread, reach, shards=(), kind=jnp.bfloat16):
    entries = spread * jax.random.normal(key, extent, jnp.float32)
    if shards:
        entries = entries * block_scale(key, extent, shards, -0.22, 0.18)
    return jnp.clip(entries, -reach, reach).astype(kind)


def bell_draw_with(rng, extent, width, bound, split, heavy, kind=jnp.bfloat16):
    entries = width * jax.random.normal(rng, extent, jnp.float32)
    if split:
        entries = entries * block_scale(rng, extent, split, -0.22, 0.18)
    return jnp.clip(raised(entries, jax.random.fold_in(rng, 3), *heavy), -bound, bound).astype(kind)


def setup_inputs(seed: int = 0) -> dict:
    arg_keys = jax.random.split(jax.random.key(seed), 22)
    inputs = normal_values(arg_keys[0], (TOKENS, D), 1.0, 6.0, ((0, 32),))
    memory = normal_values(arg_keys[1], (MEMORIES * MEM, D), 1.0, 6.0, ((0, 32),))
    cotangent = bell_draw_with(arg_keys[2], (TOKENS, D), 1.0, 6.0, ((0, 32),), (0, 1, 32, 2.75))
    answer_lengths = jax.vmap(lambda own: ragged_sizes(own, ANSWERS, SEQ_LEN, SEQ_LEN // 4, 2))(jax.random.split(arg_keys[3], ROWS)).reshape((ROWS, ANSWERS)).astype(jnp.int32)
    answer_groups = touch_ends(jax.random.randint(arg_keys[4], (ROWS, ANSWERS), 0, GROUPS), jax.random.fold_in(arg_keys[4], 1), 0, GROUPS - 1).astype(jnp.int32)
    memory_lengths = jax.vmap(lambda own: ragged_sizes(own, GROUPS, MEM, MEM // 4, 2))(jax.random.split(arg_keys[5], MEMORIES)).reshape((MEMORIES, GROUPS)).astype(jnp.int32)
    gain_attn = jnp.clip(1.0 + 0.1 * jax.random.normal(arg_keys[6], (D,), jnp.float32), 0.5, 1.5).astype(jnp.bfloat16)
    self_query = normal_values(arg_keys[7], (D, INNER), (4 * D) ** -0.5, 0.109375)
    self_key = normal_values(arg_keys[8], (D, INNER), (4 * D) ** -0.5, 0.109375)
    self_value = normal_values(arg_keys[9], (D, INNER), D ** -0.5, 0.21875)
    self_out = normal_values(arg_keys[10], (INNER, D), (D // 16) ** -0.5, 0.875)
    bucket_bias_table = normal_values(arg_keys[11], (BUCKETS, HEADS), 1.0, 4.0)
    gain_cross = jnp.clip(1.0 + 0.1 * jax.random.normal(arg_keys[12], (D,), jnp.float32), 0.5, 1.5).astype(jnp.bfloat16)
    cross_query = normal_values(arg_keys[13], (D, INNER), (4 * D) ** -0.5, 0.109375)
    cross_key_matrix = normal_values(arg_keys[14], (D, INNER), (4 * D) ** -0.5, 0.109375)
    cross_value = normal_values(arg_keys[15], (D, INNER), D ** -0.5, 0.21875)
    cross_out = normal_values(arg_keys[16], (INNER, D), (D // 16) ** -0.5, 0.875)
    gain_ffn = jnp.clip(1.0 + 0.1 * jax.random.normal(arg_keys[17], (D,), jnp.float32), 0.5, 1.5).astype(jnp.bfloat16)
    hidden_gate = normal_values(arg_keys[18], (D, FF), D ** -0.5, 0.21875)
    hidden_up = normal_values(arg_keys[19], (D, FF), D ** -0.5, 0.21875)
    hidden_down = normal_values(arg_keys[20], (FF, D), FF ** -0.5, 0.125)
    return dict(inputs=inputs, memory=memory, cotangent=cotangent, answer_lengths=answer_lengths, answer_groups=answer_groups, memory_lengths=memory_lengths, gain_attn=gain_attn, self_query=self_query, self_key=self_key, self_value=self_value, self_out=self_out, bucket_bias_table=bucket_bias_table, gain_cross=gain_cross, cross_query=cross_query, cross_key_matrix=cross_key_matrix, cross_value=cross_value, cross_out=cross_out, gain_ffn=gain_ffn, hidden_gate=hidden_gate, hidden_up=hidden_up, hidden_down=hidden_down)


@jax.custom_vjp
def low(v):
    return lax.optimization_barrier(v.astype(jnp.bfloat16)).astype(jnp.float32)

@jax.custom_vjp
def low_back(v):
    return v

def low_keep(v):
    return (low(v), None)

def low_pass(kept, grad):
    return (grad,)

def back_keep(v):
    return (v, None)

def back_low(kept, grad):
    return (low(grad),)
low.defvjp(low_keep, low_pass)
low_back.defvjp(back_keep, back_low)
epsilon = 1e-06
neg_big = -1e+30

def rounded_both(values):
    return low_back(low(values))

def matmul_high(left, right):
    return jnp.dot(left, right, precision=lax.Precision.HIGHEST, preferred_element_type=jnp.float32)

def rms_scale(values, gain_row):
    factor = lax.rsqrt(lax.optimization_barrier(jnp.mean(values * values, axis=-1, keepdims=True)) + epsilon)
    return values * factor * gain_row

def segment_of(positions, lengths):
    segment_ends = jnp.cumsum(lengths)[:-1]
    return lax.optimization_barrier(jnp.sum((positions[:, None] >= segment_ends[None, :]).astype(jnp.int32), axis=1))

def bucket_of(distance):
    exact_count = BUCKETS // 2
    log_count = BUCKETS - exact_count
    near_part = jnp.minimum(jnp.maximum(distance, 0), exact_count)
    far_part = jnp.zeros_like(distance)
    for level_index in range(1, log_count):
        edge_value = math.ceil(exact_count * (MAX_DIST / exact_count) ** (level_index / log_count))
        far_part = far_part + (distance >= edge_value).astype(jnp.int32)
    return near_part + far_part

def attend_heads(query_rows, key_rows, value_row_block, allowed, position_bias):
    query_heads = query_rows.reshape(query_rows.shape[0], HEADS, HEAD_DIM)
    key_heads = key_rows.reshape(key_rows.shape[0], HEADS, HEAD_DIM)
    value_heads = value_row_block.reshape(value_row_block.shape[0], HEADS, HEAD_DIM)
    scores = jnp.einsum('qhd,khd->hqk', query_heads, key_heads, precision=lax.Precision.HIGHEST)
    scores = low_back(scores + position_bias)
    scores = jnp.where(allowed[None], scores, neg_big)
    probs_full = jax.nn.softmax(scores, axis=-1)
    attended = jnp.einsum('hqk,khd->qhd', low(probs_full), value_heads, precision=lax.Precision.HIGHEST)
    return rounded_both(attended.reshape(query_rows.shape[0], HEADS * HEAD_DIM))

def decoder_row(params, memory_keys, memory_values, memory_segments, row_inputs, lengths_row, groups_row):
    gain_attn, self_query, self_key, self_value, self_out, bucket_bias_table, gain_cross, cross_query, cross_key_matrix, cross_value, cross_out, gain_ffn, hidden_gate, hidden_up, hidden_down = params
    positions = jnp.arange(SEQ_LEN, dtype=jnp.int32)
    segments = segment_of(positions, lengths_row)
    answer_index = jnp.arange(ANSWERS, dtype=jnp.int32)
    row_groups = lax.optimization_barrier(jnp.sum(jnp.where(segments[:, None] == answer_index[None, :], groups_row[None, :], 0), axis=1))
    normed = low(rms_scale(row_inputs, gain_attn))
    queries = rounded_both(matmul_high(normed, self_query))
    keys_row = rounded_both(matmul_high(normed, self_key))
    values_row = rounded_both(matmul_high(normed, self_value))
    buckets = bucket_of(positions[:, None] - positions[None, :])
    position_bias = jnp.transpose(jnp.take(bucket_bias_table, buckets, axis=0), (2, 0, 1))
    allowed = (positions[None, :] <= positions[:, None]) & (segments[None, :] == segments[:, None])
    attended = attend_heads(queries, keys_row, values_row, allowed, position_bias)
    residual_one = row_inputs + low_back(matmul_high(attended, self_out))
    normed_two = low(rms_scale(residual_one, gain_cross))
    cross_rows = rounded_both(matmul_high(normed_two, cross_query))
    cross_allowed = row_groups[:, None] == memory_segments[None, :]
    attended_two = attend_heads(cross_rows, memory_keys, memory_values, cross_allowed, 0.0)
    residual_two = residual_one + low_back(matmul_high(attended_two, cross_out))
    normed_three = low(rms_scale(residual_two, gain_ffn))
    gate_pre = low_back(matmul_high(normed_three, hidden_gate))
    up_pre = low_back(matmul_high(normed_three, hidden_up))
    hidden = low(jax.nn.gelu(gate_pre, approximate=True) * up_pre)
    return residual_two + low_back(matmul_high(hidden, hidden_down))

def decoder_group(params, group_inputs, group_memory, group_lengths, group_answers, group_bounds):
    memory_keys = rounded_both(matmul_high(group_memory, params[8]))
    memory_values = rounded_both(matmul_high(group_memory, params[9]))
    memory_segments = segment_of(jnp.arange(MEM, dtype=jnp.int32), group_bounds)
    row_step = jax.checkpoint(decoder_row)
    return lax.map(lambda row_args: row_step(params, memory_keys, memory_values, memory_segments, row_args[0], row_args[1], row_args[2]), (group_inputs, group_lengths, group_answers))

def reference(inputs, memory, cotangent, answer_lengths, answer_groups, memory_lengths, gain_attn, self_query, self_key, self_value, self_out, bucket_bias_table, gain_cross, cross_query, cross_key_matrix, cross_value, cross_out, gain_ffn, hidden_gate, hidden_up, hidden_down):
    weights_low = (gain_attn, self_query, self_key, self_value, self_out, bucket_bias_table, gain_cross, cross_query, cross_key_matrix, cross_value, cross_out, gain_ffn, hidden_gate, hidden_up, hidden_down)
    params = tuple((weight.astype(jnp.float32) for weight in weights_low))
    group_inputs = inputs.astype(jnp.float32).reshape(MEMORIES, PER_MEMORY, SEQ_LEN, D)
    group_memory = memory.astype(jnp.float32).reshape(MEMORIES, MEM, D)
    group_lengths = answer_lengths.reshape(MEMORIES, PER_MEMORY, ANSWERS)
    group_answers = answer_groups.reshape(MEMORIES, PER_MEMORY, ANSWERS)

    def forward(inputs_all, memory_all, *param_list):
        group_step = jax.checkpoint(decoder_group)
        return lax.map(lambda group_args: group_step(tuple(param_list), group_args[0], group_args[1], group_args[2], group_args[3], group_args[4]), (inputs_all, memory_all, group_lengths, group_answers, memory_lengths))
    layer_f32, pull_back = jax.vjp(forward, group_inputs, group_memory, *params)
    gradients = pull_back(cotangent.astype(jnp.float32).reshape(MEMORIES, PER_MEMORY, SEQ_LEN, D))
    layer_out = layer_f32.reshape(TOKENS, D).astype(jnp.bfloat16)
    input_grad = gradients[0].reshape(TOKENS, D)
    memory_grad = gradients[1].reshape(MEMORIES * MEM, D)
    return (layer_out, input_grad, memory_grad, gradients[2], gradients[3], gradients[4], gradients[5], gradients[6], gradients[7], gradients[8], gradients[9], gradients[10], gradients[11], gradients[12], gradients[13], gradients[14], gradients[15], gradients[16])
```

```python
import functools
import math

import jax
import jax.numpy as jnp
from jax import lax
from jax.experimental import pallas as pl
from jax.experimental.pallas import tpu as pltpu
from jax.sharding import PartitionSpec as P

HEADS = 12
HEAD_DIM = 64
BUCKETS = 32
MAX_DIST = 128
ANSWERS = 8
GROUPS = 16
PAIR = 2 * HEAD_DIM
PAIRS = HEADS // 2
REACH = 256
QUERY_BLOCK = 128
WINDOW = REACH + QUERY_BLOCK
CROSS_BLOCK = 256
LANES = 128
HEADER = 8
VMEM_BYTES = 56 * 2**20

epsilon = 1e-06
neg_big = -1e30
f32 = jnp.float32
bf16 = jnp.bfloat16


def mm(left, right):
    return jnp.dot(left, right, preferred_element_type=f32)


def mm_t(left, right):
    return lax.dot_general(left, right, (((1,), (1,)), ((), ())), preferred_element_type=f32)


def rms(values, gain_row):
    factor = lax.rsqrt(jnp.mean(values * values, axis=-1, keepdims=True) + epsilon)
    return values * factor * gain_row


def rms_back(values, gain_row, grad):
    factor = lax.rsqrt(jnp.mean(values * values, axis=-1, keepdims=True) + epsilon)
    unit = values * factor
    scaled = grad * gain_row
    center = jnp.mean(scaled * unit, axis=-1, keepdims=True)
    return factor * (scaled - unit * center), jnp.sum(grad * unit, axis=0, keepdims=True)


def bucket_of(distance):
    exact_count = BUCKETS // 2
    log_count = BUCKETS - exact_count
    near_part = jnp.minimum(jnp.maximum(distance, 0), exact_count)
    far_part = jnp.zeros_like(distance)
    for level_index in range(1, log_count):
        edge = math.ceil(exact_count * (MAX_DIST / exact_count) ** (level_index / log_count))
        far_part = far_part + (distance >= edge).astype(jnp.int32)
    return near_part + far_part


def iota(shape, axis):
    return lax.broadcasted_iota(jnp.int32, shape, axis)


def low_lanes(shape):
    return iota(shape, len(shape) - 1) < HEAD_DIM


def stack_heads(rows):
    low = low_lanes(rows.shape)
    zero = jnp.zeros_like(rows)
    return jnp.concatenate([jnp.where(low, rows, zero), jnp.where(low, zero, rows)], axis=0)


def stack_heads_t(columns):
    low = iota(columns.shape, 0) < HEAD_DIM
    zero = jnp.zeros_like(columns)
    return jnp.concatenate([jnp.where(low, columns, zero), jnp.where(low, zero, columns)], axis=1)


def join_heads(stacked):
    half = stacked.shape[0] // 2
    return jnp.where(low_lanes((half, PAIR)), stacked[:half], stacked[half:])


def offset_bucket():
    lane = iota((1, 4 * QUERY_BLOCK), 1)
    distance = jnp.where(lane < WINDOW, REACH - lane, REACH + 4 * QUERY_BLOCK - lane)
    chosen = iota((BUCKETS, 4 * QUERY_BLOCK), 0) == bucket_of(distance)
    return distance, chosen


def answer_ends(lengths, row):
    total, ends = lengths[row, 0], []
    for index in range(1, ANSWERS):
        ends.append(total)
        total = total + lengths[row, index]
    return ends


def memory_kernel(memory_ref, key_ref, value_ref, out_ref):
    rows = memory_ref[...]
    out_ref[0] = mm(rows, key_ref[...]).astype(bf16)
    out_ref[1] = mm(rows, value_ref[...]).astype(bf16)


def project_kernel(x_ref, gain_ref, wq_ref, wk_ref, wv_ref, h_ref, q_ref, k_ref, v_ref, tail_ref):
    @pl.when(pl.program_id(0) == 0)
    def _():
        h_ref[...] = rms(x_ref[...].astype(f32), gain_ref[...].astype(f32)).astype(bf16)

    rows = h_ref[...]
    q_ref[...] = mm(rows, wq_ref[...]).astype(bf16)
    k_ref[...] = mm(rows, wk_ref[...]).astype(bf16)
    v_ref[...] = mm(rows, wv_ref[...]).astype(bf16)
    tokens = h_ref.shape[0]
    tail_ref[0] = k_ref[tokens - REACH :, :]
    tail_ref[1] = v_ref[tokens - REACH :, :]


def self_forward_kernel(
    info, lengths,
    q_ref, k_ref, v_ref, halo_ref, table_ref, x_ref, wo_ref, gain_ref, wq_ref,
    o_ref, inv_ref, e_ref, x1_ref, h2_ref, qc_ref,
    keys, values, base, bias, reach,
):
    step = pl.program_id(0)
    tokens = q_ref.shape[0]

    @pl.when(step == 0)
    def _():
        distance, chosen = offset_bucket()
        found = lax.dot_general(
            table_ref[...], chosen.astype(bf16), (((0,), (0,)), ((), ())),
            preferred_element_type=f32,
        )
        base[0:HEADS] = jnp.where(distance < 0, neg_big, found)
        place = info[2] * tokens + iota((tokens, LANES), 0)
        start = jnp.zeros_like(place)
        for end in answer_ends(lengths, info[3]):
            start = jnp.where(place >= end, end, start)
        reach[...] = place - start
        values[:, PAIR:] = jnp.ones((values.shape[0], PAIR), bf16)
        x1_ref[...] = x_ref[...].astype(f32)

    keys[0:REACH] = halo_ref[0]
    keys[REACH:] = k_ref[...]
    values[0:REACH, 0:PAIR] = halo_ref[1]
    values[REACH:, 0:PAIR] = v_ref[...]
    for head in range(2):
        row = base[pl.ds(2 * step + head, 1), :]
        spread = jnp.broadcast_to(row, (QUERY_BLOCK, 4 * QUERY_BLOCK))
        skewed = pltpu.roll(spread, 0, 1, stride=1, stride_axis=0)
        bias[head * QUERY_BLOCK : (head + 1) * QUERY_BLOCK] = skewed[:, :WINDOW]

    distance = REACH + iota((QUERY_BLOCK, WINDOW), 0) - iota((QUERY_BLOCK, WINDOW), 1)
    distance = jnp.concatenate([distance, distance], axis=0)
    for block in range(tokens // QUERY_BLOCK):
        rows = slice(block * QUERY_BLOCK, (block + 1) * QUERY_BLOCK)
        window = slice(block * QUERY_BLOCK, block * QUERY_BLOCK + WINDOW)
        scores = mm_t(stack_heads(q_ref[rows, :]), keys[window, :])
        own_reach = reach[rows, 0:1]
        own_reach = jnp.concatenate([own_reach, own_reach], axis=0)
        scores = jnp.where(distance <= own_reach, scores + bias[...], neg_big)
        top = jnp.max(scores, axis=-1, keepdims=True)
        weights = jnp.exp(scores - top).astype(bf16)
        e_ref[0, block] = weights
        mixed = mm(weights, values[window, :])
        inverse = 1.0 / mixed[:, PAIR:]
        o_ref[rows, :] = join_heads(mixed[:, :PAIR] * inverse).astype(bf16)
        inv_ref[rows, :] = join_heads(inverse)
    x1_ref[...] += mm(o_ref[...], wo_ref[...])

    @pl.when(step == PAIRS - 1)
    def _():
        h2_ref[...] = rms(x1_ref[...], gain_ref[...].astype(f32)).astype(bf16)
        qc_ref[...] = mm(h2_ref[...], wq_ref[...]).astype(bf16)


def cross_forward_kernel(chunks, info, lengths, groups, bounds, *refs):
    q_ref, x1_ref, wo_ref, gain_ref = refs[:4]
    kv_refs = refs[4 : 4 + chunks]
    o_ref, inv_ref, e_ref, x2_ref, h3_ref = refs[4 + chunks : 9 + chunks]
    keys, values, query_group, key_group = refs[9 + chunks :]
    step = pl.program_id(0)
    tokens = q_ref.shape[0]
    part = kv_refs[0].shape[1]

    @pl.when(step == 0)
    def _():
        place = info[2] * tokens + iota((tokens, LANES), 0)
        group = jnp.zeros_like(place) + groups[info[3], 0]
        for index, end in enumerate(answer_ends(lengths, info[3])):
            group = jnp.where(place >= end, groups[info[3], index + 1], group)
        query_group[...] = group
        total, ends = bounds[info[0], 0], []
        for index in range(1, GROUPS):
            ends.append(total)
            total = total + bounds[info[0], index]
        for chunk in range(chunks):
            owner = lax.rem(info[4] + chunks - chunk, chunks)
            token = owner * part + iota((8, part), 1)
            found = jnp.zeros_like(token)
            for end in ends:
                found = found + (token >= end).astype(jnp.int32)
            key_group[:, chunk * part : (chunk + 1) * part] = found
        values[:, PAIR:] = jnp.ones((values.shape[0], PAIR), bf16)
        x2_ref[...] = x1_ref[...]

    for chunk in range(chunks):
        keys[chunk * part : (chunk + 1) * part] = kv_refs[chunk][0]
        values[chunk * part : (chunk + 1) * part, 0:PAIR] = kv_refs[chunk][1]
    for block in range(tokens // CROSS_BLOCK):
        rows = slice(block * CROSS_BLOCK, (block + 1) * CROSS_BLOCK)
        scores = mm_t(stack_heads(q_ref[rows, :]), keys[...])
        own_group = query_group[rows, 0:1]
        own_group = jnp.concatenate([own_group, own_group], axis=0)
        scores = jnp.where(own_group == key_group[0:1, :], scores, neg_big)
        top = jnp.max(scores, axis=-1, keepdims=True)
        weights = jnp.exp(scores - top).astype(bf16)
        e_ref[0, block] = weights
        mixed = mm(weights, values[...])
        inverse = 1.0 / mixed[:, PAIR:]
        o_ref[rows, :] = join_heads(mixed[:, :PAIR] * inverse).astype(bf16)
        inv_ref[rows, :] = join_heads(inverse)
    x2_ref[...] += mm(o_ref[...], wo_ref[...])

    @pl.when(step == PAIRS - 1)
    def _():
        h3_ref[...] = rms(x2_ref[...], gain_ref[...].astype(f32)).astype(bf16)


def ffn_kernel(
    h_ref, c_ref, x2_ref, gain_ref, wg_ref, wu_ref, wd_ref,
    u_ref, dga_ref, dgb_ref, out_ref, dx_ref, e_ref, gg_ref,
    total, dh,
):
    step = pl.program_id(0)
    gate = mm(h_ref[...], wg_ref[...])
    up = mm(h_ref[...], wu_ref[...])
    du = mm_t(c_ref[...], wd_ref[...])
    root = math.sqrt(2.0 / math.pi)
    square = gate * gate
    bent = jnp.tanh(root * gate * (1.0 + 0.044715 * square))
    share = 0.5 * (1.0 + bent)
    active = gate * share
    slope = share + 0.5 * gate * (1.0 - bent * bent) * (root * (1.0 + 3 * 0.044715 * square))
    u_ref[...] = (active * up).astype(bf16)
    dgb_ref[...] = (du * active).astype(bf16)
    dga_ref[...] = (du * up * slope).astype(bf16)
    out_part = mm(u_ref[...], wd_ref[...])
    dh_part = mm_t(dga_ref[...], wg_ref[...]) + mm_t(dgb_ref[...], wu_ref[...])

    @pl.when(step == 0)
    def _():
        total[...] = x2_ref[...] + out_part
        dh[...] = dh_part

    @pl.when(step > 0)
    def _():
        total[...] += out_part
        dh[...] += dh_part

    @pl.when(step == pl.num_programs(0) - 1)
    def _():
        out_ref[...] = total[...].astype(bf16)
        back, gain_grad = rms_back(x2_ref[...], gain_ref[...].astype(f32), dh[...])
        dx_ref[...] = c_ref[...].astype(f32) + back
        e_ref[...] = dx_ref[...].astype(bf16)
        gg_ref[...] = gain_grad


def cross_backward_kernel(chunks, *refs):
    e2_ref, wo_ref, o_ref, inv_ref, p_ref, q_ref, wq_ref, x1_ref, dx2_ref, gain_ref = refs[:10]
    kv_refs = refs[10 : 10 + chunks]
    dq_ref, dx_ref, e1_ref, gg_ref = refs[10 + chunks : 14 + chunks]
    dkv_refs = refs[14 + chunks : 14 + 2 * chunks]
    keys, values, dk, dv, dh = refs[14 + 2 * chunks :]
    step = pl.program_id(0)
    tokens = q_ref.shape[0]
    part = kv_refs[0].shape[1]

    for chunk in range(chunks):
        keys[chunk * part : (chunk + 1) * part] = kv_refs[chunk][0]
        values[chunk * part : (chunk + 1) * part] = kv_refs[chunk][1]
    grad = mm_t(e2_ref[...], wo_ref[...]).astype(bf16).astype(f32)
    grad = (grad * inv_ref[...]).astype(bf16)
    query_t = q_ref[...].T
    grad_t = grad.T
    for block in range(tokens // CROSS_BLOCK):
        rows = slice(block * CROSS_BLOCK, (block + 1) * CROSS_BLOCK)
        own = grad[rows, :]
        weighed = own.astype(f32) * o_ref[rows, :].astype(f32)
        center = jnp.sum(stack_heads(weighed), axis=-1, keepdims=True)
        grad_probs = mm_t(stack_heads(own), values[...])
        weights = p_ref[0, block]
        grad_scores = (weights.astype(f32) * (grad_probs - center)).astype(bf16)
        dq_ref[rows, :] = join_heads(mm(grad_scores, keys[...])).astype(bf16)
        dk_part = mm(stack_heads_t(query_t[:, rows]), grad_scores)
        dv_part = mm(stack_heads_t(grad_t[:, rows]), weights)
        if block == 0:
            dk[...] = dk_part
            dv[...] = dv_part
        else:
            dk[...] += dk_part
            dv[...] += dv_part
    dk_rows = dk[...].T.astype(bf16)
    dv_rows = dv[...].T.astype(bf16)
    for chunk in range(chunks):
        dkv_refs[chunk][0] = dk_rows[chunk * part : (chunk + 1) * part]
        dkv_refs[chunk][1] = dv_rows[chunk * part : (chunk + 1) * part]
    dh_part = mm_t(dq_ref[...], wq_ref[...])

    @pl.when(step == 0)
    def _():
        dh[...] = dh_part

    @pl.when(step > 0)
    def _():
        dh[...] += dh_part

    @pl.when(step == PAIRS - 1)
    def _():
        back, gain_grad = rms_back(x1_ref[...], gain_ref[...].astype(f32), dh[...])
        dx_ref[...] = dx2_ref[...] + back
        e1_ref[...] = dx_ref[...].astype(bf16)
        gg_ref[...] = gain_grad


def self_backward_kernel(
    e1_ref, wo_ref, o_ref, inv_ref, p_ref, q_ref, k_ref, v_ref, halo_ref,
    dq_ref, dk_ref, dv_ref, back_ref, table_ref,
    keys, values, dk, dv, by_offset, offsets,
):
    step = pl.program_id(0)
    tokens = q_ref.shape[0]
    keys[0:REACH] = halo_ref[0]
    keys[REACH:] = k_ref[...]
    values[0:REACH] = halo_ref[1]
    values[REACH:] = v_ref[...]
    grad = mm_t(e1_ref[...], wo_ref[...]).astype(bf16).astype(f32)
    grad = (grad * inv_ref[...]).astype(bf16)
    query_t = q_ref[...].T
    grad_t = grad.T
    dk[...] = jnp.zeros_like(dk)
    dv[...] = jnp.zeros_like(dv)
    for block in range(tokens // QUERY_BLOCK):
        rows = slice(block * QUERY_BLOCK, (block + 1) * QUERY_BLOCK)
        window = slice(block * QUERY_BLOCK, block * QUERY_BLOCK + WINDOW)
        own = grad[rows, :]
        weighed = own.astype(f32) * o_ref[rows, :].astype(f32)
        center = jnp.sum(stack_heads(weighed), axis=-1, keepdims=True)
        grad_probs = mm_t(stack_heads(own), values[window, :])
        weights = p_ref[0, block]
        exact = weights.astype(f32) * (grad_probs - center)
        if block == 0:
            by_offset[:, :WINDOW] = exact
        else:
            by_offset[:, :WINDOW] += exact
        grad_scores = exact.astype(bf16)
        dq_ref[rows, :] = join_heads(mm(grad_scores, keys[window, :])).astype(bf16)
        dk[:, window] += mm(stack_heads_t(query_t[:, rows]), grad_scores)
        dv[:, window] += mm(stack_heads_t(grad_t[:, rows]), weights)
    dk_rows = dk[...].T
    dv_rows = dv[...].T
    back_ref[0] = dk_rows[:REACH].astype(bf16)
    back_ref[1] = dv_rows[:REACH].astype(bf16)
    dk_ref[...] = dk_rows[REACH:]
    dv_ref[...] = dv_rows[REACH:]

    by_offset[:, WINDOW:] = jnp.zeros((2 * QUERY_BLOCK, 4 * QUERY_BLOCK - WINDOW), f32)
    row_index = iota((QUERY_BLOCK, 4 * QUERY_BLOCK), 0)
    for head in range(2):
        tile = by_offset[head * QUERY_BLOCK : (head + 1) * QUERY_BLOCK, :]
        for bit in range(QUERY_BLOCK.bit_length() - 1):
            moved = pltpu.roll(tile, 4 * QUERY_BLOCK - (1 << bit), 1)
            tile = jnp.where((row_index >> bit) & 1 == 1, moved, tile)
        offsets[pl.ds(2 * step + head, 1), :] = jnp.sum(tile, axis=0, keepdims=True)

    @pl.when(step == PAIRS - 1)
    def _():
        _, chosen = offset_bucket()
        table_ref[...] = lax.dot_general(
            chosen.astype(f32), offsets[0:HEADS], (((1,), (1,)), ((), ())),
            precision=lax.Precision.HIGHEST, preferred_element_type=f32,
        )


def input_kernel(
    dq_ref, dk_ref, dv_ref, ret_ref, wq_ref, wk_ref, wv_ref, x_ref, dx1_ref, gain_ref,
    dkl_ref, dvl_ref, dx_ref, gg_ref,
):
    tokens = dq_ref.shape[0]
    head = tokens - REACH
    for own, low, which in ((dk_ref, dkl_ref, 0), (dv_ref, dvl_ref, 1)):
        low[:head, :] = own[:head, :].astype(bf16)
        low[head:, :] = (own[head:, :] + ret_ref[which].astype(f32)).astype(bf16)
    dh = (
        mm_t(dq_ref[...], wq_ref[...])
        + mm_t(dkl_ref[...], wk_ref[...])
        + mm_t(dvl_ref[...], wv_ref[...])
    )
    back, gain_grad = rms_back(x_ref[...].astype(f32), gain_ref[...].astype(f32), dh)
    dx_ref[...] = dx1_ref[...] + back
    gg_ref[...] = gain_grad


def put_tiles(out_ref, info, side, offset, found, shards):
    rows = found.shape[0] // shards
    first = HEADER + side * shards
    for shard in range(shards):
        for tile in range(found.shape[1] // LANES):
            piece = found[
                shard * rows : (shard + 1) * rows, tile * LANES : (tile + 1) * LANES
            ].astype(bf16)
            out_ref[
                info[first + shard], offset + tile * rows : offset + (tile + 1) * rows, :
            ] = piece


def gate_up_kernel(shards, info, h_ref, gk_ref, gs_ref, uk_ref, us_ref, keep_ref, send_ref, h_t):
    @pl.when(pl.program_id(0) == 0)
    def _():
        h_t[...] = h_ref[...].T

    half = keep_ref.shape[1] // 2
    put_tiles(keep_ref, info, 0, 0, mm(h_t[...], gk_ref[...]), shards)
    put_tiles(send_ref, info, 1, 0, mm(h_t[...], gs_ref[...]), shards)
    put_tiles(keep_ref, info, 0, half, mm(h_t[...], uk_ref[...]), shards)
    put_tiles(send_ref, info, 1, half, mm(h_t[...], us_ref[...]), shards)


def down_kernel(shards, info, u_ref, c_ref, keep_in, send_in, keep_ref, send_ref, u_t, found):
    @pl.when(pl.program_id(0) == 0)
    def _():
        u_t[...] = u_ref[...].T

    found[...] = mm(u_t[...], c_ref[...])
    rows = found.shape[0] // shards // 2
    for shard in range(shards):
        for which, out_ref in enumerate((keep_ref, send_ref)):
            side = info[1] ^ which
            start = pl.multiple_of((2 * shard + side) * rows, rows)
            piece = found[pl.ds(start, rows), :].astype(bf16)
            for tile in range(found.shape[1] // LANES):
                out_ref[info[HEADER + which * shards + shard], tile * rows : (tile + 1) * rows, :] = piece[
                    :, tile * LANES : (tile + 1) * LANES
                ]


def square_kernel(shards, count, aliased, info, *refs):
    sides = refs[: 3 * count]
    keep_ref, send_ref = refs[3 * count + (2 if aliased else 0) :][:2]
    rows = keep_ref.shape[1] // count
    for index in range(count):
        left_ref, own_ref, other_ref = sides[3 * index : 3 * index + 3]
        left = left_ref[...].T
        put_tiles(keep_ref, info, 0, index * rows, mm(left, own_ref[...]), shards)
        put_tiles(send_ref, info, 1, index * rows, mm(left, other_ref[...]), shards)


def memory_back_kernel(chunks, shards, info, memory_ref, wk_ref, wv_ref, *refs):
    parts = refs[:chunks]
    keep_ref, send_ref, dm_ref, found = refs[chunks + 2 :]
    rows = keep_ref.shape[1] // 2
    columns = found.shape[1] // 2
    memory_t = memory_ref[...].T
    total = None
    for which, weight_ref in ((0, wk_ref), (1, wv_ref)):
        grad = parts[0][which].astype(f32)
        for other in parts[1:]:
            grad = grad + other[which].astype(f32)
        grad = grad.astype(bf16)
        found[...] = mm(memory_t, grad)
        for flip, out_ref in enumerate((keep_ref, send_ref)):
            start = pl.multiple_of((info[1] ^ flip) * columns, LANES)
            half = found[:, pl.ds(start, columns)]
            put_tiles(out_ref, info, flip, which * rows, half, shards)
        share = mm_t(grad, weight_ref[...])
        total = share if total is None else total + share
    dm_ref[...] = total


def last_kernel(shards, info, h_ref, *refs):
    sides = refs[:6]
    ga_ref, gc_ref, gf_ref, table_ref = refs[6:10]
    keep_ref, send_ref = refs[10:]
    width = h_ref.shape[1]
    rows = 3 * (width // shards)
    left = h_ref[...].T
    for index in range(3):
        own_ref, other_ref = sides[2 * index : 2 * index + 2]
        put_tiles(keep_ref, info, 0, index * rows, mm(left, own_ref[...]), shards)
        put_tiles(send_ref, info, 1, index * rows, mm(left, other_ref[...]), shards)
    size = width // shards
    column = iota((shards, width), 1)
    shard = iota((shards, width), 0)
    own = (column >= shard * size) & (column < (shard + 1) * size)
    to_lane = iota((width, LANES), 0)
    for _ in range(shards - 1):
        to_lane = jnp.where(to_lane >= size, to_lane - size, to_lane)
    pick = (to_lane == iota((width, LANES), 1)).astype(bf16)
    gains = []
    for ref in (ga_ref, gc_ref, gf_ref):
        spread = jnp.where(own, jnp.broadcast_to(ref[...], (shards, width)), 0.0).astype(bf16)
        gains.append(mm(spread, pick))
    table_rows = BUCKETS // shards
    table = jnp.concatenate(
        [table_ref[...], jnp.zeros((BUCKETS, LANES - HEADS), f32)], axis=1
    )
    for shard_index in range(shards):
        pieces = [g[shard_index : shard_index + 1] for g in gains]
        pieces.append(table[shard_index * table_rows : (shard_index + 1) * table_rows])
        pieces.append(jnp.zeros((16 - 3 - table_rows, LANES), f32))
        tile = jnp.concatenate(pieces, axis=0).astype(bf16)
        for which, out_ref in enumerate((keep_ref, send_ref)):
            out_ref[info[HEADER + which * shards + shard_index], 3 * rows : 3 * rows + 16, :] = tile


def halves(info, own_ref, other_ref):
    own, other = own_ref[...].astype(f32), other_ref[...].astype(f32)
    first = info[1] == 0
    return jnp.where(first, own, other), jnp.where(first, other, own)


def fill_square(out_ref, sides, offset):
    rows, columns = out_ref.shape
    count = columns // LANES // 2
    for side, found in enumerate(sides):
        for tile in range(count):
            start = (side * count + tile) * LANES
            out_ref[:, start : start + LANES] = found[
                offset + tile * rows : offset + (tile + 1) * rows
            ]


def first_unpack_kernel(info, own_ref, other_ref, gate_ref, up_ref, down_ref, square_ref):
    sides = halves(info, own_ref, other_ref)
    rows, columns = gate_ref.shape
    count = columns // LANES // 2
    for side, found in enumerate(sides):
        for tile in range(count):
            start = (side * count + tile) * LANES
            at = (tile // 2) * 4 * rows + (tile % 2) * rows
            gate_ref[:, start : start + LANES] = found[at : at + rows]
            up_ref[:, start : start + LANES] = found[at + 2 * rows : at + 3 * rows]
    offset = 2 * count * rows
    half = down_ref.shape[0] // 2
    tiles = down_ref.shape[1] // LANES
    for side, found in enumerate(sides):
        for tile in range(tiles):
            at = offset + tile * half
            down_ref[side * half : (side + 1) * half, tile * LANES : (tile + 1) * LANES] = found[
                at : at + half
            ]
    fill_square(square_ref, sides, offset + tiles * half)


def square_unpack_kernel(info, own_ref, other_ref, *out_refs):
    sides = halves(info, own_ref, other_ref)
    offset = 0
    for out_ref in out_refs:
        fill_square(out_ref, sides, offset)
        offset += out_ref.shape[0] * (out_ref.shape[1] // LANES // 2)


def last_unpack_kernel(info, own_ref, other_ref, q_ref, k_ref, v_ref, misc_ref):
    square_unpack_kernel(info, own_ref, other_ref, q_ref, k_ref, v_ref)
    misc_ref[...] = own_ref[own_ref.shape[0] - 16 :, :].astype(f32)


def whole(shape):
    return pl.BlockSpec(shape, lambda *_: (0,) * len(shape))


def call(kernel, name, grid, ins, outs, args, scalars=(), scratch=(), alias=None, flops=0):
    shapes = [jax.ShapeDtypeStruct(shape, dtype) for shape, dtype, _ in outs]
    moved = sum(math.prod(a.shape) * a.dtype.itemsize for a in (*args, *shapes))
    return pl.pallas_call(
        kernel,
        out_shape=shapes,
        grid_spec=pltpu.PrefetchScalarGridSpec(
            num_scalar_prefetch=len(scalars),
            grid=grid,
            in_specs=list(ins),
            out_specs=[spec for _, _, spec in outs],
            scratch_shapes=list(scratch),
        ),
        input_output_aliases=alias or {},
        compiler_params=pltpu.CompilerParams(
            dimension_semantics=("arbitrary",) * len(grid), vmem_limit_bytes=VMEM_BYTES
        ),
        cost_estimate=pl.CostEstimate(flops=int(flops), bytes_accessed=moved, transcendentals=0),
        name=name,
    )(*scalars, *args)


def full(*arrays):
    return [whole(a.shape) for a in arrays]


def bit_orders(bits):
    if bits < 2:
        return [list(range(bits))] * 2
    return [[0, 1] + list(range(bits - 1, 1, -1)), [1, 0] + list(range(2, bits))]


def shards(
    inputs, memory, cotangent, answer_lengths, answer_groups, memory_lengths,
    gain_attn, self_query, self_key, self_value, self_out, bucket_bias_table,
    gain_cross, cross_query, cross_key_matrix, cross_value, cross_out,
    gain_ffn, hidden_gate, hidden_up, hidden_down,
):
    tokens, width = inputs.shape
    part = memory.shape[0]
    hidden = hidden_gate.shape[1]
    wide_size = lax.axis_size("wide")
    narrow_size = lax.axis_size("narrow")
    wide_index = lax.axis_index("wide")
    narrow_index = lax.axis_index("narrow")
    side = narrow_index % 2
    bits = wide_size.bit_length() - 1
    orders = bit_orders(bits)
    relative = jnp.arange(wide_size, dtype=jnp.int32) ^ wide_index
    slots = [
        sum(((relative >> bit) & 1) << (bits - 1 - place) for place, bit in enumerate(order))
        for order in orders
    ]
    header = jnp.stack(
        [
            wide_index,
            side,
            side,
            wide_index * (narrow_size // 2) + narrow_index // 2,
            narrow_index,
        ]
        + [jnp.int32(0)] * (HEADER - 5)
    ).astype(jnp.int32)
    swap = side == 0
    info = jnp.concatenate(
        [header, jnp.where(swap, slots[0], slots[1]), jnp.where(swap, slots[1], slots[0])]
    )
    gains = [g.reshape(1, width) for g in (gain_attn, gain_cross, gain_ffn)]

    both = ("wide", "narrow")

    def to_narrow(value, target):
        pairs = [(n, target(n)) for n in range(narrow_size) if target(n) is not None]
        return lax.ppermute(value, "narrow", pairs)

    def to_wide(value, place):
        pairs = []
        for w in range(wide_size):
            for n in range(narrow_size):
                partner = w ^ (1 << orders[n % 2][place])
                pairs.append((w * narrow_size + n, partner * narrow_size + n))
        return lax.ppermute(value, both, pairs)

    def summed(pieces):
        total = pieces[0].astype(f32)
        for piece in pieces[1:]:
            total = total + piece.astype(f32)
        return total.astype(bf16)

    def reduce_group(keep, send):
        pieces = [keep, to_narrow(send, lambda n: n ^ 1)]
        count = wide_size
        for place in range(bits):
            count //= 2
            got = to_wide(summed([p[count:] for p in pieces]), place)
            pieces = [p[:count] for p in pieces] + [got]
        total = summed([p[0] for p in pieces])
        step = 2
        while step < narrow_size:
            total = summed([total, to_narrow(total, lambda n, s=step: n ^ s)])
            step *= 2
        return total, to_narrow(total, lambda n: n ^ 1)

    block = lambda rows: pl.BlockSpec((rows, PAIR), lambda j, *_: (0, j))
    out_rows = pl.BlockSpec((PAIR, width), lambda j, *_: (j, 0))

    third = pl.BlockSpec((width, 256), lambda j, *_: (0, j))
    (memory_own,) = call(
        memory_kernel, "memory_projection", (width // 256,),
        [whole(memory.shape), third, third],
        [((2, part, width), bf16, pl.BlockSpec((2, part, 256), lambda j, *_: (0, 0, j)))],
        (memory, cross_key_matrix, cross_value),
        flops=4 * part * width * width,
    )
    memory_parts = [memory_own] + [
        to_narrow(memory_own, lambda n, s=shift: (n + s) % narrow_size)
        for shift in range(1, narrow_size)
    ]
    token_third = pl.BlockSpec((tokens, 256), lambda j, *_: (0, j))
    normed, queries, keys, values, tail = call(
        project_kernel, "self_projection", (width // 256,),
        [whole(inputs.shape), whole((1, width)), third, third, third],
        [((tokens, width), bf16, whole((tokens, width)))]
        + [((tokens, width), bf16, token_third)] * 3
        + [((2, REACH, width), bf16, pl.BlockSpec((2, REACH, 256), lambda j, *_: (0, 0, j)))],
        (inputs, gains[0], self_query, self_key, self_value),
        flops=6 * tokens * width * width,
    )
    halo = to_narrow(tail, lambda n: n + 1 if n % 2 == 0 else None)

    halo_block = pl.BlockSpec((2, REACH, PAIR), lambda j, *_: (0, 0, j))
    blocks = tokens // QUERY_BLOCK
    self_probs = pl.BlockSpec(
        (1, blocks, 2 * QUERY_BLOCK, WINDOW), lambda j, *_: (j, 0, 0, 0)
    )
    model = (tokens, width)
    attended, inverse, probs, x1, normed_two, cross_rows = call(
        self_forward_kernel, "self_forward", (PAIRS,),
        [block(tokens)] * 3 + [halo_block, whole(bucket_bias_table.shape), whole(model), out_rows]
        + full(gains[1], cross_query),
        [
            (model, bf16, block(tokens)),
            (model, f32, block(tokens)),
            ((PAIRS, blocks, 2 * QUERY_BLOCK, WINDOW), bf16, self_probs),
            (model, f32, whole(model)),
            (model, bf16, whole(model)),
            (model, bf16, whole(model)),
        ],
        (queries, keys, values, halo, bucket_bias_table, inputs, self_out, gains[1], cross_query),
        scalars=(info, answer_lengths),
        scratch=(
            pltpu.VMEM((tokens + REACH, PAIR), bf16),
            pltpu.VMEM((tokens + REACH, 2 * PAIR), bf16),
            pltpu.VMEM((16, 4 * QUERY_BLOCK), f32),
            pltpu.VMEM((2 * QUERY_BLOCK, WINDOW), f32),
            pltpu.VMEM((tokens, LANES), jnp.int32),
        ),
        flops=4 * tokens * width * width + 16 * tokens * WINDOW * width,
    )

    memory_tokens = part * narrow_size
    memory_block = pl.BlockSpec((2, part, PAIR), lambda j, *_: (0, 0, j))
    cross_blocks = tokens // CROSS_BLOCK
    cross_probs = pl.BlockSpec(
        (1, cross_blocks, 2 * CROSS_BLOCK, memory_tokens), lambda j, *_: (j, 0, 0, 0)
    )
    attended_two, inverse_two, probs_two, x2, normed_three = call(
        functools.partial(cross_forward_kernel, narrow_size), "cross_forward", (PAIRS,),
        [block(tokens), whole(model), out_rows, whole((1, width))] + [memory_block] * narrow_size,
        [
            (model, bf16, block(tokens)),
            (model, f32, block(tokens)),
            ((PAIRS, cross_blocks, 2 * CROSS_BLOCK, memory_tokens), bf16, cross_probs),
            (model, f32, whole(model)),
            (model, bf16, whole(model)),
        ],
        (cross_rows, x1, cross_out, gains[2], *memory_parts),
        scalars=(info, answer_lengths, answer_groups, memory_lengths),
        scratch=(
            pltpu.VMEM((memory_tokens, PAIR), bf16),
            pltpu.VMEM((memory_tokens, 2 * PAIR), bf16),
            pltpu.VMEM((tokens, LANES), jnp.int32),
            pltpu.VMEM((8, memory_tokens), jnp.int32),
        ),
        flops=2 * tokens * width * width + 16 * tokens * memory_tokens * width,
    )

    tile = 512
    wide_tile = pl.BlockSpec((width, tile), lambda j, *_: (0, j))
    token_tile = pl.BlockSpec((tokens, tile), lambda j, *_: (0, j))
    hidden_shape = (tokens, hidden)
    unit, grad_gate, grad_up, layer_out, dx2, e2, gain_grad_ffn = call(
        ffn_kernel, "feed_forward", (hidden // tile,),
        [whole(model)] * 3
        + [whole((1, width)), wide_tile, wide_tile]
        + [pl.BlockSpec((tile, width), lambda j, *_: (j, 0))],
        [(hidden_shape, bf16, token_tile)] * 3
        + [
            (model, bf16, whole(model)),
            (model, f32, whole(model)),
            (model, bf16, whole(model)),
            ((1, width), f32, whole((1, width))),
        ],
        (normed_three, cotangent, x2, gains[2], hidden_gate, hidden_up, hidden_down),
        scratch=(pltpu.VMEM(model, f32), pltpu.VMEM(model, f32)),
        flops=12 * tokens * width * hidden,
    )

    square_rows = width // wide_size * (width // 2 // LANES)
    gate_rows = width // wide_size * (hidden // 2 // LANES)
    down_rows = hidden // wide_size // 2 * (width // LANES)
    group_rows = 2 * gate_rows + down_rows + square_rows
    step_rows = gate_rows // 2
    group_shape = (wide_size, group_rows, LANES)
    gate_side = lambda flip: pl.BlockSpec(
        (tokens, 256), lambda j, info: (0, (info[1] ^ flip) * (hidden // 512) + j)
    )
    half_side = lambda flip: pl.BlockSpec(
        (tokens, width // 2), lambda j, info: (0, info[1] ^ flip)
    )
    step_spec = pl.BlockSpec((wide_size, step_rows, LANES), lambda j, *_: (0, j, 0))
    keep, send = call(
        functools.partial(gate_up_kernel, wide_size), "gate_up_gradient", (hidden // 512,),
        [whole(model), gate_side(0), gate_side(1), gate_side(0), gate_side(1)],
        [(group_shape, bf16, step_spec)] * 2,
        (normed_three, grad_gate, grad_gate, grad_up, grad_up),
        scalars=(info,),
        scratch=(pltpu.VMEM((width, tokens), bf16),),
        flops=4 * tokens * width * hidden,
    )
    first = 2 * gate_rows // step_rows
    down_spec = pl.BlockSpec((wide_size, step_rows, LANES), lambda j, *_: (0, first + j, 0))
    anywhere = pl.BlockSpec(memory_space=pl.ANY)
    keep, send = call(
        functools.partial(down_kernel, wide_size), "down_gradient", (2,),
        [whole(hidden_shape), pl.BlockSpec((tokens, width // 2), lambda j, *_: (0, j))]
        + [anywhere] * 2,
        [(group_shape, bf16, down_spec)] * 2,
        (unit, cotangent, keep, send),
        scalars=(info,),
        scratch=(
            pltpu.VMEM((hidden, tokens), bf16),
            pltpu.VMEM((hidden, width // 2), f32),
        ),
        alias={3: 0, 4: 1},
        flops=2 * tokens * width * hidden,
    )

    def squares(name, rows_at, pairs, keep, send, shape):
        spec = pl.BlockSpec(
            (wide_size, len(pairs) * square_rows, LANES), lambda j, *_: (0, rows_at, 0)
        )
        args, specs = [], []
        for left, right in pairs:
            args += [left, right, right]
            specs += [whole(left.shape), half_side(0), half_side(1)]
        more = () if keep is None else (keep, send)
        return call(
            functools.partial(square_kernel, wide_size, len(pairs), bool(more)), name, (1,),
            specs + [anywhere] * len(more),
            [(shape, bf16, spec)] * 2,
            (*args, *more),
            scalars=(info,),
            alias={1 + len(args): 0, 2 + len(args): 1} if more else None,
            flops=2 * len(pairs) * tokens * width * width,
        )

    keep, send = squares(
        "cross_out_gradient", (group_rows - square_rows) // square_rows,
        [(attended_two, e2)], keep, send, group_shape,
    )
    first_own, first_other = reduce_group(keep, send)

    grad_cross_rows, dx1, e1, gain_grad_cross, *memory_grads = call(
        functools.partial(cross_backward_kernel, narrow_size), "cross_backward", (PAIRS,),
        [whole(model), out_rows, block(tokens), block(tokens), cross_probs, block(tokens)]
        + [block(width), whole(model), whole(model), whole((1, width))]
        + [memory_block] * narrow_size,
        [
            (model, bf16, block(tokens)),
            (model, f32, whole(model)),
            (model, bf16, whole(model)),
            ((1, width), f32, whole((1, width))),
        ]
        + [((2, part, width), bf16, memory_block)] * narrow_size,
        (e2, cross_out, attended_two, inverse_two, probs_two, cross_rows, cross_query, x1, dx2)
        + (gains[1], *memory_parts),
        scratch=(
            pltpu.VMEM((memory_tokens, PAIR), bf16),
            pltpu.VMEM((memory_tokens, PAIR), bf16),
            pltpu.VMEM((PAIR, memory_tokens), f32),
            pltpu.VMEM((PAIR, memory_tokens), f32),
            pltpu.VMEM(model, f32),
        ),
        flops=4 * tokens * width * width + 32 * tokens * memory_tokens * width,
    )
    memory_shares = [memory_grads[0]] + [
        to_narrow(memory_grads[shift], lambda n, s=shift: (n - s) % narrow_size)
        for shift in range(1, narrow_size)
    ]
    second_shape = (wide_size, 4 * square_rows, LANES)
    keep, send = squares(
        "query_out_gradient", 0, [(normed_two, grad_cross_rows), (attended, e1)],
        None, None, second_shape,
    )
    second_spec = pl.BlockSpec((wide_size, 2 * square_rows, LANES), lambda j, *_: (0, 1, 0))
    keep, send, memory_grad = call(
        functools.partial(memory_back_kernel, narrow_size, wide_size), "memory_backward", (1,),
        full(memory, cross_key_matrix, cross_value, *memory_shares) + [anywhere] * 2,
        [(second_shape, bf16, second_spec)] * 2
        + [((part, width), f32, whole((part, width)))],
        (memory, cross_key_matrix, cross_value, *memory_shares, keep, send),
        scalars=(info,),
        scratch=(pltpu.VMEM((width, width), f32),),
        alias={4 + narrow_size: 0, 5 + narrow_size: 1},
        flops=8 * part * width * width,
    )
    second_own, second_other = reduce_group(keep, send)

    grad_queries, grad_keys, grad_values, back, grad_table = call(
        self_backward_kernel, "self_backward", (PAIRS,),
        [whole(model), out_rows, block(tokens), block(tokens), self_probs]
        + [block(tokens)] * 3 + [halo_block],
        [
            (model, bf16, block(tokens)),
            (model, f32, block(tokens)),
            (model, f32, block(tokens)),
            ((2, REACH, width), bf16, halo_block),
            ((BUCKETS, HEADS), f32, whole((BUCKETS, HEADS))),
        ],
        (e1, self_out, attended, inverse, probs, queries, keys, values, halo),
        scratch=(
            pltpu.VMEM((tokens + REACH, PAIR), bf16),
            pltpu.VMEM((tokens + REACH, PAIR), bf16),
            pltpu.VMEM((PAIR, tokens + REACH), f32),
            pltpu.VMEM((PAIR, tokens + REACH), f32),
            pltpu.VMEM((2 * QUERY_BLOCK, 4 * QUERY_BLOCK), f32),
            pltpu.VMEM((16, 4 * QUERY_BLOCK), f32),
        ),
        flops=2 * tokens * width * width + 32 * tokens * WINDOW * width,
    )
    returned = to_narrow(back, lambda n: n - 1 if n % 2 == 1 else None)
    keys_low, values_low, input_grad, gain_grad_attn = call(
        input_kernel, "input_gradient", (1,),
        full(grad_queries, grad_keys, grad_values, returned)
        + full(self_query, self_key, self_value, inputs, dx1, gains[0]),
        [
            (model, bf16, whole(model)),
            (model, bf16, whole(model)),
            (model, f32, whole(model)),
            ((1, width), f32, whole((1, width))),
        ],
        (grad_queries, grad_keys, grad_values, returned)
        + (self_query, self_key, self_value, inputs, dx1, gains[0]),
        flops=6 * tokens * width * width,
    )
    last_shape = (wide_size, 3 * square_rows + 16, LANES)
    keep, send = call(
        functools.partial(last_kernel, wide_size), "self_gradient", (1,),
        [whole(model)] + [half_side(0), half_side(1)] * 3 + [whole((1, width))] * 3
        + [whole(grad_table.shape)],
        [(last_shape, bf16, whole(last_shape))] * 2,
        (normed, grad_queries, grad_queries, keys_low, keys_low, values_low, values_low)
        + (gain_grad_attn, gain_grad_cross, gain_grad_ffn, grad_table),
        scalars=(info,),
        flops=6 * tokens * width * width,
    )
    last_own, last_other = reduce_group(keep, send)

    square_out = ((width // wide_size, width), f32, whole((width // wide_size, width)))
    gate_out = ((width // wide_size, hidden), f32, whole((width // wide_size, hidden)))
    down_out = ((hidden // wide_size, width), f32, whole((hidden // wide_size, width)))
    grad_gate_w, grad_up_w, grad_down_w, grad_cross_out = call(
        first_unpack_kernel, "first_outputs", (1,), full(first_own, first_other),
        [gate_out, gate_out, down_out, square_out], (first_own, first_other), scalars=(info,),
    )
    grad_cross_query, grad_self_out, grad_cross_key, grad_cross_value = call(
        square_unpack_kernel, "second_outputs", (1,), full(second_own, second_other),
        [square_out] * 4, (second_own, second_other), scalars=(info,),
    )
    grad_self_query, grad_self_key, grad_self_value, misc = call(
        last_unpack_kernel, "last_outputs", (1,), full(last_own, last_other),
        [square_out] * 3 + [((16, LANES), f32, whole((16, LANES)))],
        (last_own, last_other), scalars=(info,),
    )
    size = width // wide_size
    table_rows = BUCKETS // wide_size
    return (
        layer_out,
        input_grad,
        memory_grad,
        misc[0, :size],
        grad_self_query,
        grad_self_key,
        grad_self_value,
        grad_self_out,
        misc[3 : 3 + table_rows, :HEADS],
        misc[1, :size],
        grad_cross_query,
        grad_cross_key,
        grad_cross_value,
        grad_cross_out,
        misc[2, :size],
        grad_gate_w,
        grad_up_w,
        grad_down_w,
    )


def solution(mesh):
    rows = P(("wide", "narrow"), None)
    vector, matrix = P("wide"), P("wide", None)
    return jax.shard_map(
        shards,
        mesh=mesh,
        in_specs=(rows,) * 3 + (P(),) * 18,
        out_specs=(rows,) * 3
        + (vector,)
        + (matrix,) * 5
        + (vector,)
        + (matrix,) * 4
        + (vector,)
        + (matrix,) * 3,
        check_vma=False,
    )
```

```python
import functools
import math

import jax
import jax.numpy as jnp
import numpy as np
from jax import lax
from jax.experimental import pallas as pl
from jax.experimental.pallas import tpu as pltpu
from jax.sharding import PartitionSpec as P

HEADS = 12
HEAD_DIM = 64
BUCKETS = 32
MAX_DIST = 128
ANSWERS = 8
GROUPS = 16
PAIR = 2 * HEAD_DIM
PAIRS = HEADS // 2
REACH = 256
QUERY_BLOCK = 128
WINDOW = REACH + QUERY_BLOCK
CROSS_BLOCK = 256
LANES = 128
HEADER = 8
VMEM_BYTES = 20 * 2**20
TIMES = {
    "projections": 5.0,
    "queries": 3.0,
    "self_forward": 12.0,
    "cross_forward": 10.5,
    "feed_forward": 15.0,
    "gate_up_gradient": 6.0,
    "down_gradient": 4.4,
    "cross_backward": 12.0,
    "square_gradients": 3.4,
    "memory_backward": 3.6,
    "self_backward": 9.2,
    "query_gradient": 9.0,
    "key_value_gradient": 2.4,
    "input_gradient": 18.0,
    "gains": 1.2,
    "partial_sum": 1.0,
    "gate_outputs": 1.4,
    "down_outputs": 1.4,
    "second_outputs": 1.4,
    "last_outputs": 1.4,
}
COVER = 1.15e9

epsilon = 1e-06
neg_big = -1e30
f32 = jnp.float32
bf16 = jnp.bfloat16


def mm(left, right):
    return jnp.dot(left, right, preferred_element_type=f32)


def mm_t(left, right):
    return lax.dot_general(left, right, (((1,), (1,)), ((), ())), preferred_element_type=f32)


def rms(values, gain_row):
    factor = lax.rsqrt(jnp.mean(values * values, axis=-1, keepdims=True) + epsilon)
    return values * factor * gain_row


def rms_back(values, gain_row, grad):
    factor = lax.rsqrt(jnp.mean(values * values, axis=-1, keepdims=True) + epsilon)
    unit = values * factor
    scaled = grad * gain_row
    center = jnp.mean(scaled * unit, axis=-1, keepdims=True)
    return factor * (scaled - unit * center), jnp.sum(grad * unit, axis=0, keepdims=True)


def bucket_of(distance):
    exact_count = BUCKETS // 2
    log_count = BUCKETS - exact_count
    near_part = jnp.minimum(jnp.maximum(distance, 0), exact_count)
    far_part = jnp.zeros_like(distance)
    for level_index in range(1, log_count):
        edge = math.ceil(exact_count * (MAX_DIST / exact_count) ** (level_index / log_count))
        far_part = far_part + (distance >= edge).astype(jnp.int32)
    return near_part + far_part


def gain_of(ref):
    return ref[...].astype(f32).reshape(1, ref.shape[0])


def iota(shape, axis):
    return lax.broadcasted_iota(jnp.int32, shape, axis)


def low_lanes(shape):
    return iota(shape, len(shape) - 1) < HEAD_DIM


def stack_heads(rows):
    low = low_lanes(rows.shape)
    zero = jnp.zeros_like(rows)
    return jnp.concatenate([jnp.where(low, rows, zero), jnp.where(low, zero, rows)], axis=0)


def stack_heads_t(columns):
    low = iota(columns.shape, 0) < HEAD_DIM
    zero = jnp.zeros_like(columns)
    return jnp.concatenate([jnp.where(low, columns, zero), jnp.where(low, zero, columns)], axis=1)


def join_heads(stacked):
    half = stacked.shape[0] // 2
    return jnp.where(low_lanes((half, PAIR)), stacked[:half], stacked[half:])


def offset_bucket():
    lane = iota((1, 4 * QUERY_BLOCK), 1)
    distance = jnp.where(lane < WINDOW, REACH - lane, REACH + 4 * QUERY_BLOCK - lane)
    chosen = iota((BUCKETS, 4 * QUERY_BLOCK), 0) == bucket_of(distance)
    return distance, chosen


def answer_ends(lengths, row):
    total, ends = lengths[0, row], []
    for index in range(1, ANSWERS):
        ends.append(total)
        total = total + lengths[index, row]
    return ends


def project_kernel(
    gain_ref, x_hbm, memory_hbm, wk_hbm, wv_hbm, wck_hbm, wcv_hbm,
    h_ref, k_ref, v_ref, tail_ref, memory_out,
    x_ref, memory_ref, wk_ref, wv_ref, wck_ref, wcv_ref, sems,
):
    copies = [
        pltpu.make_async_copy(source, target, sems.at[index])
        for index, (source, target) in enumerate(
            (
                (x_hbm, x_ref),
                (memory_hbm, memory_ref),
                (wck_hbm, wck_ref),
                (wcv_hbm, wcv_ref),
                (wk_hbm, wk_ref),
                (wv_hbm, wv_ref),
            )
        )
    ]
    for copy in copies:
        copy.start()
    copies[0].wait()
    h_ref[...] = rms(x_ref[...].astype(f32), gain_of(gain_ref)).astype(bf16)
    copies[1].wait()
    copies[2].wait()
    memory_out[0] = mm(memory_ref[...], wck_ref[...]).astype(bf16)
    copies[3].wait()
    memory_out[1] = mm(memory_ref[...], wcv_ref[...]).astype(bf16)
    tokens = h_ref.shape[0]
    copies[4].wait()
    k_ref[...] = mm(h_ref[...], wk_ref[...]).astype(bf16)
    tail_ref[0] = k_ref[tokens - REACH :, :]
    copies[5].wait()
    v_ref[...] = mm(h_ref[...], wv_ref[...]).astype(bf16)
    tail_ref[1] = v_ref[tokens - REACH :, :]


def query_kernel(h_ref, wq_hbm, table_ref, q_ref, bias_ref, wq_ref, sem):
    copy = pltpu.make_async_copy(wq_hbm, wq_ref, sem)
    copy.start()
    distance, chosen = offset_bucket()
    base = jnp.where(distance < 0, neg_big, mm(table_ref[...], chosen.astype(bf16)))
    for head in range(HEADS):
        spread = jnp.broadcast_to(base[head : head + 1], (QUERY_BLOCK, 4 * QUERY_BLOCK))
        skewed = pltpu.roll(spread, 0, 1, stride=1, stride_axis=0)
        bias_ref[head * QUERY_BLOCK : (head + 1) * QUERY_BLOCK, :] = skewed[:, :WINDOW]
    copy.wait()
    q_ref[...] = mm(h_ref[...], wq_ref[...]).astype(bf16)


def self_forward_kernel(
    info, lengths,
    q_ref, k_ref, v_ref, halo_ref, bias, x_ref, wo_ref, gain_ref, wq_ref,
    o_ref, inv_ref, e_ref, x1_ref, h2_ref, qc_ref,
    keys, values, reach,
):
    step = pl.program_id(0)
    tokens = q_ref.shape[0]

    @pl.when(step == 0)
    def _():
        place = info[2] * tokens + iota((tokens, LANES), 0)
        start = jnp.zeros_like(place)
        for end in answer_ends(lengths, info[3]):
            start = jnp.where(place >= end, end, start)
        reach[...] = place - start
        values[:, PAIR:] = jnp.ones((values.shape[0], PAIR), bf16)
        x1_ref[...] = x_ref[...].astype(f32)

    keys[0:REACH] = halo_ref[0]
    keys[REACH:] = k_ref[...]
    values[0:REACH, 0:PAIR] = halo_ref[1]
    values[REACH:, 0:PAIR] = v_ref[...]
    distance = REACH + iota((QUERY_BLOCK, WINDOW), 0) - iota((QUERY_BLOCK, WINDOW), 1)
    distance = jnp.concatenate([distance, distance], axis=0)
    for block in range(tokens // QUERY_BLOCK):
        rows = slice(block * QUERY_BLOCK, (block + 1) * QUERY_BLOCK)
        window = slice(block * QUERY_BLOCK, block * QUERY_BLOCK + WINDOW)
        scores = mm_t(stack_heads(q_ref[rows, :]), keys[window, :])
        own_reach = reach[rows, 0:1]
        own_reach = jnp.concatenate([own_reach, own_reach], axis=0)
        scores = jnp.where(distance <= own_reach, scores + bias[...], neg_big)
        top = jnp.max(scores, axis=-1, keepdims=True)
        weights = jnp.exp(scores - top).astype(bf16)
        e_ref[0, block] = weights
        mixed = mm(weights, values[window, :])
        inverse = 1.0 / mixed[:, PAIR:]
        o_ref[rows, :] = join_heads(mixed[:, :PAIR] * inverse).astype(bf16)
        inv_ref[rows, :] = join_heads(inverse)
    x1_ref[...] += mm(o_ref[...], wo_ref[...])

    @pl.when(step == PAIRS - 1)
    def _():
        h2_ref[...] = rms(x1_ref[...], gain_of(gain_ref)).astype(bf16)
        qc_ref[...] = mm(h2_ref[...], wq_ref[...]).astype(bf16)


def cross_forward_kernel(chunks, info, lengths, groups, bounds, *refs):
    q_ref, x1_ref, wo_ref, gain_ref = refs[:4]
    kv_refs = refs[4 : 4 + chunks]
    o_ref, inv_ref, e_ref, x2_ref, h3_ref = refs[4 + chunks : 9 + chunks]
    keys, values, query_group, key_group = refs[9 + chunks :]
    step = pl.program_id(0)
    tokens = q_ref.shape[0]
    part = kv_refs[0].shape[1]

    @pl.when(step == 0)
    def _():
        place = info[2] * tokens + iota((tokens, LANES), 0)
        group = jnp.zeros_like(place) + groups[0, info[3]]
        for index, end in enumerate(answer_ends(lengths, info[3])):
            group = jnp.where(place >= end, groups[index + 1, info[3]], group)
        query_group[...] = group
        total, ends = bounds[info[0], 0], []
        for index in range(1, GROUPS):
            ends.append(total)
            total = total + bounds[info[0], index]
        for chunk in range(chunks):
            owner = lax.rem(info[4] + chunks - chunk, chunks)
            token = owner * part + iota((8, part), 1)
            found = jnp.zeros_like(token)
            for end in ends:
                found = found + (token >= end).astype(jnp.int32)
            key_group[:, chunk * part : (chunk + 1) * part] = found
        values[:, PAIR:] = jnp.ones((values.shape[0], PAIR), bf16)
        x2_ref[...] = x1_ref[...]

    for chunk in range(chunks):
        keys[chunk * part : (chunk + 1) * part] = kv_refs[chunk][0]
        values[chunk * part : (chunk + 1) * part, 0:PAIR] = kv_refs[chunk][1]
    for block in range(tokens // CROSS_BLOCK):
        rows = slice(block * CROSS_BLOCK, (block + 1) * CROSS_BLOCK)
        scores = mm_t(stack_heads(q_ref[rows, :]), keys[...])
        own_group = query_group[rows, 0:1]
        own_group = jnp.concatenate([own_group, own_group], axis=0)
        scores = jnp.where(own_group == key_group[0:1, :], scores, neg_big)
        top = jnp.max(scores, axis=-1, keepdims=True)
        weights = jnp.exp(scores - top).astype(bf16)
        e_ref[0, block] = weights
        mixed = mm(weights, values[...])
        inverse = 1.0 / mixed[:, PAIR:]
        o_ref[rows, :] = join_heads(mixed[:, :PAIR] * inverse).astype(bf16)
        inv_ref[rows, :] = join_heads(inverse)
    x2_ref[...] += mm(o_ref[...], wo_ref[...])

    @pl.when(step == PAIRS - 1)
    def _():
        h3_ref[...] = rms(x2_ref[...], gain_of(gain_ref)).astype(bf16)


def ffn_kernel(
    h_ref, c_ref, x2_ref, gain_ref, wg_ref, wu_ref, wd_ref,
    u_ref, dga_ref, dgb_ref, out_ref, dx_ref, e_ref, gg_ref,
    total, dh,
):
    step = pl.program_id(0)
    gate = mm(h_ref[...], wg_ref[...])
    up = mm(h_ref[...], wu_ref[...])
    du = mm_t(c_ref[...], wd_ref[...])
    root = math.sqrt(2.0 / math.pi)
    square = gate * gate
    bent = jnp.tanh(root * gate * (1.0 + 0.044715 * square))
    share = 0.5 * (1.0 + bent)
    active = gate * share
    slope = share + 0.5 * gate * (1.0 - bent * bent) * (root * (1.0 + 3 * 0.044715 * square))
    u_ref[...] = (active * up).astype(bf16)
    dgb_ref[...] = (du * active).astype(bf16)
    dga_ref[...] = (du * up * slope).astype(bf16)
    out_part = mm(u_ref[...], wd_ref[...])
    dh_part = mm_t(dga_ref[...], wg_ref[...]) + mm_t(dgb_ref[...], wu_ref[...])

    @pl.when(step == 0)
    def _():
        total[...] = x2_ref[...] + out_part
        dh[...] = dh_part

    @pl.when(step > 0)
    def _():
        total[...] += out_part
        dh[...] += dh_part

    @pl.when(step == pl.num_programs(0) - 1)
    def _():
        out_ref[...] = total[...].astype(bf16)
        back, gain_grad = rms_back(x2_ref[...], gain_of(gain_ref), dh[...])
        dx_ref[...] = c_ref[...].astype(f32) + back
        e_ref[...] = dx_ref[...].astype(bf16)
        gg_ref[...] = gain_grad


def cross_backward_kernel(chunks, *refs):
    e2_ref, wo_ref, o_ref, inv_ref, p_ref, q_ref, wq_ref, x1_ref, dx2_ref, gain_ref = refs[:10]
    kv_refs = refs[10 : 10 + chunks]
    dq_ref, dx_ref, e1_ref, gg_ref = refs[10 + chunks : 14 + chunks]
    dkv_refs = refs[14 + chunks : 14 + 2 * chunks]
    keys, values, dk, dv, dh = refs[14 + 2 * chunks :]
    step = pl.program_id(0)
    tokens = q_ref.shape[0]
    part = kv_refs[0].shape[1]

    for chunk in range(chunks):
        keys[chunk * part : (chunk + 1) * part] = kv_refs[chunk][0]
        values[chunk * part : (chunk + 1) * part] = kv_refs[chunk][1]
    grad = mm_t(e2_ref[...], wo_ref[...]).astype(bf16).astype(f32)
    grad = (grad * inv_ref[...]).astype(bf16)
    query_t = q_ref[...].T
    grad_t = grad.T
    for block in range(tokens // CROSS_BLOCK):
        rows = slice(block * CROSS_BLOCK, (block + 1) * CROSS_BLOCK)
        own = grad[rows, :]
        weighed = own.astype(f32) * o_ref[rows, :].astype(f32)
        center = jnp.sum(stack_heads(weighed), axis=-1, keepdims=True)
        grad_probs = mm_t(stack_heads(own), values[...])
        weights = p_ref[0, block]
        grad_scores = (weights.astype(f32) * (grad_probs - center)).astype(bf16)
        dq_ref[rows, :] = join_heads(mm(grad_scores, keys[...])).astype(bf16)
        dk_part = mm(stack_heads_t(query_t[:, rows]), grad_scores)
        dv_part = mm(stack_heads_t(grad_t[:, rows]), weights)
        if block == 0:
            dk[...] = dk_part
            dv[...] = dv_part
        else:
            dk[...] += dk_part
            dv[...] += dv_part
    dk_rows = dk[...].T.astype(bf16)
    dv_rows = dv[...].T.astype(bf16)
    for chunk in range(chunks):
        dkv_refs[chunk][0] = dk_rows[chunk * part : (chunk + 1) * part]
        dkv_refs[chunk][1] = dv_rows[chunk * part : (chunk + 1) * part]
    dh_part = mm_t(dq_ref[...], wq_ref[...])

    @pl.when(step == 0)
    def _():
        dh[...] = dh_part

    @pl.when(step > 0)
    def _():
        dh[...] += dh_part

    @pl.when(step == PAIRS - 1)
    def _():
        back, gain_grad = rms_back(x1_ref[...], gain_of(gain_ref), dh[...])
        dx_ref[...] = dx2_ref[...] + back
        e1_ref[...] = dx_ref[...].astype(bf16)
        gg_ref[...] = gain_grad


def self_backward_kernel(
    begin, e1_ref, wo_ref, o_ref, inv_ref, p_ref, q_ref, k_ref, v_ref, halo_ref, *refs
):
    dq_ref, dk_ref, dv_ref, back_ref, table_ref, keys, values, dk, dv, by_offset, offsets = refs[
        -11:
    ]
    step = pl.program_id(0)
    tokens = q_ref.shape[0]
    keys[0:REACH] = halo_ref[0]
    keys[REACH:] = k_ref[...]
    values[0:REACH] = halo_ref[1]
    values[REACH:] = v_ref[...]
    grad = mm_t(e1_ref[...], wo_ref[...]).astype(bf16).astype(f32)
    grad = (grad * inv_ref[...]).astype(bf16)
    query_t = q_ref[...].T
    grad_t = grad.T
    dk[...] = jnp.zeros_like(dk)
    dv[...] = jnp.zeros_like(dv)
    for block in range(tokens // QUERY_BLOCK):
        rows = slice(block * QUERY_BLOCK, (block + 1) * QUERY_BLOCK)
        window = slice(block * QUERY_BLOCK, block * QUERY_BLOCK + WINDOW)
        own = grad[rows, :]
        weighed = own.astype(f32) * o_ref[rows, :].astype(f32)
        center = jnp.sum(stack_heads(weighed), axis=-1, keepdims=True)
        grad_probs = mm_t(stack_heads(own), values[window, :])
        weights = p_ref[0, block]
        exact = weights.astype(f32) * (grad_probs - center)
        if block == 0:
            by_offset[:, :WINDOW] = exact
        else:
            by_offset[:, :WINDOW] += exact
        grad_scores = exact.astype(bf16)
        dq_ref[rows, :] = join_heads(mm(grad_scores, keys[window, :])).astype(bf16)
        dk[:, window] += mm(stack_heads_t(query_t[:, rows]), grad_scores)
        dv[:, window] += mm(stack_heads_t(grad_t[:, rows]), weights)
    dk_rows = dk[...].T
    dv_rows = dv[...].T
    back_ref[0] = dk_rows[:REACH].astype(bf16)
    back_ref[1] = dv_rows[:REACH].astype(bf16)
    dk_ref[...] = dk_rows[REACH:]
    dv_ref[...] = dv_rows[REACH:]

    by_offset[:, WINDOW:] = jnp.zeros((2 * QUERY_BLOCK, 4 * QUERY_BLOCK - WINDOW), f32)
    row_index = iota((QUERY_BLOCK, 4 * QUERY_BLOCK), 0)
    for head in range(2):
        tile = by_offset[head * QUERY_BLOCK : (head + 1) * QUERY_BLOCK, :]
        for bit in range(QUERY_BLOCK.bit_length() - 1):
            moved = pltpu.roll(tile, 4 * QUERY_BLOCK - (1 << bit), 1)
            tile = jnp.where((row_index >> bit) & 1 == 1, moved, tile)
        offsets[pl.ds(2 * (begin + step) + head, 1), :] = jnp.sum(tile, axis=0, keepdims=True)

    @pl.when(step == 0)
    def _():
        if begin:
            offsets[0 : 2 * begin] = jnp.zeros((2 * begin, offsets.shape[1]), f32)
        else:
            offsets[2:HEADS] = jnp.zeros((HEADS - 2, offsets.shape[1]), f32)

    @pl.when(step == pl.num_programs(0) - 1)
    def _():
        _, chosen = offset_bucket()
        table_ref[...] = lax.dot_general(
            chosen.astype(f32), offsets[0:HEADS], (((1,), (1,)), ((), ())),
            precision=lax.Precision.HIGHEST, preferred_element_type=f32,
        )


def input_kernel(
    dq_ref, dkl_ref, dvl_ref, wq_ref, wk_ref, wv_ref, x_ref, dx1_ref, gain_ref, dx_ref, gg_ref
):
    dh = (
        mm_t(dq_ref[...], wq_ref[...])
        + mm_t(dkl_ref[...], wk_ref[...])
        + mm_t(dvl_ref[...], wv_ref[...])
    )
    back, gain_grad = rms_back(x_ref[...].astype(f32), gain_of(gain_ref), dh)
    dx_ref[...] = dx1_ref[...] + back
    gg_ref[...] = gain_grad


def put_tiles(out_ref, info, side, offset, found, shards):
    rows = found.shape[0] // shards
    first = HEADER + side * shards
    for shard in range(shards):
        for tile in range(found.shape[1] // LANES):
            piece = found[
                shard * rows : (shard + 1) * rows, tile * LANES : (tile + 1) * LANES
            ].astype(bf16)
            out_ref[
                info[first + shard], offset + tile * rows : offset + (tile + 1) * rows, :
            ] = piece


def gate_up_kernel(shards, info, h_ref, gk_ref, gs_ref, uk_ref, us_ref, keep_ref, send_ref, h_t):
    @pl.when(pl.program_id(0) == 0)
    def _():
        h_t[...] = h_ref[...].T

    half = keep_ref.shape[1] // 2
    put_tiles(keep_ref, info, 0, 0, mm(h_t[...], gk_ref[...]), shards)
    put_tiles(send_ref, info, 1, 0, mm(h_t[...], gs_ref[...]), shards)
    put_tiles(keep_ref, info, 0, half, mm(h_t[...], uk_ref[...]), shards)
    put_tiles(send_ref, info, 1, half, mm(h_t[...], us_ref[...]), shards)


def down_kernel(shards, info, u_ref, c_ref, keep_ref, send_ref, u_t, found):
    @pl.when(pl.program_id(0) == 0)
    def _():
        u_t[...] = u_ref[...].T

    found[...] = mm(u_t[...], c_ref[...])
    rows = found.shape[0] // shards // 2
    for shard in range(shards):
        for which, out_ref in enumerate((keep_ref, send_ref)):
            side = info[1] ^ which
            start = pl.multiple_of((2 * shard + side) * rows, rows)
            piece = found[pl.ds(start, rows), :].astype(bf16)
            for tile in range(found.shape[1] // LANES):
                out_ref[info[HEADER + (2 + which) * shards + shard], tile * rows : (tile + 1) * rows, :] = piece[
                    :, tile * LANES : (tile + 1) * LANES
                ]


def square_kernel(shards, count, info, *refs):
    sides = refs[: 3 * count]
    keep_ref, send_ref = refs[3 * count :]
    rows = keep_ref.shape[1] // count
    for index in range(count):
        left_ref, own_ref, other_ref = sides[3 * index : 3 * index + 3]
        left = left_ref[...].T
        put_tiles(keep_ref, info, 0, index * rows, mm(left, own_ref[...]), shards)
        put_tiles(send_ref, info, 1, index * rows, mm(left, other_ref[...]), shards)


def memory_back_kernel(chunks, shards, info, memory_ref, wk_ref, wv_ref, *refs):
    parts = refs[:chunks]
    keep_ref, send_ref, dm_ref, found, grad, memory_t = refs[chunks + 2 :]
    columns = found.shape[1] // 2

    def add(which, weight_ref):
        total = parts[0][which].astype(f32)
        for other in parts[1:]:
            total = total + other[which].astype(f32)
        grad[...] = total.astype(bf16)
        share = mm_t(grad[...], weight_ref[...])
        dm_ref[...] = share if which == 0 else dm_ref[...] + share

    @pl.when(pl.program_id(0) == 0)
    def _():
        memory_t[...] = memory_ref[...].T
        add(0, wk_ref)

    @pl.when(pl.program_id(0) == 1)
    def _():
        add(1, wv_ref)

    found[...] = mm(memory_t[...], grad[...])
    for flip, out_ref in enumerate((keep_ref, send_ref)):
        start = pl.multiple_of((info[1] ^ flip) * columns, LANES)
        put_tiles(out_ref, info, flip, 0, found[:, pl.ds(start, columns)], shards)


def keys_values_kernel(
    shards, info, h_ref, dk_ref, dv_ref, ret_ref, keep_in, send_in,
    keep_ref, send_ref, dkl_ref, dvl_ref, found,
):
    head = h_ref.shape[0] - REACH
    rows = keep_ref.shape[1] // 2
    columns = found.shape[1] // 2
    left = h_ref[...].T
    for which, own, low in ((0, dk_ref, dkl_ref), (1, dv_ref, dvl_ref)):
        low[:head, :] = own[:head, :].astype(bf16)
        low[head:, :] = (own[head:, :] + ret_ref[which].astype(f32)).astype(bf16)
        found[...] = mm(left, low[...])
        for flip, out_ref in enumerate((keep_ref, send_ref)):
            start = pl.multiple_of((info[1] ^ flip) * columns, LANES)
            half = found[:, pl.ds(start, columns)]
            put_tiles(out_ref, info, flip, which * rows, half, shards)


def small_kernel(
    shards, info, ga_ref, gc_ref, gf_ref, table_ref, table_more, keep_ref, send_ref
):
    width = ga_ref.shape[1]
    size = width // shards
    column = iota((shards, width), 1)
    shard = iota((shards, width), 0)
    own = (column >= shard * size) & (column < (shard + 1) * size)
    to_lane = iota((width, LANES), 0)
    for _ in range(shards - 1):
        to_lane = jnp.where(to_lane >= size, to_lane - size, to_lane)
    pick = (to_lane == iota((width, LANES), 1)).astype(bf16)
    gains = []
    for ref in (ga_ref, gc_ref, gf_ref):
        spread = jnp.where(own, jnp.broadcast_to(ref[...], (shards, width)), 0.0).astype(bf16)
        gains.append(mm(spread, pick))
    table_rows = BUCKETS // shards
    table = jnp.concatenate(
        [table_ref[...] + table_more[...], jnp.zeros((BUCKETS, LANES - HEADS), f32)], axis=1
    )
    for index in range(shards):
        pieces = [g[index : index + 1] for g in gains]
        pieces.append(table[index * table_rows : (index + 1) * table_rows])
        pieces.append(jnp.zeros((16 - 3 - table_rows, LANES), f32))
        tile = jnp.concatenate(pieces, axis=0).astype(bf16)
        for which, out_ref in enumerate((keep_ref, send_ref)):
            out_ref[info[HEADER + which * shards + index]] = tile


def sum_kernel(*refs):
    total = refs[0][...].astype(f32)
    for ref in refs[1:-1]:
        total = total + ref[...].astype(f32)
    refs[-1][...] = total.astype(bf16)


def halves(info, own_ref, other_ref):
    own, other = own_ref[...].astype(f32), other_ref[...].astype(f32)
    first = info[1] == 0
    return jnp.where(first, own, other), jnp.where(first, other, own)


def fill_square(out_ref, sides, offset):
    rows, columns = out_ref.shape
    count = columns // LANES // 2
    for side, found in enumerate(sides):
        for tile in range(count):
            start = (side * count + tile) * LANES
            out_ref[:, start : start + LANES] = found[
                offset + tile * rows : offset + (tile + 1) * rows
            ]


def gate_unpack_kernel(info, own_ref, other_ref, gate_ref, up_ref):
    rows, columns = gate_ref.shape
    count = columns // LANES // 2
    for side, found in enumerate(halves(info, own_ref, other_ref)):
        for tile in range(count):
            start = (side * count + tile) * LANES
            at = (tile // 2) * 4 * rows + (tile % 2) * rows
            gate_ref[:, start : start + LANES] = found[at : at + rows]
            up_ref[:, start : start + LANES] = found[at + 2 * rows : at + 3 * rows]


def down_unpack_kernel(info, own_ref, other_ref, down_ref):
    half = down_ref.shape[0] // 2
    for side, found in enumerate(halves(info, own_ref, other_ref)):
        for tile in range(down_ref.shape[1] // LANES):
            down_ref[side * half : (side + 1) * half, tile * LANES : (tile + 1) * LANES] = found[
                tile * half : (tile + 1) * half
            ]


def square_unpack_kernel(info, own_ref, other_ref, *out_refs):
    sides = halves(info, own_ref, other_ref)
    offset = 0
    for out_ref in out_refs:
        fill_square(out_ref, sides, offset)
        offset += out_ref.shape[0] * (out_ref.shape[1] // LANES // 2)


def whole(shape):
    return pl.BlockSpec(shape, lambda *_: (0,) * len(shape))


def call(kernel, name, grid, ins, outs, args, scalars=(), scratch=(), alias=None):
    shapes = [jax.ShapeDtypeStruct(shape, dtype) for shape, dtype, _ in outs]
    return pl.pallas_call(
        kernel,
        out_shape=shapes,
        grid_spec=pltpu.PrefetchScalarGridSpec(
            num_scalar_prefetch=len(scalars),
            grid=grid,
            in_specs=list(ins),
            out_specs=[spec for _, _, spec in outs],
            scratch_shapes=list(scratch),
        ),
        input_output_aliases=alias or {},
        compiler_params=pltpu.CompilerParams(
            dimension_semantics=("arbitrary",) * len(grid), vmem_limit_bytes=VMEM_BYTES
        ),
        cost_estimate=pl.CostEstimate(flops=int(TIMES[name] * COVER), bytes_accessed=1, transcendentals=0),
        name=name,
    )(*scalars, *args)


def full(*arrays):
    return [whole(a.shape) for a in arrays]


def bit_orders(bits, last_first):
    low, high = list(range(min(bits, 2))), list(range(2, bits))
    first, second = (low + high[::-1], low[::-1] + high)
    if last_first:
        first, second = (high[::-1] + low, high + low[::-1])
    return [first, second]


def info_table(wide_size, narrow_size, order_pairs):
    bits = wide_size.bit_length() - 1
    rows = []
    for w in range(wide_size):
        for n in range(narrow_size):
            side = n % 2
            row = [w, side, side, w * (narrow_size // 2) + n // 2, n]
            row += [0] * (HEADER - len(row))
            for pair in order_pairs:
                for order in (pair[side], pair[1 - side]):
                    for shard in range(wide_size):
                        apart = shard ^ w
                        slot = [((apart >> bit) & 1) << (bits - 1 - k) for k, bit in enumerate(order)]
                        row.append(sum(slot))
            rows.append(row)
    return np.array(rows, np.int32)


def shards(
    inputs, memory, cotangent, answer_lengths, answer_groups, memory_lengths,
    gain_attn, self_query, self_key, self_value, self_out, bucket_bias_table,
    gain_cross, cross_query, cross_key_matrix, cross_value, cross_out,
    gain_ffn, hidden_gate, hidden_up, hidden_down,
):
    tokens, width = inputs.shape
    answer_lengths, answer_groups = answer_lengths.T, answer_groups.T
    part = memory.shape[0]
    hidden = hidden_gate.shape[1]
    wide_size = lax.axis_size("wide")
    narrow_size = lax.axis_size("narrow")
    wide_index = lax.axis_index("wide")
    narrow_index = lax.axis_index("narrow")
    bits = wide_size.bit_length() - 1
    orders = bit_orders(bits, False)
    orders_last_first = bit_orders(bits, True)
    info = jnp.asarray(info_table(wide_size, narrow_size, (orders, orders_last_first)))
    info = lax.dynamic_slice(
        info, (wide_index * narrow_size + narrow_index, 0), (1, info.shape[1])
    )
    info = info.reshape(-1)
    gains = (gain_attn, gain_cross, gain_ffn)

    both = ("wide", "narrow")

    def to_narrow(value, target):
        pairs = [(n, target(n)) for n in range(narrow_size) if target(n) is not None]
        return lax.ppermute(value, "narrow", pairs)

    def to_wide(value, place, order_pair):
        pairs = []
        for w in range(wide_size):
            for n in range(narrow_size):
                partner = w ^ (1 << order_pair[n % 2][place])
                pairs.append((w * narrow_size + n, partner * narrow_size + n))
        return lax.ppermute(value, both, pairs)

    def after(values, *needed):
        return lax.optimization_barrier((tuple(values), needed))[0]

    turn = []

    def now(*values):
        return after(values, *turn) if turn else values

    def run(kernel, name, grid, ins, outs, args, **more):
        found = call(kernel, name, grid, ins, outs, (*now(args[0]), *args[1:]), **more)
        turn[:] = found[:1]
        return found

    class Group:
        def __init__(self, keep, send, order_pair=orders):
            self.pieces, self.place, self.count = [keep], 0, wide_size
            self.order_pair = order_pair
            self.pending = to_narrow(send, lambda n: n ^ 1)

        def total(self, first, count):
            pieces = (*self.pieces, self.pending)
            rows, lanes = pieces[0].shape[1:]
            parts = 2 if count * rows >= 4096 and rows % 32 == 0 else 1
            spec = lambda at: pl.BlockSpec(
                (count, rows // parts, lanes), lambda j: (at, j, 0)
            )
            shape = (count, rows, lanes)
            (found,) = run(
                sum_kernel, "partial_sum", (parts,), [spec(first)] * len(pieces),
                [(shape, bf16, spec(0))], pieces,
            )
            self.pieces = list(pieces)
            return found

        def step(self):
            self.count //= 2
            self.pending = to_wide(self.total(1, self.count), self.place, self.order_pair)
            self.place += 1

        def finish(self):
            while self.place < bits:
                self.step()
            total = self.total(0, 1)
            step = 2
            while step < narrow_size:
                self.pieces, self.pending = [total], to_narrow(total, lambda n, s=step: n ^ s)
                total = self.total(0, 1)
                step *= 2
            return total[0], to_narrow(total, lambda n: n ^ 1)[0]

    block = lambda rows: pl.BlockSpec((rows, PAIR), lambda j, *_: (0, j))
    out_rows = pl.BlockSpec((PAIR, width), lambda j, *_: (j, 0))

    model = (tokens, width)
    square = (width, width)
    in_hbm = pl.BlockSpec(memory_space=pltpu.HBM)
    normed, keys, values, tail, memory_own = run(
        project_kernel, "projections", (1,),
        [whole((width,))] + [in_hbm] * 6,
        [(model, bf16, whole(model))] * 3
        + [((2, REACH, width), bf16, whole((2, REACH, width)))]
        + [((2, part, width), bf16, whole((2, part, width)))],
        (gains[0],)
        + tuple(
            pltpu.with_memory_space_constraint(a, pltpu.HBM)
            for a in (inputs, memory, self_key, self_value, cross_key_matrix, cross_value)
        ),
        scratch=(pltpu.VMEM(model, bf16), pltpu.VMEM((part, width), bf16))
        + (pltpu.VMEM(square, bf16),) * 4
        + (pltpu.SemaphoreType.DMA((6,)),),
    )
    halo = to_narrow(tail, lambda n: n + 1 if n % 2 == 0 else None)
    memory_parts = [memory_own] + [
        to_narrow(memory_own, lambda n, s=shift: (n + s) % narrow_size)
        for shift in range(1, narrow_size)
    ]

    queries, bias = run(
        query_kernel, "queries", (1,),
        [whole(model), in_hbm, whole((HEADS, BUCKETS))],
        [
            (model, bf16, whole(model)),
            ((HEADS * QUERY_BLOCK, WINDOW), f32, whole((HEADS * QUERY_BLOCK, WINDOW))),
        ],
        (normed, pltpu.with_memory_space_constraint(self_query, pltpu.HBM), bucket_bias_table.T),
        scratch=(pltpu.VMEM(square, bf16), pltpu.SemaphoreType.DMA),
    )

    halo_block = pl.BlockSpec((2, REACH, PAIR), lambda j, *_: (0, 0, j))
    blocks = tokens // QUERY_BLOCK
    self_probs = pl.BlockSpec(
        (1, blocks, 2 * QUERY_BLOCK, WINDOW), lambda j, *_: (j, 0, 0, 0)
    )
    attended, inverse, probs, x1, normed_two, cross_rows = run(
        self_forward_kernel, "self_forward", (PAIRS,),
        [block(tokens)] * 3 + [halo_block]
        + [pl.BlockSpec((2 * QUERY_BLOCK, WINDOW), lambda j, *_: (j, 0)), whole(model), out_rows]
        + full(gains[1], cross_query),
        [
            (model, bf16, block(tokens)),
            (model, f32, block(tokens)),
            ((PAIRS, blocks, 2 * QUERY_BLOCK, WINDOW), bf16, self_probs),
            (model, f32, whole(model)),
            (model, bf16, whole(model)),
            (model, bf16, whole(model)),
        ],
        (queries, keys, values, halo, bias, inputs, self_out, gains[1], cross_query),
        scalars=(info, answer_lengths),
        scratch=(
            pltpu.VMEM((tokens + REACH, PAIR), bf16),
            pltpu.VMEM((tokens + REACH, 2 * PAIR), bf16),
            pltpu.VMEM((tokens, LANES), jnp.int32),
        ),
    )

    memory_tokens = part * narrow_size
    memory_block = pl.BlockSpec((2, part, PAIR), lambda j, *_: (0, 0, j))
    cross_blocks = tokens // CROSS_BLOCK
    cross_probs = pl.BlockSpec(
        (1, cross_blocks, 2 * CROSS_BLOCK, memory_tokens), lambda j, *_: (j, 0, 0, 0)
    )
    attended_two, inverse_two, probs_two, x2, normed_three = run(
        functools.partial(cross_forward_kernel, narrow_size), "cross_forward", (PAIRS,),
        [block(tokens), whole(model), out_rows, whole((width,))] + [memory_block] * narrow_size,
        [
            (model, bf16, block(tokens)),
            (model, f32, block(tokens)),
            ((PAIRS, cross_blocks, 2 * CROSS_BLOCK, memory_tokens), bf16, cross_probs),
            (model, f32, whole(model)),
            (model, bf16, whole(model)),
        ],
        (cross_rows, x1, cross_out, gains[2], *memory_parts),
        scalars=(info, answer_lengths, answer_groups, memory_lengths),
        scratch=(
            pltpu.VMEM((memory_tokens, PAIR), bf16),
            pltpu.VMEM((memory_tokens, 2 * PAIR), bf16),
            pltpu.VMEM((tokens, LANES), jnp.int32),
            pltpu.VMEM((8, memory_tokens), jnp.int32),
        ),
    )

    tile = 512
    wide_tile = pl.BlockSpec((width, tile), lambda j, *_: (0, j))
    token_tile = pl.BlockSpec((tokens, tile), lambda j, *_: (0, j))
    hidden_shape = (tokens, hidden)
    unit, grad_gate, grad_up, layer_out, dx2, e2, gain_grad_ffn = run(
        ffn_kernel, "feed_forward", (hidden // tile,),
        [whole(model)] * 3
        + [whole((width,)), wide_tile, wide_tile]
        + [pl.BlockSpec((tile, width), lambda j, *_: (j, 0))],
        [(hidden_shape, bf16, token_tile)] * 3
        + [
            (model, bf16, whole(model)),
            (model, f32, whole(model)),
            (model, bf16, whole(model)),
            ((1, width), f32, whole((1, width))),
        ],
        (normed_three, cotangent, x2, gains[2], hidden_gate, hidden_up, hidden_down),
        scratch=(pltpu.VMEM(model, f32), pltpu.VMEM(model, f32)),
    )

    square_rows = width // wide_size * (width // 2 // LANES)
    gate_rows = width // wide_size * (hidden // 2 // LANES)
    down_rows = hidden // wide_size // 2 * (width // LANES)
    step_rows = gate_rows // 2
    gate_side = lambda flip: pl.BlockSpec(
        (tokens, 256), lambda j, info: (0, (info[1] ^ flip) * (hidden // 512) + j)
    )
    half_side = lambda flip: pl.BlockSpec(
        (tokens, width // 2), lambda j, info: (0, info[1] ^ flip)
    )
    anywhere = pl.BlockSpec(memory_space=pl.ANY)

    gate_shape = (wide_size, 2 * gate_rows, LANES)
    step_spec = pl.BlockSpec((wide_size, step_rows, LANES), lambda j, *_: (0, j, 0))
    keep, send = run(
        functools.partial(gate_up_kernel, wide_size), "gate_up_gradient", (hidden // 512,),
        [whole(model), gate_side(0), gate_side(1), gate_side(0), gate_side(1)],
        [(gate_shape, bf16, step_spec)] * 2,
        (normed_three, grad_gate, grad_gate, grad_up, grad_up),
        scalars=(info,),
        scratch=(pltpu.VMEM((width, tokens), bf16),),
    )
    gate_group = Group(keep, send)
    down_shape = (wide_size, down_rows, LANES)
    down_spec = pl.BlockSpec((wide_size, down_rows // 2, LANES), lambda j, *_: (0, j, 0))
    keep, send = run(
        functools.partial(down_kernel, wide_size), "down_gradient", (2,),
        [whole(hidden_shape), pl.BlockSpec((tokens, width // 2), lambda j, *_: (0, j))],
        [(down_shape, bf16, down_spec)] * 2,
        (unit, cotangent),
        scalars=(info,),
        scratch=(
            pltpu.VMEM((hidden, tokens), bf16),
            pltpu.VMEM((hidden, width // 2), f32),
        ),
    )
    down_group = Group(keep, send, orders_last_first)
    gate_group.step()

    grad_cross_rows, dx1, e1, gain_grad_cross, *memory_grads = run(
        functools.partial(cross_backward_kernel, narrow_size), "cross_backward", (PAIRS,),
        [whole(model), out_rows, block(tokens), block(tokens), cross_probs, block(tokens)]
        + [block(width), whole(model), whole(model), whole((width,))]
        + [memory_block] * narrow_size,
        [
            (model, bf16, block(tokens)),
            (model, f32, whole(model)),
            (model, bf16, whole(model)),
            ((1, width), f32, whole((1, width))),
        ]
        + [((2, part, width), bf16, memory_block)] * narrow_size,
        (e2, cross_out, attended_two, inverse_two, probs_two, cross_rows, cross_query, x1, dx2)
        + (gains[1], *memory_parts),
        scratch=(
            pltpu.VMEM((memory_tokens, PAIR), bf16),
            pltpu.VMEM((memory_tokens, PAIR), bf16),
            pltpu.VMEM((PAIR, memory_tokens), f32),
            pltpu.VMEM((PAIR, memory_tokens), f32),
            pltpu.VMEM(model, f32),
        ),
    )
    memory_shares = [memory_grads[0]] + [
        to_narrow(memory_grads[shift], lambda n, s=shift: (n - s) % narrow_size)
        for shift in range(1, narrow_size)
    ]
    down_group.step()
    second_shape = (wide_size, 5 * square_rows, LANES)
    triple = ((attended_two, e2), (normed_two, grad_cross_rows), (attended, e1))
    second_spec = pl.BlockSpec((wide_size, 3 * square_rows, LANES), lambda j, *_: (0, 0, 0))
    keep, send = run(
        functools.partial(square_kernel, wide_size, 3), "square_gradients", (1,),
        [whole(model), half_side(0), half_side(1)] * 3,
        [(second_shape, bf16, second_spec)] * 2,
        [side_of for left, right in triple for side_of in (left, right, right)],
        scalars=(info,),
    )
    gate_group.step()
    memory_spec = pl.BlockSpec((wide_size, square_rows, LANES), lambda j, *_: (0, 3 + j, 0))
    keep, send, memory_grad = run(
        functools.partial(memory_back_kernel, narrow_size, wide_size), "memory_backward", (2,),
        full(memory, cross_key_matrix, cross_value, *memory_shares) + [anywhere] * 2,
        [(second_shape, bf16, memory_spec)] * 2
        + [((part, width), f32, whole((part, width)))],
        (memory, cross_key_matrix, cross_value, *memory_shares, keep, send),
        scalars=(info,),
        scratch=(
            pltpu.VMEM((width, width), f32),
            pltpu.VMEM((part, width), bf16),
            pltpu.VMEM((width, part), bf16),
        ),
        alias={4 + narrow_size: 0, 5 + narrow_size: 1},
    )
    second_group = Group(keep, send)

    tables, carried, parts_of = [], [], 2
    for index in range(parts_of):
        count = PAIRS // parts_of
        begin = index * count
        at = lambda rows, b=begin: pl.BlockSpec((rows, PAIR), lambda j, *_: (0, b + j))
        here = lambda *lead, b=begin: pl.BlockSpec(
            (1, *lead), lambda j, *_: (b + j,) + (0,) * len(lead)
        )
        halo_at = pl.BlockSpec((2, REACH, PAIR), lambda j, *_, b=begin: (0, 0, b + j))
        out_at = pl.BlockSpec((PAIR, width), lambda j, *_, b=begin: (b + j, 0))
        if index:
            second_group.step()
            down_group.step()
            gate_group.step()
        *carried, table = run(
            functools.partial(self_backward_kernel, begin), "self_backward", (count,),
            [whole(model), out_at, at(tokens), at(tokens)]
            + [here(blocks, 2 * QUERY_BLOCK, WINDOW)]
            + [at(tokens)] * 3 + [halo_at] + [anywhere] * len(carried),
            [
                (model, bf16, at(tokens)),
                (model, f32, at(tokens)),
                (model, f32, at(tokens)),
                ((2, REACH, width), bf16, halo_at),
                ((BUCKETS, HEADS), f32, whole((BUCKETS, HEADS))),
            ],
            (e1, self_out, attended, inverse, probs, queries, keys, values, halo, *carried),
            scratch=(
                pltpu.VMEM((tokens + REACH, PAIR), bf16),
                pltpu.VMEM((tokens + REACH, PAIR), bf16),
                pltpu.VMEM((PAIR, tokens + REACH), f32),
                pltpu.VMEM((PAIR, tokens + REACH), f32),
                pltpu.VMEM((2 * QUERY_BLOCK, 4 * QUERY_BLOCK), f32),
                pltpu.VMEM((16, 4 * QUERY_BLOCK), f32),
            ),
            alias={9 + i: i for i in range(4)} if index else None,
        )
        tables.append(table)
    grad_queries, grad_keys, grad_values, back = carried
    returned = to_narrow(back, lambda n: n - 1 if n % 2 == 1 else None)
    last_shape = (wide_size, 3 * square_rows, LANES)
    query_spec = pl.BlockSpec((wide_size, square_rows, LANES), lambda j, *_: (0, 2, 0))
    down_group.step()
    gate_group.step()
    keep, send = run(
        functools.partial(square_kernel, wide_size, 1), "query_gradient", (1,),
        [whole(model), half_side(0), half_side(1)],
        [(last_shape, bf16, query_spec)] * 2,
        (normed, grad_queries, grad_queries),
        scalars=(info,),
    )
    pair_spec = pl.BlockSpec((wide_size, 2 * square_rows, LANES), lambda j, *_: (0, 0, 0))
    keep, send, keys_low, values_low = run(
        functools.partial(keys_values_kernel, wide_size), "key_value_gradient", (1,),
        full(normed, grad_keys, grad_values, returned) + [anywhere] * 2,
        [(last_shape, bf16, pair_spec)] * 2 + [(model, bf16, whole(model))] * 2,
        (normed, grad_keys, grad_values, returned, keep, send),
        scalars=(info,),
        scratch=(pltpu.VMEM(square, f32),),
        alias={5: 0, 6: 1},
    )
    last_group = Group(keep, send)
    second_group.step()
    input_grad, gain_grad_attn = run(
        input_kernel, "input_gradient", (1,),
        full(grad_queries, keys_low, values_low)
        + full(self_query, self_key, self_value, inputs, dx1, gains[0]),
        [
            (model, f32, whole(model)),
            ((1, width), f32, whole((1, width))),
        ],
        (grad_queries, keys_low, values_low)
        + (self_query, self_key, self_value, inputs, dx1, gains[0]),
    )
    last_group.step()
    small_shape = (wide_size, 16, LANES)
    keep, send = run(
        functools.partial(small_kernel, wide_size), "gains", (1,),
        [whole((1, width))] * 3 + [whole((BUCKETS, HEADS))] * 2,
        [(small_shape, bf16, whole(small_shape))] * 2,
        (gain_grad_attn, gain_grad_cross, gain_grad_ffn, *tables),
        scalars=(info,),
    )
    small_group = Group(keep, send)
    square_out = ((width // wide_size, width), f32, whole((width // wide_size, width)))
    gate_out = ((width // wide_size, hidden), f32, whole((width // wide_size, hidden)))
    down_out = ((hidden // wide_size, width), f32, whole((hidden // wide_size, width)))
    gate_own, gate_other = gate_group.finish()
    second_group.step()
    small_group.step()
    last_group.step()
    down_group.step()
    grad_gate_w, grad_up_w = run(
        gate_unpack_kernel, "gate_outputs", (1,), full(gate_own, gate_other),
        [gate_out] * 2, (gate_own, gate_other), scalars=(info,),
    )
    small_group.step()
    second_group.step()
    down_own, down_other = down_group.finish()
    last_group.step()
    small_group.step()
    (grad_down_w,) = run(
        down_unpack_kernel, "down_outputs", (1,), full(down_own, down_other),
        [down_out], (down_own, down_other), scalars=(info,),
    )
    second_own, second_other = second_group.finish()
    last_group.step()
    small_group.step()
    grad_cross_out, grad_cross_query, grad_self_out, grad_cross_key, grad_cross_value = run(
        square_unpack_kernel, "second_outputs", (1,), full(second_own, second_other),
        [square_out] * 5, (second_own, second_other), scalars=(info,),
    )
    last_own, last_other = last_group.finish()
    small_own, _ = small_group.finish()
    grad_self_key, grad_self_value, grad_self_query = run(
        square_unpack_kernel, "last_outputs", (1,), full(last_own, last_other),
        [square_out] * 3, (last_own, last_other), scalars=(info,),
    )
    misc = small_own.astype(f32)
    size = width // wide_size
    table_rows = BUCKETS // wide_size
    return (
        layer_out,
        input_grad,
        memory_grad,
        misc[0, :size],
        grad_self_query,
        grad_self_key,
        grad_self_value,
        grad_self_out,
        misc[3 : 3 + table_rows, :HEADS],
        misc[1, :size],
        grad_cross_query,
        grad_cross_key,
        grad_cross_value,
        grad_cross_out,
        misc[2, :size],
        grad_gate_w,
        grad_up_w,
        grad_down_w,
    )


def solution(mesh):
    rows = P(("wide", "narrow"), None)
    vector, matrix = P("wide"), P("wide", None)
    return jax.shard_map(
        shards,
        mesh=mesh,
        in_specs=(rows,) * 3 + (P(),) * 18,
        out_specs=(rows,) * 3
        + (vector,)
        + (matrix,) * 5
        + (vector,)
        + (matrix,) * 4
        + (vector,)
        + (matrix,) * 3,
        check_vma=False,
    )
```

```python
import functools
import math

import jax
import jax.numpy as jnp
import numpy as np
from jax import lax
from jax.experimental import pallas as pl
from jax.experimental.pallas import tpu as pltpu
from jax.sharding import PartitionSpec as P

HEADS = 12
HEAD_DIM = 64
BUCKETS = 32
MAX_DIST = 128
ANSWERS = 8
GROUPS = 16
PAIR = 2 * HEAD_DIM
PAIRS = HEADS // 2
REACH = 256
QUERY_BLOCK = 128
WINDOW = REACH + QUERY_BLOCK
CROSS_BLOCK = 256
LANES = 128
HEADER = 8
GRANTS = {
    "projections": 14,
    "queries": 8,
    "self_forward": 14,
    "cross_forward": 12,
    "feed_forward": 24,
    "gate_up_gradient": 14,
    "down_gradient": 16,
    "cross_backward": 16,
    "square_gradients": 16,
    "memory_backward": 14,
    "self_backward_first": 14,
    "self_backward": 14,
    "query_gradient": 8,
    "key_value_gradient": 14,
    "input_gradient": 16,
    "partial_sum": 12,
    "partial_sum_late": 12,
    "partial_sum_beside": 12,
    "gate_outputs": 6,
    "down_outputs": 6,
    "second_outputs": 6,
    "last_outputs": 6,
}
TIMES = {
    "projections": 5.0,
    "queries": 3.0,
    "self_forward": 12.0,
    "cross_forward": 10.5,
    "feed_forward": 15.0,
    "gate_up_gradient": 6.0,
    "down_gradient": 4.4,
    "cross_backward": 12.0,
    "square_gradients": 2.0,
    "memory_backward": 3.6,
    "self_backward_first": 30.0,
    "self_backward": 7.0,
    "query_gradient": 9.0,
    "key_value_gradient": 2.4,
    "input_gradient": 1.0,
    "partial_sum": 1.0,
    "partial_sum_late": 0.0,
    "partial_sum_beside": 20.0,
    "gate_outputs": 0.0,
    "down_outputs": 0.0,
    "second_outputs": 0.0,
    "last_outputs": 0.0,
}
COVER = 1.15e9

epsilon = 1e-06
neg_big = -1e30
f32 = jnp.float32
bf16 = jnp.bfloat16


def mm(left, right):
    return jnp.dot(left, right, preferred_element_type=f32)


def mm_t(left, right):
    return lax.dot_general(left, right, (((1,), (1,)), ((), ())), preferred_element_type=f32)


def rms(values, gain_row):
    factor = lax.rsqrt(jnp.mean(values * values, axis=-1, keepdims=True) + epsilon)
    return values * factor * gain_row


def rms_back(values, gain_row, grad):
    factor = lax.rsqrt(jnp.mean(values * values, axis=-1, keepdims=True) + epsilon)
    unit = values * factor
    scaled = grad * gain_row
    center = jnp.mean(scaled * unit, axis=-1, keepdims=True)
    return factor * (scaled - unit * center)


def bucket_of(distance):
    exact_count = BUCKETS // 2
    log_count = BUCKETS - exact_count
    near_part = jnp.minimum(jnp.maximum(distance, 0), exact_count)
    far_part = jnp.zeros_like(distance)
    for level_index in range(1, log_count):
        edge = math.ceil(exact_count * (MAX_DIST / exact_count) ** (level_index / log_count))
        far_part = far_part + (distance >= edge).astype(jnp.int32)
    return near_part + far_part


def gain_of(ref):
    return ref[...].astype(f32).reshape(1, ref.shape[0])


def iota(shape, axis):
    return lax.broadcasted_iota(jnp.int32, shape, axis)


def low_lanes(shape):
    return iota(shape, len(shape) - 1) < HEAD_DIM


def stack_heads(rows):
    low = low_lanes(rows.shape)
    zero = jnp.zeros_like(rows)
    return jnp.concatenate([jnp.where(low, rows, zero), jnp.where(low, zero, rows)], axis=0)


def stack_heads_t(columns):
    low = iota(columns.shape, 0) < HEAD_DIM
    zero = jnp.zeros_like(columns)
    return jnp.concatenate([jnp.where(low, columns, zero), jnp.where(low, zero, columns)], axis=1)


def join_heads(stacked):
    half = stacked.shape[0] // 2
    return jnp.where(low_lanes((half, PAIR)), stacked[:half], stacked[half:])


def offset_bucket():
    lane = iota((1, 4 * QUERY_BLOCK), 1)
    distance = jnp.where(lane < WINDOW, REACH - lane, REACH + 4 * QUERY_BLOCK - lane)
    chosen = iota((BUCKETS, 4 * QUERY_BLOCK), 0) == bucket_of(distance)
    return distance, chosen


def answer_ends(lengths, row):
    total, ends = lengths[0, row], []
    for index in range(1, ANSWERS):
        ends.append(total)
        total = total + lengths[index, row]
    return ends


def project_kernel(
    gain_ref, x_hbm, memory_hbm, wk_hbm, wv_hbm, wck_hbm, wcv_hbm,
    h_ref, k_ref, v_ref, tail_ref, memory_out,
    x_ref, memory_ref, wk_ref, wv_ref, wck_ref, wcv_ref, sems,
):
    copies = [
        pltpu.make_async_copy(source, target, sems.at[index])
        for index, (source, target) in enumerate(
            (
                (x_hbm, x_ref),
                (memory_hbm, memory_ref),
                (wck_hbm, wck_ref),
                (wcv_hbm, wcv_ref),
                (wk_hbm, wk_ref),
                (wv_hbm, wv_ref),
            )
        )
    ]
    for copy in copies:
        copy.start()
    copies[0].wait()
    h_ref[...] = rms(x_ref[...].astype(f32), gain_of(gain_ref)).astype(bf16)
    copies[1].wait()
    copies[2].wait()
    memory_out[0] = mm(memory_ref[...], wck_ref[...]).astype(bf16)
    copies[3].wait()
    memory_out[1] = mm(memory_ref[...], wcv_ref[...]).astype(bf16)
    tokens = h_ref.shape[0]
    copies[4].wait()
    k_ref[...] = mm(h_ref[...], wk_ref[...]).astype(bf16)
    tail_ref[0] = k_ref[tokens - REACH :, :]
    copies[5].wait()
    v_ref[...] = mm(h_ref[...], wv_ref[...]).astype(bf16)
    tail_ref[1] = v_ref[tokens - REACH :, :]


def query_kernel(h_ref, wq_hbm, table_ref, q_ref, bias_ref, wq_ref, sem):
    copy = pltpu.make_async_copy(wq_hbm, wq_ref, sem)
    copy.start()
    distance, chosen = offset_bucket()
    base = jnp.where(distance < 0, neg_big, mm(table_ref[...], chosen.astype(bf16)))
    for head in range(HEADS):
        spread = jnp.broadcast_to(base[head : head + 1], (QUERY_BLOCK, 4 * QUERY_BLOCK))
        skewed = pltpu.roll(spread, 0, 1, stride=1, stride_axis=0)
        bias_ref[head * QUERY_BLOCK : (head + 1) * QUERY_BLOCK, :] = skewed[:, :WINDOW]
    copy.wait()
    q_ref[...] = mm(h_ref[...], wq_ref[...]).astype(bf16)


def self_forward_kernel(
    info, lengths,
    q_ref, k_ref, v_ref, halo_ref, bias, x_ref, wo_ref, gain_ref, wq_ref,
    o_ref, inv_ref, e_ref, x1_ref, h2_ref, qc_ref,
    keys, values, reach,
):
    step = pl.program_id(0)
    tokens = q_ref.shape[0]

    @pl.when(step == 0)
    def _():
        place = info[2] * tokens + iota((tokens, LANES), 0)
        start = jnp.zeros_like(place)
        for end in answer_ends(lengths, info[3]):
            start = jnp.where(place >= end, end, start)
        reach[...] = place - start
        values[:, PAIR:] = jnp.ones((values.shape[0], PAIR), bf16)
        x1_ref[...] = x_ref[...].astype(f32)

    keys[0:REACH] = halo_ref[0]
    keys[REACH:] = k_ref[...]
    values[0:REACH, 0:PAIR] = halo_ref[1]
    values[REACH:, 0:PAIR] = v_ref[...]
    distance = REACH + iota((QUERY_BLOCK, WINDOW), 0) - iota((QUERY_BLOCK, WINDOW), 1)
    distance = jnp.concatenate([distance, distance], axis=0)
    for block in range(tokens // QUERY_BLOCK):
        rows = slice(block * QUERY_BLOCK, (block + 1) * QUERY_BLOCK)
        window = slice(block * QUERY_BLOCK, block * QUERY_BLOCK + WINDOW)
        scores = mm_t(stack_heads(q_ref[rows, :]), keys[window, :])
        own_reach = reach[rows, 0:1]
        own_reach = jnp.concatenate([own_reach, own_reach], axis=0)
        scores = jnp.where(distance <= own_reach, scores + bias[...], neg_big)
        top = jnp.max(scores, axis=-1, keepdims=True)
        weights = jnp.exp(scores - top).astype(bf16)
        e_ref[0, block] = weights
        mixed = mm(weights, values[window, :])
        inverse = 1.0 / mixed[:, PAIR:]
        o_ref[rows, :] = join_heads(mixed[:, :PAIR] * inverse).astype(bf16)
        inv_ref[rows, :] = join_heads(inverse)
    x1_ref[...] += mm(o_ref[...], wo_ref[...])

    @pl.when(step == PAIRS - 1)
    def _():
        h2_ref[...] = rms(x1_ref[...], gain_of(gain_ref)).astype(bf16)
        qc_ref[...] = mm(h2_ref[...], wq_ref[...]).astype(bf16)


def cross_forward_kernel(chunks, info, lengths, groups, bounds, *refs):
    q_ref, x1_ref, wo_ref, gain_ref = refs[:4]
    kv_refs = refs[4 : 4 + chunks]
    o_ref, inv_ref, e_ref, x2_ref, h3_ref = refs[4 + chunks : 9 + chunks]
    keys, values, query_group, key_group = refs[9 + chunks :]
    step = pl.program_id(0)
    tokens = q_ref.shape[0]
    part = kv_refs[0].shape[1]

    @pl.when(step == 0)
    def _():
        place = info[2] * tokens + iota((tokens, LANES), 0)
        group = jnp.zeros_like(place) + groups[0, info[3]]
        for index, end in enumerate(answer_ends(lengths, info[3])):
            group = jnp.where(place >= end, groups[index + 1, info[3]], group)
        query_group[...] = group
        total, ends = bounds[info[0], 0], []
        for index in range(1, GROUPS):
            ends.append(total)
            total = total + bounds[info[0], index]
        for chunk in range(chunks):
            owner = lax.rem(info[4] + chunks - chunk, chunks)
            token = owner * part + iota((8, part), 1)
            found = jnp.zeros_like(token)
            for end in ends:
                found = found + (token >= end).astype(jnp.int32)
            key_group[:, chunk * part : (chunk + 1) * part] = found
        values[:, PAIR:] = jnp.ones((values.shape[0], PAIR), bf16)
        x2_ref[...] = x1_ref[...]

    for chunk in range(chunks):
        keys[chunk * part : (chunk + 1) * part] = kv_refs[chunk][0]
        values[chunk * part : (chunk + 1) * part, 0:PAIR] = kv_refs[chunk][1]
    for block in range(tokens // CROSS_BLOCK):
        rows = slice(block * CROSS_BLOCK, (block + 1) * CROSS_BLOCK)
        scores = mm_t(stack_heads(q_ref[rows, :]), keys[...])
        own_group = query_group[rows, 0:1]
        own_group = jnp.concatenate([own_group, own_group], axis=0)
        scores = jnp.where(own_group == key_group[0:1, :], scores, neg_big)
        top = jnp.max(scores, axis=-1, keepdims=True)
        weights = jnp.exp(scores - top).astype(bf16)
        e_ref[0, block] = weights
        mixed = mm(weights, values[...])
        inverse = 1.0 / mixed[:, PAIR:]
        o_ref[rows, :] = join_heads(mixed[:, :PAIR] * inverse).astype(bf16)
        inv_ref[rows, :] = join_heads(inverse)
    x2_ref[...] += mm(o_ref[...], wo_ref[...])

    @pl.when(step == PAIRS - 1)
    def _():
        h3_ref[...] = rms(x2_ref[...], gain_of(gain_ref)).astype(bf16)


def ffn_kernel(
    h_ref, c_ref, x2_ref, gain_ref, wg_ref, wu_ref, wd_ref,
    u_ref, dga_ref, dgb_ref, out_ref, dx_ref, e_ref,
    total, dh,
):
    step = pl.program_id(0)
    gate = mm(h_ref[...], wg_ref[...])
    up = mm(h_ref[...], wu_ref[...])
    du = mm_t(c_ref[...], wd_ref[...])
    root = math.sqrt(2.0 / math.pi)
    square = gate * gate
    bent = jnp.tanh(root * gate * (1.0 + 0.044715 * square))
    share = 0.5 * (1.0 + bent)
    active = gate * share
    slope = share + 0.5 * gate * (1.0 - bent * bent) * (root * (1.0 + 3 * 0.044715 * square))
    u_ref[...] = (active * up).astype(bf16)
    dgb_ref[...] = (du * active).astype(bf16)
    dga_ref[...] = (du * up * slope).astype(bf16)
    out_part = mm(u_ref[...], wd_ref[...])
    dh_part = mm_t(dga_ref[...], wg_ref[...]) + mm_t(dgb_ref[...], wu_ref[...])

    @pl.when(step == 0)
    def _():
        total[...] = x2_ref[...] + out_part
        dh[...] = dh_part

    @pl.when(step > 0)
    def _():
        total[...] += out_part
        dh[...] += dh_part

    @pl.when(step == pl.num_programs(0) - 1)
    def _():
        out_ref[...] = total[...].astype(bf16)
        back = rms_back(x2_ref[...], gain_of(gain_ref), dh[...])
        dx_ref[...] = c_ref[...].astype(f32) + back
        e_ref[...] = dx_ref[...].astype(bf16)


def cross_backward_kernel(chunks, *refs):
    e2_ref, wo_ref, o_ref, inv_ref, p_ref, q_ref, wq_ref, x1_ref, dx2_ref, gain_ref = refs[:10]
    kv_refs = refs[10 : 10 + chunks]
    dq_ref, dx_ref, e1_ref = refs[10 + chunks : 13 + chunks]
    dkv_refs = refs[13 + chunks : 13 + 2 * chunks]
    keys, values, dk, dv, dh = refs[13 + 2 * chunks :]
    step = pl.program_id(0)
    tokens = q_ref.shape[0]
    part = kv_refs[0].shape[1]

    for chunk in range(chunks):
        keys[chunk * part : (chunk + 1) * part] = kv_refs[chunk][0]
        values[chunk * part : (chunk + 1) * part] = kv_refs[chunk][1]
    grad = mm_t(e2_ref[...], wo_ref[...]).astype(bf16).astype(f32)
    grad = (grad * inv_ref[...]).astype(bf16)
    query_t = q_ref[...].T
    grad_t = grad.T
    for block in range(tokens // CROSS_BLOCK):
        rows = slice(block * CROSS_BLOCK, (block + 1) * CROSS_BLOCK)
        own = grad[rows, :]
        weighed = own.astype(f32) * o_ref[rows, :].astype(f32)
        center = jnp.sum(stack_heads(weighed), axis=-1, keepdims=True)
        grad_probs = mm_t(stack_heads(own), values[...])
        weights = p_ref[0, block]
        grad_scores = (weights.astype(f32) * (grad_probs - center)).astype(bf16)
        dq_ref[rows, :] = join_heads(mm(grad_scores, keys[...])).astype(bf16)
        dk_part = mm(stack_heads_t(query_t[:, rows]), grad_scores)
        dv_part = mm(stack_heads_t(grad_t[:, rows]), weights)
        if block == 0:
            dk[...] = dk_part
            dv[...] = dv_part
        else:
            dk[...] += dk_part
            dv[...] += dv_part
    dk_rows = dk[...].T.astype(bf16)
    dv_rows = dv[...].T.astype(bf16)
    for chunk in range(chunks):
        dkv_refs[chunk][0] = dk_rows[chunk * part : (chunk + 1) * part]
        dkv_refs[chunk][1] = dv_rows[chunk * part : (chunk + 1) * part]
    dh_part = mm_t(dq_ref[...], wq_ref[...])

    @pl.when(step == 0)
    def _():
        dh[...] = dh_part

    @pl.when(step > 0)
    def _():
        dh[...] += dh_part

    @pl.when(step == PAIRS - 1)
    def _():
        back = rms_back(x1_ref[...], gain_of(gain_ref), dh[...])
        dx_ref[...] = dx2_ref[...] + back
        e1_ref[...] = dx_ref[...].astype(bf16)


def self_backward_kernel(
    begin, e1_ref, wo_ref, o_ref, inv_ref, p_ref, q_ref, k_ref, v_ref, halo_ref, *refs
):
    dq_ref, dk_ref, dv_ref, back_ref, table_ref, keys, values, dk, dv, by_offset, offsets = refs[
        -11:
    ]
    step = pl.program_id(0)
    tokens = q_ref.shape[0]
    keys[0:REACH] = halo_ref[0]
    keys[REACH:] = k_ref[...]
    values[0:REACH] = halo_ref[1]
    values[REACH:] = v_ref[...]
    grad = mm_t(e1_ref[...], wo_ref[...]).astype(bf16).astype(f32)
    grad = (grad * inv_ref[...]).astype(bf16)
    query_t = q_ref[...].T
    grad_t = grad.T
    dk[...] = jnp.zeros_like(dk)
    dv[...] = jnp.zeros_like(dv)
    for block in range(tokens // QUERY_BLOCK):
        rows = slice(block * QUERY_BLOCK, (block + 1) * QUERY_BLOCK)
        window = slice(block * QUERY_BLOCK, block * QUERY_BLOCK + WINDOW)
        own = grad[rows, :]
        weighed = own.astype(f32) * o_ref[rows, :].astype(f32)
        center = jnp.sum(stack_heads(weighed), axis=-1, keepdims=True)
        grad_probs = mm_t(stack_heads(own), values[window, :])
        weights = p_ref[0, block]
        exact = weights.astype(f32) * (grad_probs - center)
        if block == 0:
            by_offset[:, :WINDOW] = exact
        else:
            by_offset[:, :WINDOW] += exact
        grad_scores = exact.astype(bf16)
        dq_ref[rows, :] = join_heads(mm(grad_scores, keys[window, :])).astype(bf16)
        dk[:, window] += mm(stack_heads_t(query_t[:, rows]), grad_scores)
        dv[:, window] += mm(stack_heads_t(grad_t[:, rows]), weights)
    dk_rows = dk[...].T
    dv_rows = dv[...].T
    back_ref[0] = dk_rows[:REACH].astype(bf16)
    back_ref[1] = dv_rows[:REACH].astype(bf16)
    dk_ref[...] = dk_rows[REACH:]
    dv_ref[...] = dv_rows[REACH:]

    by_offset[:, WINDOW:] = jnp.zeros((2 * QUERY_BLOCK, 4 * QUERY_BLOCK - WINDOW), f32)
    row_index = iota((QUERY_BLOCK, 4 * QUERY_BLOCK), 0)
    for head in range(2):
        tile = by_offset[head * QUERY_BLOCK : (head + 1) * QUERY_BLOCK, :]
        for bit in range(QUERY_BLOCK.bit_length() - 1):
            moved = pltpu.roll(tile, 4 * QUERY_BLOCK - (1 << bit), 1)
            tile = jnp.where((row_index >> bit) & 1 == 1, moved, tile)
        offsets[pl.ds(2 * (begin + step) + head, 1), :] = jnp.sum(tile, axis=0, keepdims=True)

    @pl.when(step == 0)
    def _():
        if begin:
            offsets[0 : 2 * begin] = jnp.zeros((2 * begin, offsets.shape[1]), f32)
        else:
            offsets[2:HEADS] = jnp.zeros((HEADS - 2, offsets.shape[1]), f32)

    @pl.when(step == pl.num_programs(0) - 1)
    def _():
        _, chosen = offset_bucket()
        table_ref[...] = lax.dot_general(
            chosen.astype(f32), offsets[0:HEADS], (((1,), (1,)), ((), ())),
            precision=lax.Precision.HIGHEST, preferred_element_type=f32,
        )


def input_kernel(
    dq_ref, dkl_ref, dvl_ref, wq_ref, wk_ref, wv_ref, x_ref, dx1_ref, gain_ref, dx_ref
):
    dh = (
        mm_t(dq_ref[...], wq_ref[...])
        + mm_t(dkl_ref[...], wk_ref[...])
        + mm_t(dvl_ref[...], wv_ref[...])
    )
    back = rms_back(x_ref[...].astype(f32), gain_of(gain_ref), dh)
    dx_ref[...] = dx1_ref[...] + back


def put_tiles(out_ref, info, side, offset, found, shards):
    rows = found.shape[0] // shards
    first = HEADER + side * shards
    for shard in range(shards):
        for tile in range(found.shape[1] // LANES):
            piece = found[
                shard * rows : (shard + 1) * rows, tile * LANES : (tile + 1) * LANES
            ].astype(bf16)
            out_ref[
                info[first + shard], offset + tile * rows : offset + (tile + 1) * rows, :
            ] = piece


def gate_up_kernel(shards, info, h_ref, gk_ref, gs_ref, uk_ref, us_ref, keep_ref, send_ref, h_t):
    @pl.when(pl.program_id(0) == 0)
    def _():
        h_t[...] = h_ref[...].T

    half = keep_ref.shape[1] // 2
    put_tiles(keep_ref, info, 0, 0, mm(h_t[...], gk_ref[...]), shards)
    put_tiles(send_ref, info, 1, 0, mm(h_t[...], gs_ref[...]), shards)
    put_tiles(keep_ref, info, 0, half, mm(h_t[...], uk_ref[...]), shards)
    put_tiles(send_ref, info, 1, half, mm(h_t[...], us_ref[...]), shards)


def down_kernel(shards, info, u_ref, c_ref, keep_ref, send_ref, u_t, found):
    @pl.when(pl.program_id(0) == 0)
    def _():
        u_t[...] = u_ref[...].T

    found[...] = mm(u_t[...], c_ref[...])
    rows = found.shape[0] // shards // 2
    for shard in range(shards):
        for which, out_ref in enumerate((keep_ref, send_ref)):
            side = info[1] ^ which
            start = pl.multiple_of((2 * shard + side) * rows, rows)
            piece = found[pl.ds(start, rows), :].astype(bf16)
            for tile in range(found.shape[1] // LANES):
                out_ref[info[HEADER + (2 + which) * shards + shard], tile * rows : (tile + 1) * rows, :] = piece[
                    :, tile * LANES : (tile + 1) * LANES
                ]


def square_kernel(shards, count, info, *refs):
    sides = refs[: 3 * count]
    keep_ref, send_ref = refs[3 * count :]
    rows = keep_ref.shape[1] // count
    for index in range(count):
        left_ref, own_ref, other_ref = sides[3 * index : 3 * index + 3]
        left = left_ref[...].T
        put_tiles(keep_ref, info, 0, index * rows, mm(left, own_ref[...]), shards)
        put_tiles(send_ref, info, 1, index * rows, mm(left, other_ref[...]), shards)


def memory_back_kernel(chunks, shards, info, memory_ref, wk_ref, wv_ref, *refs):
    parts = refs[:chunks]
    keep_ref, send_ref, dm_ref, found, grad, memory_t = refs[chunks + 2 :]
    columns = found.shape[1] // 2

    def add(which, weight_ref):
        total = parts[0][which].astype(f32)
        for other in parts[1:]:
            total = total + other[which].astype(f32)
        grad[...] = total.astype(bf16)
        share = mm_t(grad[...], weight_ref[...])
        dm_ref[...] = share if which == 0 else dm_ref[...] + share

    @pl.when(pl.program_id(0) == 0)
    def _():
        memory_t[...] = memory_ref[...].T
        add(0, wk_ref)

    @pl.when(pl.program_id(0) == 1)
    def _():
        add(1, wv_ref)

    found[...] = mm(memory_t[...], grad[...])
    for flip, out_ref in enumerate((keep_ref, send_ref)):
        start = pl.multiple_of((info[1] ^ flip) * columns, LANES)
        put_tiles(out_ref, info, flip, 0, found[:, pl.ds(start, columns)], shards)


def keys_values_kernel(
    shards, info, h_ref, dk_ref, dv_ref, ret_ref, keep_in, send_in,
    keep_ref, send_ref, dkl_ref, dvl_ref, found,
):
    head = h_ref.shape[0] - REACH
    rows = (keep_ref.shape[1] - keep_in.shape[1]) // 2
    keep_ref[:, 2 * rows :, :] = keep_in[...]
    send_ref[:, 2 * rows :, :] = send_in[...]
    columns = found.shape[1] // 2
    left = h_ref[...].T
    for which, own, low in ((0, dk_ref, dkl_ref), (1, dv_ref, dvl_ref)):
        low[:head, :] = own[:head, :].astype(bf16)
        low[head:, :] = (own[head:, :] + ret_ref[which].astype(f32)).astype(bf16)
        found[...] = mm(left, low[...])
        for flip, out_ref in enumerate((keep_ref, send_ref)):
            start = pl.multiple_of((info[1] ^ flip) * columns, LANES)
            half = found[:, pl.ds(start, columns)]
            put_tiles(out_ref, info, flip, which * rows, half, shards)


def query_gradient_kernel(
    shards, info, h_ref, own_ref, other_ref, *refs
):
    *tables, keep_ref, send_ref = refs
    left = h_ref[...].T
    rows = keep_ref.shape[1] - 16
    put_tiles(keep_ref, info, 0, 0, mm(left, own_ref[...]), shards)
    put_tiles(send_ref, info, 1, 0, mm(left, other_ref[...]), shards)
    count = BUCKETS // shards
    table = jnp.concatenate(
        [sum(ref[...] for ref in tables), jnp.zeros((BUCKETS, LANES - HEADS), f32)], axis=1
    )
    for index in range(shards):
        piece = table[index * count : (index + 1) * count]
        tile = jnp.concatenate([piece, jnp.zeros((16 - count, LANES), f32)], axis=0).astype(bf16)
        for which, out_ref in enumerate((keep_ref, send_ref)):
            out_ref[info[HEADER + which * shards + index], rows:] = tile


def sum_kernel(*refs):
    total = refs[0][...].astype(f32)
    for ref in refs[1:-1]:
        total = total + ref[...].astype(f32)
    refs[-1][...] = total.astype(bf16)


def halves(info, own_ref, other_ref):
    own, other = own_ref[...].astype(f32), other_ref[...].astype(f32)
    first = info[1] == 0
    return jnp.where(first, own, other), jnp.where(first, other, own)


def fill_square(out_ref, sides, offset):
    rows, columns = out_ref.shape
    count = columns // LANES // 2
    for side, found in enumerate(sides):
        for tile in range(count):
            start = (side * count + tile) * LANES
            out_ref[:, start : start + LANES] = found[
                offset + tile * rows : offset + (tile + 1) * rows
            ]


def put_gain(info, pairs, gain_ref, out_ref):
    rows, width = pairs[0][0].shape[0], gain_ref.shape[0]
    total = None
    for weight_ref, grad_ref in pairs:
        share = jnp.sum(weight_ref[...].astype(f32) * grad_ref[...], axis=1, keepdims=True)
        total = share if total is None else total + share
    here = iota((rows, width), 1) == info[0] * rows + iota((rows, width), 0)
    gain = jnp.sum(jnp.where(here, gain_of(gain_ref), 0.0), axis=1, keepdims=True)
    spread = jnp.where(iota((rows, LANES), 0) == iota((rows, LANES), 1), total / gain, 0.0)
    out_ref[...] = jnp.sum(spread, axis=0)[:rows]


def gate_unpack_kernel(
    info, own_ref, other_ref, wg_ref, wu_ref, gain_ref, gate_ref, up_ref, gg_ref
):
    rows, columns = gate_ref.shape
    count = columns // LANES // 2
    for side, found in enumerate(halves(info, own_ref, other_ref)):
        for tile in range(count):
            start = (side * count + tile) * LANES
            at = (tile // 2) * 4 * rows + (tile % 2) * rows
            gate_ref[:, start : start + LANES] = found[at : at + rows]
            up_ref[:, start : start + LANES] = found[at + 2 * rows : at + 3 * rows]
    put_gain(info, ((wg_ref, gate_ref), (wu_ref, up_ref)), gain_ref, gg_ref)


def down_unpack_kernel(info, own_ref, other_ref, down_ref):
    half = down_ref.shape[0] // 2
    for side, found in enumerate(halves(info, own_ref, other_ref)):
        for tile in range(down_ref.shape[1] // LANES):
            down_ref[side * half : (side + 1) * half, tile * LANES : (tile + 1) * LANES] = found[
                tile * half : (tile + 1) * half
            ]


def square_unpack_kernel(gained, info, own_ref, other_ref, *refs):
    weights, gain_ref = refs[: len(gained)], refs[len(gained)]
    out_refs, gg_ref = refs[len(gained) + 1 : -1], refs[-1]
    sides = halves(info, own_ref, other_ref)
    offset = 0
    for out_ref in out_refs:
        fill_square(out_ref, sides, offset)
        offset += out_ref.shape[0] * (out_ref.shape[1] // LANES // 2)
    put_gain(info, [(w, out_refs[at]) for w, at in zip(weights, gained)], gain_ref, gg_ref)


def last_unpack_kernel(info, own_ref, other_ref, *refs):
    table_ref = refs[7]
    square_unpack_kernel((0, 1, 2), info, own_ref, other_ref, *refs[:7], refs[8])
    rows, heads = table_ref.shape
    table_ref[...] = own_ref[own_ref.shape[0] - 16 :, :].astype(f32)[:rows, :heads]


def whole(shape):
    return pl.BlockSpec(shape, lambda *_: (0,) * len(shape))


def call(kernel, name, grid, ins, outs, args, scalars=(), scratch=(), alias=None):
    shapes = [
        pltpu.HBM(out[0], out[1]) if len(out) > 3 else jax.ShapeDtypeStruct(out[0], out[1])
        for out in outs
    ]
    return pl.pallas_call(
        kernel,
        out_shape=shapes,
        grid_spec=pltpu.PrefetchScalarGridSpec(
            num_scalar_prefetch=len(scalars),
            grid=grid,
            in_specs=list(ins),
            out_specs=[out[2] for out in outs],
            scratch_shapes=list(scratch),
        ),
        input_output_aliases=alias or {},
        compiler_params=pltpu.CompilerParams(
            dimension_semantics=("arbitrary",) * len(grid), vmem_limit_bytes=GRANTS[name] * 2**20
        ),
        cost_estimate=pl.CostEstimate(flops=int(TIMES[name] * COVER), bytes_accessed=1, transcendentals=0),
        name=name,
    )(*scalars, *args)


def full(*arrays):
    return [whole(a.shape) for a in arrays]


def bit_orders(bits, last_first):
    low, high = list(range(min(bits, 2))), list(range(2, bits))
    first, second = (low + high[::-1], low[::-1] + high)
    if last_first:
        first, second = (high[::-1] + low, high + low[::-1])
    return [first, second]


def info_table(wide_size, narrow_size, order_pairs):
    bits = wide_size.bit_length() - 1
    rows = []
    for w in range(wide_size):
        for n in range(narrow_size):
            side = n % 2
            row = [w, side, side, w * (narrow_size // 2) + n // 2, n]
            row += [0] * (HEADER - len(row))
            for pair in order_pairs:
                for order in (pair[side], pair[1 - side]):
                    for shard in range(wide_size):
                        apart = shard ^ w
                        slot = [((apart >> bit) & 1) << (bits - 1 - k) for k, bit in enumerate(order)]
                        row.append(sum(slot))
            rows.append(row)
    return np.array(rows, np.int32)


def shards(
    inputs, memory, cotangent, answer_lengths, answer_groups, memory_lengths,
    gain_attn, self_query, self_key, self_value, self_out, bucket_bias_table,
    gain_cross, cross_query, cross_key_matrix, cross_value, cross_out,
    gain_ffn, hidden_gate, hidden_up, hidden_down,
):
    tokens, width = inputs.shape
    answer_lengths, answer_groups = answer_lengths.T, answer_groups.T
    part = memory.shape[0]
    hidden = hidden_gate.shape[1]
    wide_size = lax.axis_size("wide")
    narrow_size = lax.axis_size("narrow")
    wide_index = lax.axis_index("wide")
    narrow_index = lax.axis_index("narrow")
    bits = wide_size.bit_length() - 1
    orders = bit_orders(bits, False)
    orders_last_first = bit_orders(bits, True)
    info = jnp.asarray(info_table(wide_size, narrow_size, (orders, orders_last_first)))
    info = lax.dynamic_slice(
        info, (wide_index * narrow_size + narrow_index, 0), (1, info.shape[1])
    )
    info = info.reshape(-1)
    gains = (gain_attn, gain_cross, gain_ffn)
    turn = [info]

    both = ("wide", "narrow")

    def to_narrow(value, target):
        pairs = [(n, target(n)) for n in range(narrow_size) if target(n) is not None]
        return lax.ppermute(value, "narrow", pairs)

    def to_wide(value, place, order_pair):
        pairs = []
        for w in range(wide_size):
            for n in range(narrow_size):
                partner = w ^ (1 << order_pair[n % 2][place])
                pairs.append((w * narrow_size + n, partner * narrow_size + n))
        return lax.ppermute(value, both, pairs)

    def after(values, *needed):
        return lax.optimization_barrier((tuple(values), needed))[0]

    def now(*values):
        return after(values, *turn) if turn else values

    def run(kernel, name, grid, ins, outs, args, **more):
        found = call(kernel, name, grid, ins, outs, (*now(args[0]), *args[1:]), **more)
        turn[:] = found[:1]
        return found

    class Group:
        def __init__(self, keep, send, order_pair=orders):
            self.pieces, self.place, self.count = [keep], 0, wide_size
            self.order_pair = order_pair
            self.pending = to_narrow(send, lambda n: n ^ 1)

        def total(self, first, count, name="partial_sum"):
            pieces = (*self.pieces, self.pending)
            rows, lanes = pieces[0].shape[1:]
            parts = 2 if count * rows >= 4096 and rows % 32 == 0 else 1
            spec = lambda at: pl.BlockSpec(
                (count, rows // parts, lanes), lambda j: (at, j, 0)
            )
            shape = (count, rows, lanes)
            (found,) = run(
                sum_kernel, name, (parts,), [spec(first)] * len(pieces),
                [(shape, bf16, spec(0))], pieces,
            )
            self.pieces = list(pieces)
            return found

        def step(self, name="partial_sum"):
            self.count //= 2
            sent = self.total(1, self.count, name)
            self.pending = to_wide(sent, self.place, self.order_pair)
            self.place += 1

        def finish(self, name="partial_sum"):
            while self.place < bits:
                self.step()
            total = self.total(0, 1, name)
            step = 2
            while step < narrow_size:
                self.pieces, self.pending = [total], to_narrow(total, lambda n, s=step: n ^ s)
                total = self.total(0, 1)
                step *= 2
            return total[0], to_narrow(total, lambda n: n ^ 1)[0]

    block = lambda rows: pl.BlockSpec((rows, PAIR), lambda j, *_: (0, j))
    out_rows = pl.BlockSpec((PAIR, width), lambda j, *_: (j, 0))

    model = (tokens, width)
    square = (width, width)
    in_hbm = pl.BlockSpec(memory_space=pltpu.HBM)
    normed, keys, values, tail, memory_own = run(
        project_kernel, "projections", (1,),
        [whole((width,))] + [in_hbm] * 6,
        [(model, bf16, whole(model))] * 3
        + [((2, REACH, width), bf16, whole((2, REACH, width)))]
        + [((2, part, width), bf16, whole((2, part, width)))],
        (gains[0],)
        + tuple(
            pltpu.with_memory_space_constraint(a, pltpu.HBM)
            for a in (inputs, memory, self_key, self_value, cross_key_matrix, cross_value)
        ),
        scratch=(pltpu.VMEM(model, bf16), pltpu.VMEM((part, width), bf16))
        + (pltpu.VMEM(square, bf16),) * 4
        + (pltpu.SemaphoreType.DMA((6,)),),
    )
    halo = to_narrow(tail, lambda n: n + 1 if n % 2 == 0 else None)
    memory_parts = [memory_own] + [
        to_narrow(memory_own, lambda n, s=shift: (n + s) % narrow_size)
        for shift in range(1, narrow_size)
    ]

    queries, bias = run(
        query_kernel, "queries", (1,),
        [whole(model), in_hbm, whole((HEADS, BUCKETS))],
        [
            (model, bf16, whole(model)),
            ((HEADS * QUERY_BLOCK, WINDOW), f32, whole((HEADS * QUERY_BLOCK, WINDOW))),
        ],
        (normed, pltpu.with_memory_space_constraint(self_query, pltpu.HBM), bucket_bias_table.T),
        scratch=(pltpu.VMEM(square, bf16), pltpu.SemaphoreType.DMA),
    )

    halo_block = pl.BlockSpec((2, REACH, PAIR), lambda j, *_: (0, 0, j))
    blocks = tokens // QUERY_BLOCK
    self_probs = pl.BlockSpec(
        (1, blocks, 2 * QUERY_BLOCK, WINDOW), lambda j, *_: (j, 0, 0, 0)
    )
    attended, inverse, probs, x1, normed_two, cross_rows = run(
        self_forward_kernel, "self_forward", (PAIRS,),
        [block(tokens)] * 3 + [halo_block]
        + [pl.BlockSpec((2 * QUERY_BLOCK, WINDOW), lambda j, *_: (j, 0)), whole(model), out_rows]
        + full(gains[1], cross_query),
        [
            (model, bf16, block(tokens)),
            (model, f32, block(tokens), "hbm"),
            ((PAIRS, blocks, 2 * QUERY_BLOCK, WINDOW), bf16, self_probs, "hbm"),
            (model, f32, whole(model)),
            (model, bf16, whole(model)),
            (model, bf16, whole(model)),
        ],
        (queries, keys, values, halo, bias, inputs, self_out, gains[1], cross_query),
        scalars=(info, answer_lengths),
        scratch=(
            pltpu.VMEM((tokens + REACH, PAIR), bf16),
            pltpu.VMEM((tokens + REACH, 2 * PAIR), bf16),
            pltpu.VMEM((tokens, LANES), jnp.int32),
        ),
    )

    memory_tokens = part * narrow_size
    memory_block = pl.BlockSpec((2, part, PAIR), lambda j, *_: (0, 0, j))
    cross_blocks = tokens // CROSS_BLOCK
    cross_probs = pl.BlockSpec(
        (1, cross_blocks, 2 * CROSS_BLOCK, memory_tokens), lambda j, *_: (j, 0, 0, 0)
    )
    attended_two, inverse_two, probs_two, x2, normed_three = run(
        functools.partial(cross_forward_kernel, narrow_size), "cross_forward", (PAIRS,),
        [block(tokens), whole(model), out_rows, whole((width,))] + [memory_block] * narrow_size,
        [
            (model, bf16, block(tokens)),
            (model, f32, block(tokens), "hbm"),
            ((PAIRS, cross_blocks, 2 * CROSS_BLOCK, memory_tokens), bf16, cross_probs, "hbm"),
            (model, f32, whole(model)),
            (model, bf16, whole(model)),
        ],
        (cross_rows, x1, cross_out, gains[2], *memory_parts),
        scalars=(info, answer_lengths, answer_groups, memory_lengths),
        scratch=(
            pltpu.VMEM((memory_tokens, PAIR), bf16),
            pltpu.VMEM((memory_tokens, 2 * PAIR), bf16),
            pltpu.VMEM((tokens, LANES), jnp.int32),
            pltpu.VMEM((8, memory_tokens), jnp.int32),
        ),
    )

    inverse, probs, inverse_two, probs_two = (
        pltpu.with_memory_space_constraint(a, pltpu.HBM)
        for a in (inverse, probs, inverse_two, probs_two)
    )

    tile = 512
    wide_tile = pl.BlockSpec((width, tile), lambda j, *_: (0, j))
    token_tile = pl.BlockSpec((tokens, tile), lambda j, *_: (0, j))
    hidden_shape = (tokens, hidden)
    unit, grad_gate, grad_up, layer_out, dx2, e2 = run(
        ffn_kernel, "feed_forward", (hidden // tile,),
        [whole(model)] * 3
        + [whole((width,)), wide_tile, wide_tile]
        + [pl.BlockSpec((tile, width), lambda j, *_: (j, 0))],
        [(hidden_shape, bf16, token_tile)] * 3
        + [
            (model, bf16, whole(model)),
            (model, f32, whole(model)),
            (model, bf16, whole(model)),
        ],
        (normed_three, cotangent, x2, gains[2], hidden_gate, hidden_up, hidden_down),
        scratch=(pltpu.VMEM(model, f32), pltpu.VMEM(model, f32)),
    )

    square_rows = width // wide_size * (width // 2 // LANES)
    gate_rows = width // wide_size * (hidden // 2 // LANES)
    down_rows = hidden // wide_size // 2 * (width // LANES)
    step_rows = gate_rows // 2
    gate_side = lambda flip: pl.BlockSpec(
        (tokens, 256), lambda j, info: (0, (info[1] ^ flip) * (hidden // 512) + j)
    )
    half_side = lambda flip: pl.BlockSpec(
        (tokens, width // 2), lambda j, info: (0, info[1] ^ flip)
    )
    anywhere = pl.BlockSpec(memory_space=pl.ANY)

    gate_shape = (wide_size, 2 * gate_rows, LANES)
    step_spec = pl.BlockSpec((wide_size, step_rows, LANES), lambda j, *_: (0, j, 0))
    keep, send = run(
        functools.partial(gate_up_kernel, wide_size), "gate_up_gradient", (hidden // 512,),
        [whole(model), gate_side(0), gate_side(1), gate_side(0), gate_side(1)],
        [(gate_shape, bf16, step_spec)] * 2,
        (normed_three, grad_gate, grad_gate, grad_up, grad_up),
        scalars=(info,),
        scratch=(pltpu.VMEM((width, tokens), bf16),),
    )
    gate_group = Group(keep, send)
    down_shape = (wide_size, down_rows, LANES)
    down_spec = pl.BlockSpec((wide_size, down_rows // 2, LANES), lambda j, *_: (0, j, 0))
    keep, send = run(
        functools.partial(down_kernel, wide_size), "down_gradient", (2,),
        [whole(hidden_shape), pl.BlockSpec((tokens, width // 2), lambda j, *_: (0, j))],
        [(down_shape, bf16, down_spec)] * 2,
        (unit, cotangent),
        scalars=(info,),
        scratch=(
            pltpu.VMEM((hidden, tokens), bf16),
            pltpu.VMEM((hidden, width // 2), f32),
        ),
    )
    down_group = Group(keep, send, orders_last_first)
    gate_group.step()

    grad_cross_rows, dx1, e1, *memory_grads = run(
        functools.partial(cross_backward_kernel, narrow_size), "cross_backward", (PAIRS,),
        [whole(model), out_rows, block(tokens), block(tokens), cross_probs, block(tokens)]
        + [block(width), whole(model), whole(model), whole((width,))]
        + [memory_block] * narrow_size,
        [
            (model, bf16, block(tokens)),
            (model, f32, whole(model)),
            (model, bf16, whole(model)),
        ]
        + [((2, part, width), bf16, memory_block)] * narrow_size,
        (e2, cross_out, attended_two, inverse_two, probs_two, cross_rows, cross_query, x1, dx2)
        + (gains[1], *memory_parts),
        scratch=(
            pltpu.VMEM((memory_tokens, PAIR), bf16),
            pltpu.VMEM((memory_tokens, PAIR), bf16),
            pltpu.VMEM((PAIR, memory_tokens), f32),
            pltpu.VMEM((PAIR, memory_tokens), f32),
            pltpu.VMEM(model, f32),
        ),
    )
    memory_shares = [memory_grads[0]] + [
        to_narrow(memory_grads[shift], lambda n, s=shift: (n - s) % narrow_size)
        for shift in range(1, narrow_size)
    ]
    down_group.step()
    second_shape = (wide_size, 5 * square_rows, LANES)
    triple = ((attended_two, e2), (normed_two, grad_cross_rows), (attended, e1))
    second_spec = pl.BlockSpec((wide_size, 3 * square_rows, LANES), lambda j, *_: (0, 0, 0))
    keep, send = run(
        functools.partial(square_kernel, wide_size, 3), "square_gradients", (1,),
        [whole(model), half_side(0), half_side(1)] * 3,
        [(second_shape, bf16, second_spec)] * 2,
        [side_of for left, right in triple for side_of in (left, right, right)],
        scalars=(info,),
    )
    gate_group.step()
    memory_spec = pl.BlockSpec((wide_size, square_rows, LANES), lambda j, *_: (0, 3 + j, 0))
    keep, send, memory_grad = run(
        functools.partial(memory_back_kernel, narrow_size, wide_size), "memory_backward", (2,),
        full(memory, cross_key_matrix, cross_value, *memory_shares) + [anywhere] * 2,
        [(second_shape, bf16, memory_spec)] * 2
        + [((part, width), f32, whole((part, width)))],
        (memory, cross_key_matrix, cross_value, *memory_shares, keep, send),
        scalars=(info,),
        scratch=(
            pltpu.VMEM((width, width), f32),
            pltpu.VMEM((part, width), bf16),
            pltpu.VMEM((width, part), bf16),
        ),
        alias={4 + narrow_size: 0, 5 + narrow_size: 1},
    )
    second_group = Group(keep, send)

    tables, carried, parts_of = [], [], 3
    for index in range(parts_of):
        count = PAIRS // parts_of
        begin = index * count
        at = lambda rows, b=begin: pl.BlockSpec((rows, PAIR), lambda j, *_: (0, b + j))
        here = lambda *lead, b=begin: pl.BlockSpec(
            (1, *lead), lambda j, *_: (b + j,) + (0,) * len(lead)
        )
        halo_at = pl.BlockSpec((2, REACH, PAIR), lambda j, *_, b=begin: (0, 0, b + j))
        out_at = pl.BlockSpec((PAIR, width), lambda j, *_, b=begin: (b + j, 0))
        if index == 1:
            second_group.step()
            gate_group.step()
        if index == 2:
            down_group.step()
        *carried, table = run(
            functools.partial(self_backward_kernel, begin),
            "self_backward" if index else "self_backward_first", (count,),
            [whole(model), out_at, at(tokens), at(tokens)]
            + [here(blocks, 2 * QUERY_BLOCK, WINDOW)]
            + [at(tokens)] * 3 + [halo_at] + [anywhere] * len(carried),
            [
                (model, bf16, at(tokens)),
                (model, f32, at(tokens)),
                (model, f32, at(tokens)),
                ((2, REACH, width), bf16, halo_at),
                ((BUCKETS, HEADS), f32, whole((BUCKETS, HEADS))),
            ],
            (e1, self_out, attended, inverse, probs, queries, keys, values, halo, *carried),
            scratch=(
                pltpu.VMEM((tokens + REACH, PAIR), bf16),
                pltpu.VMEM((tokens + REACH, PAIR), bf16),
                pltpu.VMEM((PAIR, tokens + REACH), f32),
                pltpu.VMEM((PAIR, tokens + REACH), f32),
                pltpu.VMEM((2 * QUERY_BLOCK, 4 * QUERY_BLOCK), f32),
                pltpu.VMEM((16, 4 * QUERY_BLOCK), f32),
            ),
            alias={9 + i: i for i in range(4)} if index else None,
        )
        tables.append(table)
    grad_queries, grad_keys, grad_values, back = carried
    returned = to_narrow(back, lambda n: n - 1 if n % 2 == 1 else None)
    second_group.step()
    query_shape = (wide_size, square_rows + 16, LANES)
    last_shape = (wide_size, 3 * square_rows + 16, LANES)
    query_keep, query_send = run(
        functools.partial(query_gradient_kernel, wide_size), "query_gradient", (1,),
        [whole(model), half_side(0), half_side(1)] + [whole((BUCKETS, HEADS))] * parts_of,
        [(query_shape, bf16, whole(query_shape))] * 2,
        (normed, grad_queries, grad_queries, *tables),
        scalars=(info,),
    )
    keep, send, keys_low, values_low = run(
        functools.partial(keys_values_kernel, wide_size), "key_value_gradient", (1,),
        full(normed, grad_keys, grad_values, returned, query_keep, query_send),
        [(last_shape, bf16, whole(last_shape))] * 2 + [(model, bf16, whole(model))] * 2,
        (normed, grad_keys, grad_values, returned, query_keep, query_send),
        scalars=(info,),
        scratch=(pltpu.VMEM(square, f32),),
    )
    last_group = Group(keep, send)
    gate_group.step()
    down_group.step("partial_sum_beside")
    last_group.step()
    (input_grad,) = run(
        input_kernel, "input_gradient", (1,),
        full(grad_queries, keys_low, values_low)
        + full(self_query, self_key, self_value, inputs, dx1, gains[0]),
        [(model, f32, whole(model))],
        (grad_queries, keys_low, values_low)
        + (self_query, self_key, self_value, inputs, dx1, gains[0]),
    )

    square_out = ((width // wide_size, width), f32, whole((width // wide_size, width)))
    gate_out = ((width // wide_size, hidden), f32, whole((width // wide_size, hidden)))
    down_out = ((hidden // wide_size, width), f32, whole((hidden // wide_size, width)))
    size = width // wide_size
    gain_out = ((size,), f32, whole((size,)))
    own_rows = lambda columns: pl.BlockSpec((size, columns), lambda j, info: (info[0], 0))
    second_group.step()
    gate_own, gate_other = gate_group.finish()
    last_group.step()
    grad_gate_w, grad_up_w, grad_gain_ffn = run(
        gate_unpack_kernel, "gate_outputs", (1,),
        full(gate_own, gate_other) + [own_rows(hidden)] * 2 + [whole((width,))],
        [gate_out] * 2 + [gain_out],
        (gate_own, gate_other, hidden_gate, hidden_up, gain_ffn), scalars=(info,),
    )
    down_group.step("partial_sum_late")
    last_group.step("partial_sum_late")
    second_group.step("partial_sum_late")
    down_own, down_other = down_group.finish("partial_sum_late")
    (grad_down_w,) = run(
        down_unpack_kernel, "down_outputs", (1,), full(down_own, down_other),
        [down_out], (down_own, down_other), scalars=(info,),
    )
    last_group.step("partial_sum_late")
    second_own, second_other = second_group.finish("partial_sum_late")
    (
        grad_cross_out, grad_cross_query, grad_self_out, grad_cross_key, grad_cross_value,
        grad_gain_cross,
    ) = run(
        functools.partial(square_unpack_kernel, (1,)), "second_outputs", (1,),
        full(second_own, second_other) + [own_rows(width), whole((width,))],
        [square_out] * 5 + [gain_out],
        (second_own, second_other, cross_query, gain_cross), scalars=(info,),
    )
    last_own, last_other = last_group.finish()
    table_out = ((BUCKETS // wide_size, HEADS), f32, whole((BUCKETS // wide_size, HEADS)))
    grad_self_key, grad_self_value, grad_self_query, grad_table, grad_gain_attn = run(
        last_unpack_kernel, "last_outputs", (1,),
        full(last_own, last_other) + [own_rows(width)] * 3 + [whole((width,))],
        [square_out] * 3 + [table_out, gain_out],
        (last_own, last_other, self_key, self_value, self_query, gain_attn), scalars=(info,),
    )
    return (
        layer_out,
        input_grad,
        memory_grad,
        grad_gain_attn,
        grad_self_query,
        grad_self_key,
        grad_self_value,
        grad_self_out,
        grad_table,
        grad_gain_cross,
        grad_cross_query,
        grad_cross_key,
        grad_cross_value,
        grad_cross_out,
        grad_gain_ffn,
        grad_gate_w,
        grad_up_w,
        grad_down_w,
    )


def solution(mesh):
    rows = P(("wide", "narrow"), None)
    vector, matrix = P("wide"), P("wide", None)
    return jax.shard_map(
        shards,
        mesh=mesh,
        in_specs=(rows,) * 3 + (P(),) * 18,
        out_specs=(rows,) * 3
        + (vector,)
        + (matrix,) * 5
        + (vector,)
        + (matrix,) * 4
        + (vector,)
        + (matrix,) * 3,
        check_vma=False,
    )
```

```python
import functools
import math

import jax
import jax.numpy as jnp
import numpy as np
from jax import lax
from jax.experimental import pallas as pl
from jax.experimental.pallas import tpu as pltpu
from jax.sharding import PartitionSpec as P

HEADS = 12
HEAD_DIM = 64
BUCKETS = 32
MAX_DIST = 128
ANSWERS = 8
GROUPS = 16
PAIR = 2 * HEAD_DIM
PAIRS = HEADS // 2
REACH = 256
QUERY_BLOCK = 128
WINDOW = REACH + QUERY_BLOCK
CROSS_BLOCK = 256
LANES = 128
HEADER = 8
TOGETHER = 2
PLANS = dict(
    projections=(14, 5.0),
    queries=(8, 3.0),
    self_forward=(20, 12.0),
    cross_forward=(16, 10.5),
    feed_forward=(24, 15.0),
    gate_up_gradient=(14, 6.0),
    down_gradient=(16, 4.4),
    cross_backward=(20, 12.0),
    square_gradients=(16, 2.0),
    memory_backward=(14, 3.6),
    self_backward_first=(14, 30.0),
    self_backward=(14, 7.0),
    query_gradient=(8, 9.0),
    key_value_gradient=(14, 2.4),
    input_gradient=(16, 1.0),
    partial_sum=(12, 1.0),
    partial_sum_late=(12, 0.0),
    partial_sum_beside=(12, 20.0),
    gate_outputs=(6, 0.0),
    down_outputs=(6, 0.0),
    second_outputs=(6, 0.0),
    last_outputs=(6, 0.0),
)
COVER = 1.15e9

epsilon = 1e-06
neg_big = -1e30
f32 = jnp.float32
bf16 = jnp.bfloat16


def mm(left, right):
    return jnp.dot(left, right, preferred_element_type=f32)


def mm_t(left, right):
    return lax.dot_general(left, right, (((1,), (1,)), ((), ())), preferred_element_type=f32)


def rms(values, gain_row):
    factor = lax.rsqrt(jnp.mean(values * values, axis=-1, keepdims=True) + epsilon)
    return values * factor * gain_row


def rms_back(values, gain_row, grad):
    factor = lax.rsqrt(jnp.mean(values * values, axis=-1, keepdims=True) + epsilon)
    unit = values * factor
    scaled = grad * gain_row
    center = jnp.mean(scaled * unit, axis=-1, keepdims=True)
    return factor * (scaled - unit * center)


def bucket_of(distance):
    exact_count = BUCKETS // 2
    log_count = BUCKETS - exact_count
    near_part = jnp.minimum(jnp.maximum(distance, 0), exact_count)
    far_part = jnp.zeros_like(distance)
    for level_index in range(1, log_count):
        edge = math.ceil(exact_count * (MAX_DIST / exact_count) ** (level_index / log_count))
        far_part = far_part + (distance >= edge).astype(jnp.int32)
    return near_part + far_part


def gain_of(ref):
    return ref[...].astype(f32).reshape(1, ref.shape[0])


def iota(shape, axis):
    return lax.broadcasted_iota(jnp.int32, shape, axis)


def low_lanes(shape):
    return iota(shape, len(shape) - 1) < HEAD_DIM


def stack_heads(rows):
    low = low_lanes(rows.shape)
    zero = jnp.zeros_like(rows)
    return jnp.concatenate([jnp.where(low, rows, zero), jnp.where(low, zero, rows)], axis=0)


def stack_heads_t(columns):
    low = iota(columns.shape, 0) < HEAD_DIM
    zero = jnp.zeros_like(columns)
    return jnp.concatenate([jnp.where(low, columns, zero), jnp.where(low, zero, columns)], axis=1)


def join_heads(stacked):
    half = stacked.shape[0] // 2
    return jnp.where(low_lanes((half, PAIR)), stacked[:half], stacked[half:])


def offset_bucket():
    lane = iota((1, 4 * QUERY_BLOCK), 1)
    distance = jnp.where(lane < WINDOW, REACH - lane, REACH + 4 * QUERY_BLOCK - lane)
    chosen = iota((BUCKETS, 4 * QUERY_BLOCK), 0) == bucket_of(distance)
    return distance, chosen


def answer_ends(lengths, row):
    total, ends = lengths[0, row], []
    for index in range(1, ANSWERS):
        ends.append(total)
        total = total + lengths[index, row]
    return ends


def project_kernel(
    gain_ref, x_hbm, memory_hbm, wk_hbm, wv_hbm, wck_hbm, wcv_hbm,
    h_ref, k_ref, v_ref, tail_ref, memory_out,
    x_ref, memory_ref, wk_ref, wv_ref, wck_ref, wcv_ref, sems,
):
    copies = [
        pltpu.make_async_copy(source, target, sems.at[index])
        for index, (source, target) in enumerate(
            (
                (x_hbm, x_ref),
                (memory_hbm, memory_ref),
                (wck_hbm, wck_ref),
                (wcv_hbm, wcv_ref),
                (wk_hbm, wk_ref),
                (wv_hbm, wv_ref),
            )
        )
    ]
    for copy in copies:
        copy.start()
    copies[0].wait()
    h_ref[...] = rms(x_ref[...].astype(f32), gain_of(gain_ref)).astype(bf16)
    copies[1].wait()
    copies[2].wait()
    memory_out[0] = mm(memory_ref[...], wck_ref[...]).astype(bf16)
    copies[3].wait()
    memory_out[1] = mm(memory_ref[...], wcv_ref[...]).astype(bf16)
    tokens = h_ref.shape[0]
    copies[4].wait()
    k_ref[...] = mm(h_ref[...], wk_ref[...]).astype(bf16)
    tail_ref[0] = k_ref[tokens - REACH :, :]
    copies[5].wait()
    v_ref[...] = mm(h_ref[...], wv_ref[...]).astype(bf16)
    tail_ref[1] = v_ref[tokens - REACH :, :]


def query_kernel(h_ref, wq_hbm, table_ref, q_ref, bias_ref, wq_ref, sem):
    copy = pltpu.make_async_copy(wq_hbm, wq_ref, sem)
    copy.start()
    distance, chosen = offset_bucket()
    base = jnp.where(distance < 0, neg_big, mm(table_ref[...], chosen.astype(bf16)))
    for head in range(HEADS):
        spread = jnp.broadcast_to(base[head : head + 1], (QUERY_BLOCK, 4 * QUERY_BLOCK))
        skewed = pltpu.roll(spread, 0, 1, stride=1, stride_axis=0)
        bias_ref[head * QUERY_BLOCK : (head + 1) * QUERY_BLOCK, :] = skewed[:, :WINDOW]
    copy.wait()
    q_ref[...] = mm(h_ref[...], wq_ref[...]).astype(bf16)


def self_forward_kernel(
    info, lengths,
    q_ref, k_ref, v_ref, halo_ref, bias, x_ref, wo_ref, gain_ref, wq_ref,
    o_ref, inv_ref, e_ref, x1_ref, h2_ref, qc_ref,
    keys, values, reach,
):
    step = pl.program_id(0)
    tokens = q_ref.shape[0]

    @pl.when(step == 0)
    def _():
        place = info[2] * tokens + iota((tokens, LANES), 0)
        start = jnp.zeros_like(place)
        for end in answer_ends(lengths, info[3]):
            start = jnp.where(place >= end, end, start)
        reach[...] = place - start
        for p in range(TOGETHER):
            ones = slice((2 * p + 1) * PAIR, 2 * (p + 1) * PAIR)
            values[:, ones] = jnp.ones((values.shape[0], PAIR), bf16)
        x1_ref[...] = x_ref[...].astype(f32)

    keys[0:REACH] = halo_ref[0]
    keys[REACH:] = k_ref[...]
    pairs = [slice(p * PAIR, (p + 1) * PAIR) for p in range(TOGETHER)]
    valued = [slice(2 * p * PAIR, 2 * (p + 1) * PAIR) for p in range(TOGETHER)]
    for pair, both in zip(pairs, valued):
        own = slice(both.start, both.start + PAIR)
        values[0:REACH, own] = halo_ref[1, :, pair]
        values[REACH:, own] = v_ref[:, pair]

    distance = REACH + iota((QUERY_BLOCK, WINDOW), 0) - iota((QUERY_BLOCK, WINDOW), 1)
    distance = jnp.concatenate([distance, distance], axis=0)
    items = [(b, p) for p in range(TOGETHER) for b in range(tokens // QUERY_BLOCK)]
    rows = [slice(b * QUERY_BLOCK, (b + 1) * QUERY_BLOCK) for b, _ in items]
    windows = [slice(b * QUERY_BLOCK, b * QUERY_BLOCK + WINDOW) for b, _ in items]
    scores = [
        mm_t(stack_heads(q_ref[r, pairs[p]]), keys[w, pairs[p]])
        for (_, p), r, w in zip(items, rows, windows)
    ]
    weights = []
    for (block, p), r, found in zip(items, rows, scores):
        own_reach = reach[r, 0:1]
        own_reach = jnp.concatenate([own_reach, own_reach], axis=0)
        shifted = found + bias[2 * p * QUERY_BLOCK : 2 * (p + 1) * QUERY_BLOCK, :]
        masked = jnp.where(distance <= own_reach, shifted, neg_big)
        top = jnp.max(masked, axis=-1, keepdims=True)
        weights.append(jnp.exp(masked - top).astype(bf16))
        e_ref[p, block] = weights[-1]
    mixed = [mm(e, values[w, valued[p]]) for (_, p), e, w in zip(items, weights, windows)]
    for (_, p), r, found in zip(items, rows, mixed):
        inverse = 1.0 / found[:, PAIR:]
        o_ref[r, pairs[p]] = join_heads(found[:, :PAIR] * inverse).astype(bf16)
        inv_ref[r, pairs[p]] = join_heads(inverse)
    x1_ref[...] += mm(o_ref[...], wo_ref[...])

    @pl.when(step == pl.num_programs(0) - 1)
    def _():
        h2_ref[...] = rms(x1_ref[...], gain_of(gain_ref)).astype(bf16)
        qc_ref[...] = mm(h2_ref[...], wq_ref[...]).astype(bf16)


def cross_forward_kernel(chunks, info, lengths, groups, bounds, *refs):
    q_ref, x1_ref, wo_ref, gain_ref = refs[:4]
    kv_refs = refs[4 : 4 + chunks]
    o_ref, inv_ref, e_ref, x2_ref, h3_ref = refs[4 + chunks : 9 + chunks]
    keys, values, query_group, key_group = refs[9 + chunks :]
    step = pl.program_id(0)
    tokens = q_ref.shape[0]
    part = kv_refs[0].shape[1]

    @pl.when(step == 0)
    def _():
        place = info[2] * tokens + iota((tokens, LANES), 0)
        group = jnp.zeros_like(place) + groups[0, info[3]]
        for index, end in enumerate(answer_ends(lengths, info[3])):
            group = jnp.where(place >= end, groups[index + 1, info[3]], group)
        query_group[...] = group
        total, ends = bounds[info[0], 0], []
        for index in range(1, GROUPS):
            ends.append(total)
            total = total + bounds[info[0], index]
        for chunk in range(chunks):
            owner = lax.rem(info[4] + chunks - chunk, chunks)
            token = owner * part + iota((8, part), 1)
            found = jnp.zeros_like(token)
            for end in ends:
                found = found + (token >= end).astype(jnp.int32)
            key_group[:, chunk * part : (chunk + 1) * part] = found
        for p in range(TOGETHER):
            ones = slice((2 * p + 1) * PAIR, 2 * (p + 1) * PAIR)
            values[:, ones] = jnp.ones((values.shape[0], PAIR), bf16)
        x2_ref[...] = x1_ref[...]

    pairs = [slice(p * PAIR, (p + 1) * PAIR) for p in range(TOGETHER)]
    valued = [slice(2 * p * PAIR, 2 * (p + 1) * PAIR) for p in range(TOGETHER)]
    for chunk in range(chunks):
        at = slice(chunk * part, (chunk + 1) * part)
        keys[at] = kv_refs[chunk][0]
        for pair, both in zip(pairs, valued):
            values[at, both.start : both.start + PAIR] = kv_refs[chunk][1, :, pair]
    items = [(b, p) for p in range(TOGETHER) for b in range(tokens // CROSS_BLOCK)]
    rows = [slice(b * CROSS_BLOCK, (b + 1) * CROSS_BLOCK) for b, _ in items]
    scores = [
        mm_t(stack_heads(q_ref[r, pairs[p]]), keys[:, pairs[p]]) for (_, p), r in zip(items, rows)
    ]
    weights = []
    for (block, p), r, found in zip(items, rows, scores):
        own_group = query_group[r, 0:1]
        own_group = jnp.concatenate([own_group, own_group], axis=0)
        masked = jnp.where(own_group == key_group[0:1, :], found, neg_big)
        top = jnp.max(masked, axis=-1, keepdims=True)
        weights.append(jnp.exp(masked - top).astype(bf16))
        e_ref[p, block] = weights[-1]
    mixed = [mm(e, values[:, valued[p]]) for (_, p), e in zip(items, weights)]
    for (_, p), r, found in zip(items, rows, mixed):
        inverse = 1.0 / found[:, PAIR:]
        o_ref[r, pairs[p]] = join_heads(found[:, :PAIR] * inverse).astype(bf16)
        inv_ref[r, pairs[p]] = join_heads(inverse)
    x2_ref[...] += mm(o_ref[...], wo_ref[...])

    @pl.when(step == pl.num_programs(0) - 1)
    def _():
        h3_ref[...] = rms(x2_ref[...], gain_of(gain_ref)).astype(bf16)


def ffn_kernel(
    h_ref, c_ref, x2_ref, gain_ref, wg_ref, wu_ref, wd_ref,
    u_ref, dga_ref, dgb_ref, out_ref, dx_ref, e_ref,
    total, dh,
):
    step = pl.program_id(0)
    root = math.sqrt(2.0 / math.pi)
    gate = mm(h_ref[...], wg_ref[...])
    up = mm(h_ref[...], wu_ref[...])
    du = mm_t(c_ref[...], wd_ref[...])
    square = gate * gate
    bent = jnp.tanh(gate * (root + (0.044715 * root) * square))
    share = 0.5 + 0.5 * bent
    active = gate * share
    bend = (0.5 - 0.5 * bent) * (2.0 * root + (6 * 0.044715 * root) * square)
    slope = share + active * bend
    u_ref[...] = (active * up).astype(bf16)
    dgb_ref[...] = (du * active).astype(bf16)
    dga_ref[...] = (du * up * slope).astype(bf16)
    out_part = mm(u_ref[...], wd_ref[...])
    dh_part = mm_t(dga_ref[...], wg_ref[...]) + mm_t(dgb_ref[...], wu_ref[...])

    @pl.when(step == 0)
    def _():
        total[...] = x2_ref[...] + out_part
        dh[...] = dh_part

    @pl.when(step > 0)
    def _():
        total[...] += out_part
        dh[...] += dh_part

    @pl.when(step == pl.num_programs(0) - 1)
    def _():
        out_ref[...] = total[...].astype(bf16)
        back = rms_back(x2_ref[...], gain_of(gain_ref), dh[...])
        dx_ref[...] = c_ref[...].astype(f32) + back
        e_ref[...] = dx_ref[...].astype(bf16)


def cross_backward_kernel(chunks, *refs):
    e2_ref, wo_ref, o_ref, inv_ref, p_ref, q_ref, wq_ref, x1_ref, dx2_ref, gain_ref = refs[:10]
    kv_refs = refs[10 : 10 + chunks]
    dq_ref, dx_ref, e1_ref = refs[10 + chunks : 13 + chunks]
    dkv_refs = refs[13 + chunks : 13 + 2 * chunks]
    keys, values, dk, dv, dh = refs[13 + 2 * chunks :]
    step = pl.program_id(0)
    tokens = q_ref.shape[0]
    part = kv_refs[0].shape[1]

    for chunk in range(chunks):
        keys[chunk * part : (chunk + 1) * part] = kv_refs[chunk][0]
        values[chunk * part : (chunk + 1) * part] = kv_refs[chunk][1]
    grad = mm_t(e2_ref[...], wo_ref[...]).astype(bf16).astype(f32)
    grad = (grad * inv_ref[...]).astype(bf16)
    query_t = q_ref[...].T
    grad_t = grad.T
    pairs = [slice(p * PAIR, (p + 1) * PAIR) for p in range(TOGETHER)]
    items = [(b, p) for p in range(TOGETHER) for b in range(tokens // CROSS_BLOCK)]
    rows = [slice(b * CROSS_BLOCK, (b + 1) * CROSS_BLOCK) for b, _ in items]
    grad_probs = [
        mm_t(stack_heads(grad[r, pairs[p]]), values[:, pairs[p]]) for (_, p), r in zip(items, rows)
    ]
    for pair in range(TOGETHER):
        dv[pairs[pair]] = sum(
            mm(stack_heads_t(grad_t[pairs[p], r]), p_ref[p, b])
            for (b, p), r in zip(items, rows)
            if p == pair
        )
    scored = []
    for (block, p), r, found in zip(items, rows, grad_probs):
        weighed = grad[r, pairs[p]].astype(f32) * o_ref[r, pairs[p]].astype(f32)
        center = jnp.sum(stack_heads(weighed), axis=-1, keepdims=True)
        scored.append((p_ref[p, block].astype(f32) * (found - center)).astype(bf16))
    for (_, p), r, found in zip(items, rows, scored):
        dq_ref[r, pairs[p]] = join_heads(mm(found, keys[:, pairs[p]])).astype(bf16)
    for pair in range(TOGETHER):
        dk[pairs[pair]] = sum(
            mm(stack_heads_t(query_t[pairs[p], r]), found)
            for (_, p), r, found in zip(items, rows, scored)
            if p == pair
        )
    dk_rows = dk[...].T.astype(bf16)
    dv_rows = dv[...].T.astype(bf16)
    for chunk in range(chunks):
        dkv_refs[chunk][0] = dk_rows[chunk * part : (chunk + 1) * part]
        dkv_refs[chunk][1] = dv_rows[chunk * part : (chunk + 1) * part]
    dh_part = mm_t(dq_ref[...], wq_ref[...])

    @pl.when(step == 0)
    def _():
        dh[...] = dh_part

    @pl.when(step > 0)
    def _():
        dh[...] += dh_part

    @pl.when(step == pl.num_programs(0) - 1)
    def _():
        back = rms_back(x1_ref[...], gain_of(gain_ref), dh[...])
        dx_ref[...] = dx2_ref[...] + back
        e1_ref[...] = dx_ref[...].astype(bf16)


def self_backward_kernel(
    begin, e1_ref, wo_ref, o_ref, inv_ref, p_ref, q_ref, k_ref, v_ref, halo_ref, *refs
):
    dq_ref, dk_ref, dv_ref, back_ref, table_ref, keys, values, dk, dv, by_offset, offsets = refs[
        -11:
    ]
    step = pl.program_id(0)
    tokens = q_ref.shape[0]
    keys[0:REACH] = halo_ref[0]
    keys[REACH:] = k_ref[...]
    values[0:REACH] = halo_ref[1]
    values[REACH:] = v_ref[...]
    grad = mm_t(e1_ref[...], wo_ref[...]).astype(bf16).astype(f32)
    grad = (grad * inv_ref[...]).astype(bf16)
    query_t = q_ref[...].T
    grad_t = grad.T
    dk[...] = jnp.zeros_like(dk)
    dv[...] = jnp.zeros_like(dv)
    count = tokens // QUERY_BLOCK
    rows = [slice(b * QUERY_BLOCK, (b + 1) * QUERY_BLOCK) for b in range(count)]
    windows = [slice(b * QUERY_BLOCK, b * QUERY_BLOCK + WINDOW) for b in range(count)]
    grad_probs = [mm_t(stack_heads(grad[r, :]), values[w, :]) for r, w in zip(rows, windows)]
    for block, (r, w) in enumerate(zip(rows, windows)):
        dv[:, w] += mm(stack_heads_t(grad_t[:, r]), p_ref[0, block])
    scored = []
    for block, r in enumerate(rows):
        weighed = grad[r, :].astype(f32) * o_ref[r, :].astype(f32)
        center = jnp.sum(stack_heads(weighed), axis=-1, keepdims=True)
        exact = p_ref[0, block].astype(f32) * (grad_probs[block] - center)
        near = exact[:, QUERY_BLOCK:]
        by_offset[...] = near if block == 0 else by_offset[...] + near
        scored.append(exact.astype(bf16))
    for block, (r, w) in enumerate(zip(rows, windows)):
        dq_ref[r, :] = join_heads(mm(scored[block], keys[w, :])).astype(bf16)
        dk[:, w] += mm(stack_heads_t(query_t[:, r]), scored[block])
    dk_rows = dk[...].T
    dv_rows = dv[...].T
    back_ref[0] = dk_rows[:REACH].astype(bf16)
    back_ref[1] = dv_rows[:REACH].astype(bf16)
    dk_ref[...] = dk_rows[REACH:]
    dv_ref[...] = dv_rows[REACH:]

    @pl.when(step == 0)
    def _():
        offsets[...] = jnp.zeros_like(offsets)

    row_index = iota((QUERY_BLOCK, 2 * QUERY_BLOCK), 0)
    for head in range(2):
        tile = by_offset[head * QUERY_BLOCK : (head + 1) * QUERY_BLOCK, :]
        for bit in range(QUERY_BLOCK.bit_length() - 1):
            moved = pltpu.roll(tile, 2 * QUERY_BLOCK - (1 << bit), 1)
            tile = jnp.where((row_index >> bit) & 1 == 1, moved, tile)
        offsets[pl.ds(2 * (begin + step) + head, 1), :] = jnp.sum(tile, axis=0, keepdims=True)

    @pl.when(step == pl.num_programs(0) - 1)
    def _():
        lane = iota((1, 2 * QUERY_BLOCK), 1)
        far = BUCKETS - 1
        bucket = bucket_of(QUERY_BLOCK - lane)
        row = iota((BUCKETS, 2 * QUERY_BLOCK), 0)
        inside = (lane <= QUERY_BLOCK) & (bucket < far)
        sign = jnp.where(row == far, -1.0, jnp.where(row == bucket, 1.0, 0.0))
        table_ref[...] = lax.dot_general(
            jnp.where(inside, sign, 0.0), offsets[0:HEADS], (((1,), (1,)), ((), ())),
            precision=lax.Precision.HIGHEST, preferred_element_type=f32,
        )


def input_kernel(
    dq_ref, dkl_ref, dvl_ref, wq_ref, wk_ref, wv_ref, x_ref, dx1_ref, gain_ref, dx_ref
):
    dh = (
        mm_t(dq_ref[...], wq_ref[...])
        + mm_t(dkl_ref[...], wk_ref[...])
        + mm_t(dvl_ref[...], wv_ref[...])
    )
    back = rms_back(x_ref[...].astype(f32), gain_of(gain_ref), dh)
    dx_ref[...] = dx1_ref[...] + back


def put_tiles(out_ref, info, side, offset, found, shards):
    rows = found.shape[0] // shards
    first = HEADER + side * shards
    for shard in range(shards):
        for tile in range(found.shape[1] // LANES):
            piece = found[
                shard * rows : (shard + 1) * rows, tile * LANES : (tile + 1) * LANES
            ].astype(bf16)
            out_ref[
                info[first + shard], offset + tile * rows : offset + (tile + 1) * rows, :
            ] = piece


def gate_up_kernel(shards, info, h_ref, gk_ref, gs_ref, uk_ref, us_ref, keep_ref, send_ref, h_t):
    @pl.when(pl.program_id(0) == 0)
    def _():
        h_t[...] = h_ref[...].T

    half = keep_ref.shape[1] // 2
    put_tiles(keep_ref, info, 0, 0, mm(h_t[...], gk_ref[...]), shards)
    put_tiles(send_ref, info, 1, 0, mm(h_t[...], gs_ref[...]), shards)
    put_tiles(keep_ref, info, 0, half, mm(h_t[...], uk_ref[...]), shards)
    put_tiles(send_ref, info, 1, half, mm(h_t[...], us_ref[...]), shards)


def down_kernel(
    shards, info, u_ref, c_ref, left_ref, own_ref, other_ref, keep_ref, send_ref, u_t, found
):
    u_t[...] = u_ref[...].T
    rows = found.shape[0] // shards // 2
    columns = found.shape[1]
    tiles = columns // LANES
    for begin in range(0, c_ref.shape[1], columns):
        found[...] = mm(u_t[...], c_ref[:, begin : begin + columns])
        offset = begin // LANES * rows
        for shard in range(shards):
            for which, out_ref in enumerate((keep_ref, send_ref)):
                slot = info[HEADER + (2 + which) * shards + shard]
                start = pl.multiple_of((2 * shard + (info[1] ^ which)) * rows, rows)
                piece = found[pl.ds(start, rows), :].astype(bf16)
                for tile in range(tiles):
                    at = offset + tile * rows
                    lane = tile * LANES
                    out_ref[slot, at : at + rows, :] = piece[:, lane : lane + LANES]
    left = left_ref[...].T
    offset = c_ref.shape[1] // LANES * rows
    put_tiles(keep_ref, info, 2, offset, mm(left, own_ref[...]), shards)
    put_tiles(send_ref, info, 3, offset, mm(left, other_ref[...]), shards)


def square_kernel(shards, count, info, *refs):
    sides = refs[: 3 * count]
    keep_ref, send_ref = refs[3 * count :]
    rows = keep_ref.shape[1] // count
    for index in range(count):
        left_ref, own_ref, other_ref = sides[3 * index : 3 * index + 3]
        left = left_ref[...].T
        put_tiles(keep_ref, info, 0, index * rows, mm(left, own_ref[...]), shards)
        put_tiles(send_ref, info, 1, index * rows, mm(left, other_ref[...]), shards)


def memory_back_kernel(chunks, shards, info, memory_ref, wk_ref, wv_ref, *refs):
    parts = refs[:chunks]
    keep_ref, send_ref, dm_ref, found, grad, memory_t = refs[chunks + 2 :]
    columns = found.shape[1] // 2

    def add(which, weight_ref):
        total = parts[0][which].astype(f32)
        for other in parts[1:]:
            total = total + other[which].astype(f32)
        grad[...] = total.astype(bf16)
        share = mm_t(grad[...], weight_ref[...])
        dm_ref[...] = share if which == 0 else dm_ref[...] + share

    @pl.when(pl.program_id(0) == 0)
    def _():
        memory_t[...] = memory_ref[...].T
        add(0, wk_ref)

    @pl.when(pl.program_id(0) == 1)
    def _():
        add(1, wv_ref)

    found[...] = mm(memory_t[...], grad[...])
    for flip, out_ref in enumerate((keep_ref, send_ref)):
        start = pl.multiple_of((info[1] ^ flip) * columns, LANES)
        put_tiles(out_ref, info, flip, 0, found[:, pl.ds(start, columns)], shards)


def keys_values_kernel(
    shards, info, h_ref, dk_ref, dv_ref, ret_ref, keep_in, send_in,
    keep_ref, send_ref, dkl_ref, dvl_ref, found,
):
    head = h_ref.shape[0] - REACH
    rows = (keep_ref.shape[1] - keep_in.shape[1]) // 2
    keep_ref[:, 2 * rows :, :] = keep_in[...]
    send_ref[:, 2 * rows :, :] = send_in[...]
    columns = found.shape[1] // 2
    left = h_ref[...].T
    for which, own, low in ((0, dk_ref, dkl_ref), (1, dv_ref, dvl_ref)):
        low[:head, :] = own[:head, :].astype(bf16)
        low[head:, :] = (own[head:, :] + ret_ref[which].astype(f32)).astype(bf16)
        found[...] = mm(left, low[...])
        for flip, out_ref in enumerate((keep_ref, send_ref)):
            start = pl.multiple_of((info[1] ^ flip) * columns, LANES)
            half = found[:, pl.ds(start, columns)]
            put_tiles(out_ref, info, flip, which * rows, half, shards)


def query_gradient_kernel(
    shards, info, h_ref, own_ref, other_ref, *refs
):
    *tables, keep_ref, send_ref = refs
    left = h_ref[...].T
    rows = keep_ref.shape[1] - 16
    put_tiles(keep_ref, info, 0, 0, mm(left, own_ref[...]), shards)
    put_tiles(send_ref, info, 1, 0, mm(left, other_ref[...]), shards)
    count = BUCKETS // shards
    table = jnp.concatenate(
        [sum(ref[...] for ref in tables), jnp.zeros((BUCKETS, LANES - HEADS), f32)], axis=1
    )
    for index in range(shards):
        piece = table[index * count : (index + 1) * count]
        tile = jnp.concatenate([piece, jnp.zeros((16 - count, LANES), f32)], axis=0).astype(bf16)
        for which, out_ref in enumerate((keep_ref, send_ref)):
            out_ref[info[HEADER + which * shards + index], rows:] = tile


def sum_kernel(*refs):
    total = refs[0][...].astype(f32)
    for ref in refs[1:-1]:
        total = total + ref[...].astype(f32)
    refs[-1][...] = total.astype(bf16)


def halves(info, own_ref, other_ref):
    own, other = own_ref[...].astype(f32), other_ref[...].astype(f32)
    first = info[1] == 0
    return jnp.where(first, own, other), jnp.where(first, other, own)


def fill_square(out_ref, sides, offset):
    rows, columns = out_ref.shape
    count = columns // LANES // 2
    for side, found in enumerate(sides):
        for tile in range(count):
            start = (side * count + tile) * LANES
            out_ref[:, start : start + LANES] = found[
                offset + tile * rows : offset + (tile + 1) * rows
            ]


def put_gain(info, pairs, gain_ref, out_ref):
    rows, width = pairs[0][0].shape[0], gain_ref.shape[0]
    total = None
    for weight_ref, grad_ref in pairs:
        share = jnp.sum(weight_ref[...].astype(f32) * grad_ref[...], axis=1, keepdims=True)
        total = share if total is None else total + share
    here = iota((rows, width), 1) == info[0] * rows + iota((rows, width), 0)
    gain = jnp.sum(jnp.where(here, gain_of(gain_ref), 0.0), axis=1, keepdims=True)
    spread = jnp.where(iota((rows, LANES), 0) == iota((rows, LANES), 1), total / gain, 0.0)
    out_ref[...] = jnp.sum(spread, axis=0)[:rows]


def gate_unpack_kernel(
    info, own_ref, other_ref, wg_ref, wu_ref, gain_ref, gate_ref, up_ref, gg_ref
):
    rows, columns = gate_ref.shape
    count = columns // LANES // 2
    for side, found in enumerate(halves(info, own_ref, other_ref)):
        for tile in range(count):
            start = (side * count + tile) * LANES
            at = (tile // 2) * 4 * rows + (tile % 2) * rows
            gate_ref[:, start : start + LANES] = found[at : at + rows]
            up_ref[:, start : start + LANES] = found[at + 2 * rows : at + 3 * rows]
    put_gain(info, ((wg_ref, gate_ref), (wu_ref, up_ref)), gain_ref, gg_ref)


def down_unpack_kernel(info, own_ref, other_ref, down_ref, square_ref):
    half = down_ref.shape[0] // 2
    tiles = down_ref.shape[1] // LANES
    sides = halves(info, own_ref, other_ref)
    for side, found in enumerate(sides):
        for tile in range(tiles):
            down_ref[side * half : (side + 1) * half, tile * LANES : (tile + 1) * LANES] = found[
                tile * half : (tile + 1) * half
            ]
    fill_square(square_ref, sides, tiles * half)


def square_unpack_kernel(gained, info, own_ref, other_ref, *refs):
    weights, gain_ref = refs[: len(gained)], refs[len(gained)]
    out_refs, gg_ref = refs[len(gained) + 1 : -1], refs[-1]
    sides = halves(info, own_ref, other_ref)
    offset = 0
    for out_ref in out_refs:
        fill_square(out_ref, sides, offset)
        offset += out_ref.shape[0] * (out_ref.shape[1] // LANES // 2)
    put_gain(info, [(w, out_refs[at]) for w, at in zip(weights, gained)], gain_ref, gg_ref)


def last_unpack_kernel(info, own_ref, other_ref, *refs):
    table_ref = refs[7]
    square_unpack_kernel((0, 1, 2), info, own_ref, other_ref, *refs[:7], refs[8])
    rows, heads = table_ref.shape
    table_ref[...] = own_ref[own_ref.shape[0] - 16 :, :].astype(f32)[:rows, :heads]


def whole(shape):
    return pl.BlockSpec(shape, lambda *_: (0,) * len(shape))


def call(kernel, name, grid, ins, outs, args, scalars=(), scratch=(), alias=None, more=0):
    grant, time = PLANS[name]
    shapes = [
        pltpu.HBM(out[0], out[1]) if len(out) > 3 else jax.ShapeDtypeStruct(out[0], out[1])
        for out in outs
    ]
    return pl.pallas_call(
        kernel,
        out_shape=shapes,
        grid_spec=pltpu.PrefetchScalarGridSpec(
            num_scalar_prefetch=len(scalars),
            grid=grid,
            in_specs=list(ins),
            out_specs=[out[2] for out in outs],
            scratch_shapes=list(scratch),
        ),
        input_output_aliases=alias or {},
        compiler_params=pltpu.CompilerParams(
            dimension_semantics=("arbitrary",) * len(grid), vmem_limit_bytes=(grant + more) * 2**20
        ),
        cost_estimate=pl.CostEstimate(
            flops=int(time * COVER), bytes_accessed=1, transcendentals=0
        ),
        name=name,
    )(*scalars, *args)


def full(*arrays):
    return [whole(a.shape) for a in arrays]


def bit_orders(bits, last_first):
    low, high = list(range(min(bits, 2))), list(range(2, bits))
    first, second = (low + high[::-1], low[::-1] + high)
    if last_first:
        first, second = (high[::-1] + low, high + low[::-1])
    return [first, second]


def info_table(wide_size, narrow_size, order_pairs):
    bits = wide_size.bit_length() - 1
    rows = []
    for w in range(wide_size):
        for n in range(narrow_size):
            side = n % 2
            row = [w, side, side, w * (narrow_size // 2) + n // 2, n]
            row += [0] * (HEADER - len(row))
            for pair in order_pairs:
                for order in (pair[side], pair[1 - side]):
                    for shard in range(wide_size):
                        apart = shard ^ w
                        slot = [((apart >> bit) & 1) << (bits - 1 - k) for k, bit in enumerate(order)]
                        row.append(sum(slot))
            rows.append(row)
    return np.array(rows, np.int32)


def shards(
    inputs, memory, cotangent, answer_lengths, answer_groups, memory_lengths,
    gain_attn, self_query, self_key, self_value, self_out, bucket_bias_table,
    gain_cross, cross_query, cross_key_matrix, cross_value, cross_out,
    gain_ffn, hidden_gate, hidden_up, hidden_down,
):
    tokens, width = inputs.shape
    answer_lengths, answer_groups = answer_lengths.T, answer_groups.T
    part = memory.shape[0]
    hidden = hidden_gate.shape[1]
    wide_size = lax.axis_size("wide")
    narrow_size = lax.axis_size("narrow")
    wide_index = lax.axis_index("wide")
    narrow_index = lax.axis_index("narrow")
    bits = wide_size.bit_length() - 1
    orders = bit_orders(bits, False)
    orders_last_first = bit_orders(bits, True)
    info = jnp.asarray(info_table(wide_size, narrow_size, (orders, orders_last_first)))
    info = lax.dynamic_slice(
        info, (wide_index * narrow_size + narrow_index, 0), (1, info.shape[1])
    )
    info = info.reshape(-1)
    gains = (gain_attn, gain_cross, gain_ffn)
    turn = [info]

    both = ("wide", "narrow")

    def to_narrow(value, target):
        pairs = [(n, target(n)) for n in range(narrow_size) if target(n) is not None]
        return lax.ppermute(value, "narrow", pairs)

    def to_wide(value, place, order_pair):
        pairs = []
        for w in range(wide_size):
            for n in range(narrow_size):
                partner = w ^ (1 << order_pair[n % 2][place])
                pairs.append((w * narrow_size + n, partner * narrow_size + n))
        return lax.ppermute(value, both, pairs)

    def after(values, *needed):
        return lax.optimization_barrier((tuple(values), needed))[0]

    def now(*values):
        return after(values, *turn) if turn else values

    def run(kernel, name, grid, ins, outs, args, **more):
        found = call(kernel, name, grid, ins, outs, (*now(args[0]), *args[1:]), **more)
        turn[:] = found[:1]
        return found

    class Group:
        def __init__(self, keep, send, order_pair=orders):
            self.pieces, self.place, self.count = [keep], 0, wide_size
            self.order_pair = order_pair
            self.pending = to_narrow(send, lambda n: n ^ 1)

        def total(self, first, count, name="partial_sum"):
            pieces = (*self.pieces, self.pending)
            rows, lanes = pieces[0].shape[1:]
            parts = 2 if count * rows >= 4096 and rows % 32 == 0 else 1
            spec = lambda at: pl.BlockSpec(
                (count, rows // parts, lanes), lambda j: (at, j, 0)
            )
            shape = (count, rows, lanes)
            (found,) = run(
                sum_kernel, name, (parts,), [spec(first)] * len(pieces),
                [(shape, bf16, spec(0))], pieces,
            )
            self.pieces = list(pieces)
            return found

        def step(self, name="partial_sum"):
            self.count //= 2
            sent = self.total(1, self.count, name)
            self.pending = to_wide(sent, self.place, self.order_pair)
            self.place += 1

        def finish(self, name="partial_sum"):
            while self.place < bits:
                self.step()
            total = self.total(0, 1, name)
            step = 2
            while step < narrow_size:
                self.pieces, self.pending = [total], to_narrow(total, lambda n, s=step: n ^ s)
                total = self.total(0, 1)
                step *= 2
            return total[0], to_narrow(total, lambda n: n ^ 1)[0]

    lanes = TOGETHER * PAIR
    steps = (PAIRS // TOGETHER,)
    block = lambda rows: pl.BlockSpec((rows, lanes), lambda j, *_: (0, j))
    out_rows = pl.BlockSpec((lanes, width), lambda j, *_: (j, 0))

    model = (tokens, width)
    square = (width, width)
    in_hbm = pl.BlockSpec(memory_space=pltpu.HBM)
    normed, keys, values, tail, memory_own = run(
        project_kernel, "projections", (1,),
        [whole((width,))] + [in_hbm] * 6,
        [(model, bf16, whole(model))] * 3
        + [((2, REACH, width), bf16, whole((2, REACH, width)))]
        + [((2, part, width), bf16, whole((2, part, width)))],
        (gains[0],)
        + tuple(
            pltpu.with_memory_space_constraint(a, pltpu.HBM)
            for a in (inputs, memory, self_key, self_value, cross_key_matrix, cross_value)
        ),
        scratch=(pltpu.VMEM(model, bf16), pltpu.VMEM((part, width), bf16))
        + (pltpu.VMEM(square, bf16),) * 4
        + (pltpu.SemaphoreType.DMA((6,)),),
    )
    halo = to_narrow(tail, lambda n: n + 1 if n % 2 == 0 else None)
    memory_parts = [memory_own] + [
        to_narrow(memory_own, lambda n, s=shift: (n + s) % narrow_size)
        for shift in range(1, narrow_size)
    ]

    queries, bias = run(
        query_kernel, "queries", (1,),
        [whole(model), in_hbm, whole((HEADS, BUCKETS))],
        [
            (model, bf16, whole(model)),
            ((HEADS * QUERY_BLOCK, WINDOW), f32, whole((HEADS * QUERY_BLOCK, WINDOW))),
        ],
        (normed, pltpu.with_memory_space_constraint(self_query, pltpu.HBM), bucket_bias_table.T),
        scratch=(pltpu.VMEM(square, bf16), pltpu.SemaphoreType.DMA),
    )

    halo_block = pl.BlockSpec((2, REACH, lanes), lambda j, *_: (0, 0, j))
    blocks = tokens // QUERY_BLOCK
    self_probs = pl.BlockSpec(
        (TOGETHER, blocks, 2 * QUERY_BLOCK, WINDOW), lambda j, *_: (j, 0, 0, 0)
    )
    attended, inverse, probs, x1, normed_two, cross_rows = run(
        self_forward_kernel, "self_forward", steps,
        [block(tokens)] * 3 + [halo_block]
        + [pl.BlockSpec((2 * TOGETHER * QUERY_BLOCK, WINDOW), lambda j, *_: (j, 0))]
        + [whole(model), out_rows]
        + full(gains[1], cross_query),
        [
            (model, bf16, block(tokens)),
            (model, f32, block(tokens), "hbm"),
            ((PAIRS, blocks, 2 * QUERY_BLOCK, WINDOW), bf16, self_probs, "hbm"),
            (model, f32, whole(model)),
            (model, bf16, whole(model)),
            (model, bf16, whole(model)),
        ],
        (queries, keys, values, halo, bias, inputs, self_out, gains[1], cross_query),
        scalars=(info, answer_lengths),
        scratch=(
            pltpu.VMEM((tokens + REACH, lanes), bf16),
            pltpu.VMEM((tokens + REACH, 2 * lanes), bf16),
            pltpu.VMEM((tokens, LANES), jnp.int32),
        ),
    )

    memory_tokens = part * narrow_size
    memory_block = pl.BlockSpec((2, part, lanes), lambda j, *_: (0, 0, j))
    cross_blocks = tokens // CROSS_BLOCK
    cross_probs = pl.BlockSpec(
        (TOGETHER, cross_blocks, 2 * CROSS_BLOCK, memory_tokens), lambda j, *_: (j, 0, 0, 0)
    )
    attended_two, inverse_two, probs_two, x2, normed_three = run(
        functools.partial(cross_forward_kernel, narrow_size), "cross_forward", steps,
        [block(tokens), whole(model), out_rows, whole((width,))] + [memory_block] * narrow_size,
        [
            (model, bf16, block(tokens)),
            (model, f32, block(tokens), "hbm"),
            ((PAIRS, cross_blocks, 2 * CROSS_BLOCK, memory_tokens), bf16, cross_probs, "hbm"),
            (model, f32, whole(model)),
            (model, bf16, whole(model)),
        ],
        (cross_rows, x1, cross_out, gains[2], *memory_parts),
        scalars=(info, answer_lengths, answer_groups, memory_lengths),
        more=memory_tokens // 32 - 8,
        scratch=(
            pltpu.VMEM((memory_tokens, lanes), bf16),
            pltpu.VMEM((memory_tokens, 2 * lanes), bf16),
            pltpu.VMEM((tokens, LANES), jnp.int32),
            pltpu.VMEM((8, memory_tokens), jnp.int32),
        ),
    )

    inverse, probs, inverse_two, probs_two = (
        pltpu.with_memory_space_constraint(a, pltpu.HBM)
        for a in (inverse, probs, inverse_two, probs_two)
    )

    tile = 512
    wide_tile = pl.BlockSpec((width, tile), lambda j, *_: (0, j))
    token_tile = pl.BlockSpec((tokens, tile), lambda j, *_: (0, j))
    hidden_shape = (tokens, hidden)
    unit, grad_gate, grad_up, layer_out, dx2, e2 = run(
        ffn_kernel, "feed_forward", (hidden // tile,),
        [whole(model)] * 3
        + [whole((width,)), wide_tile, wide_tile]
        + [pl.BlockSpec((tile, width), lambda j, *_: (j, 0))],
        [(hidden_shape, bf16, token_tile)] * 3
        + [
            (model, bf16, whole(model)),
            (model, f32, whole(model)),
            (model, bf16, whole(model)),
        ],
        (normed_three, cotangent, x2, gains[2], hidden_gate, hidden_up, hidden_down),
        scratch=(pltpu.VMEM(model, f32), pltpu.VMEM(model, f32)),
    )

    square_rows = width // wide_size * (width // 2 // LANES)
    gate_rows = width // wide_size * (hidden // 2 // LANES)
    down_rows = hidden // wide_size // 2 * (width // LANES)
    step_rows = gate_rows // 2
    gate_side = lambda flip: pl.BlockSpec(
        (tokens, 256), lambda j, info: (0, (info[1] ^ flip) * (hidden // 512) + j)
    )
    half_side = lambda flip: pl.BlockSpec(
        (tokens, width // 2), lambda j, info: (0, info[1] ^ flip)
    )
    anywhere = pl.BlockSpec(memory_space=pl.ANY)

    gate_shape = (wide_size, 2 * gate_rows, LANES)
    step_spec = pl.BlockSpec((wide_size, step_rows, LANES), lambda j, *_: (0, j, 0))
    keep, send = run(
        functools.partial(gate_up_kernel, wide_size), "gate_up_gradient", (hidden // 512,),
        [whole(model), gate_side(0), gate_side(1), gate_side(0), gate_side(1)],
        [(gate_shape, bf16, step_spec)] * 2,
        (normed_three, grad_gate, grad_gate, grad_up, grad_up),
        scalars=(info,),
        scratch=(pltpu.VMEM((width, tokens), bf16),),
    )
    gate_group = Group(keep, send)
    down_shape = (wide_size, down_rows + square_rows, LANES)
    keep, send = run(
        functools.partial(down_kernel, wide_size), "down_gradient", (1,),
        [whole(hidden_shape), whole(model), whole(model), half_side(0), half_side(1)],
        [(down_shape, bf16, whole(down_shape))] * 2,
        (unit, cotangent, attended_two, e2, e2),
        scalars=(info,),
        scratch=(
            pltpu.VMEM((hidden, tokens), bf16),
            pltpu.VMEM((hidden, width // 2), f32),
        ),
    )
    down_group = Group(keep, send, orders_last_first)
    gate_group.step()

    grad_cross_rows, dx1, e1, *memory_grads = run(
        functools.partial(cross_backward_kernel, narrow_size), "cross_backward", steps,
        [whole(model), out_rows, block(tokens), block(tokens), cross_probs, block(tokens)]
        + [block(width), whole(model), whole(model), whole((width,))]
        + [memory_block] * narrow_size,
        [
            (model, bf16, block(tokens)),
            (model, f32, whole(model)),
            (model, bf16, whole(model)),
        ]
        + [((2, part, width), bf16, memory_block)] * narrow_size,
        (e2, cross_out, attended_two, inverse_two, probs_two, cross_rows, cross_query, x1, dx2)
        + (gains[1], *memory_parts),
        scratch=(
            pltpu.VMEM((memory_tokens, lanes), bf16),
            pltpu.VMEM((memory_tokens, lanes), bf16),
            pltpu.VMEM((lanes, memory_tokens), f32),
            pltpu.VMEM((lanes, memory_tokens), f32),
            pltpu.VMEM(model, f32),
        ),
        more=memory_tokens // 32 - 8,
    )
    memory_shares = [memory_grads[0]] + [
        to_narrow(memory_grads[shift], lambda n, s=shift: (n - s) % narrow_size)
        for shift in range(1, narrow_size)
    ]
    down_group.step()
    second_shape = (wide_size, 4 * square_rows, LANES)
    couple = ((normed_two, grad_cross_rows), (attended, e1))
    second_spec = pl.BlockSpec((wide_size, 2 * square_rows, LANES), lambda j, *_: (0, 0, 0))
    keep, send = run(
        functools.partial(square_kernel, wide_size, 2), "square_gradients", (1,),
        [whole(model), half_side(0), half_side(1)] * 2,
        [(second_shape, bf16, second_spec)] * 2,
        [side_of for left, right in couple for side_of in (left, right, right)],
        scalars=(info,),
    )
    memory_spec = pl.BlockSpec((wide_size, square_rows, LANES), lambda j, *_: (0, 2 + j, 0))
    keep, send, memory_grad = run(
        functools.partial(memory_back_kernel, narrow_size, wide_size), "memory_backward", (2,),
        full(memory, cross_key_matrix, cross_value, *memory_shares) + [anywhere] * 2,
        [(second_shape, bf16, memory_spec)] * 2
        + [((part, width), f32, whole((part, width)))],
        (memory, cross_key_matrix, cross_value, *memory_shares, keep, send),
        scalars=(info,),
        scratch=(
            pltpu.VMEM((width, width), f32),
            pltpu.VMEM((part, width), bf16),
            pltpu.VMEM((width, part), bf16),
        ),
        alias={4 + narrow_size: 0, 5 + narrow_size: 1},
    )
    second_group = Group(keep, send)
    gate_group.step()

    tables, carried, parts_of = [], [], 3
    for index in range(parts_of):
        count = PAIRS // parts_of
        begin = index * count
        at = lambda rows, b=begin: pl.BlockSpec((rows, PAIR), lambda j, *_: (0, b + j))
        here = lambda *lead, b=begin: pl.BlockSpec(
            (1, *lead), lambda j, *_: (b + j,) + (0,) * len(lead)
        )
        halo_at = pl.BlockSpec((2, REACH, PAIR), lambda j, *_, b=begin: (0, 0, b + j))
        out_at = pl.BlockSpec((PAIR, width), lambda j, *_, b=begin: (b + j, 0))
        if index:
            (None, second_group, gate_group)[index].step()
        if index == 2:
            down_group.step()
        *carried, table = run(
            functools.partial(self_backward_kernel, begin),
            "self_backward" if index else "self_backward_first", (count,),
            [whole(model), out_at, at(tokens), at(tokens)]
            + [here(blocks, 2 * QUERY_BLOCK, WINDOW)]
            + [at(tokens)] * 3 + [halo_at] + [anywhere] * len(carried),
            [
                (model, bf16, at(tokens)),
                (model, f32, at(tokens)),
                (model, f32, at(tokens)),
                ((2, REACH, width), bf16, halo_at),
                ((BUCKETS, HEADS), f32, whole((BUCKETS, HEADS))),
            ],
            (e1, self_out, attended, inverse, probs, queries, keys, values, halo, *carried),
            scratch=(
                pltpu.VMEM((tokens + REACH, PAIR), bf16),
                pltpu.VMEM((tokens + REACH, PAIR), bf16),
                pltpu.VMEM((PAIR, tokens + REACH), f32),
                pltpu.VMEM((PAIR, tokens + REACH), f32),
                pltpu.VMEM((2 * QUERY_BLOCK, 2 * QUERY_BLOCK), f32),
                pltpu.VMEM((16, 2 * QUERY_BLOCK), f32),
            ),
            alias={9 + i: i for i in range(4)} if index else None,
        )
        tables.append(table)
    grad_queries, grad_keys, grad_values, back = carried
    returned = to_narrow(back, lambda n: n - 1 if n % 2 == 1 else None)
    second_group.step()
    query_shape = (wide_size, square_rows + 16, LANES)
    last_shape = (wide_size, 3 * square_rows + 16, LANES)
    query_keep, query_send = run(
        functools.partial(query_gradient_kernel, wide_size), "query_gradient", (1,),
        [whole(model), half_side(0), half_side(1)] + [whole((BUCKETS, HEADS))] * parts_of,
        [(query_shape, bf16, whole(query_shape))] * 2,
        (normed, grad_queries, grad_queries, *tables),
        scalars=(info,),
    )
    keep, send, keys_low, values_low = run(
        functools.partial(keys_values_kernel, wide_size), "key_value_gradient", (1,),
        full(normed, grad_keys, grad_values, returned, query_keep, query_send),
        [(last_shape, bf16, whole(last_shape))] * 2 + [(model, bf16, whole(model))] * 2,
        (normed, grad_keys, grad_values, returned, query_keep, query_send),
        scalars=(info,),
        scratch=(pltpu.VMEM(square, f32),),
    )
    last_group = Group(keep, send)
    down_group.step("partial_sum_beside")
    gate_group.step()
    second_group.step()
    last_group.step()
    (input_grad,) = run(
        input_kernel, "input_gradient", (1,),
        full(grad_queries, keys_low, values_low)
        + full(self_query, self_key, self_value, inputs, dx1, gains[0]),
        [(model, f32, whole(model))],
        (grad_queries, keys_low, values_low)
        + (self_query, self_key, self_value, inputs, dx1, gains[0]),
    )

    square_out = ((width // wide_size, width), f32, whole((width // wide_size, width)))
    gate_out = ((width // wide_size, hidden), f32, whole((width // wide_size, hidden)))
    down_out = ((hidden // wide_size, width), f32, whole((hidden // wide_size, width)))
    size = width // wide_size
    gain_out = ((size,), f32, whole((size,)))
    own_rows = lambda columns: pl.BlockSpec((size, columns), lambda j, info: (info[0], 0))
    gate_own, gate_other = gate_group.finish()
    last_group.step()
    grad_gate_w, grad_up_w, grad_gain_ffn = run(
        gate_unpack_kernel, "gate_outputs", (1,),
        full(gate_own, gate_other) + [own_rows(hidden)] * 2 + [whole((width,))],
        [gate_out] * 2 + [gain_out],
        (gate_own, gate_other, hidden_gate, hidden_up, gain_ffn), scalars=(info,),
    )
    last_group.step("partial_sum_late")
    down_group.step("partial_sum_late")
    second_group.step("partial_sum_late")
    down_own, down_other = down_group.finish("partial_sum_late")
    second_own, second_other = second_group.finish("partial_sum_late")
    grad_down_w, grad_cross_out = run(
        down_unpack_kernel, "down_outputs", (1,), full(down_own, down_other),
        [down_out, square_out], (down_own, down_other), scalars=(info,),
    )
    last_group.step("partial_sum_late")
    (
        grad_cross_query, grad_self_out, grad_cross_key, grad_cross_value, grad_gain_cross,
    ) = run(
        functools.partial(square_unpack_kernel, (0,)), "second_outputs", (1,),
        full(second_own, second_other) + [own_rows(width), whole((width,))],
        [square_out] * 4 + [gain_out],
        (second_own, second_other, cross_query, gain_cross), scalars=(info,),
    )
    last_own, last_other = last_group.finish("partial_sum_late")
    table_out = ((BUCKETS // wide_size, HEADS), f32, whole((BUCKETS // wide_size, HEADS)))
    grad_self_key, grad_self_value, grad_self_query, grad_table, grad_gain_attn = run(
        last_unpack_kernel, "last_outputs", (1,),
        full(last_own, last_other) + [own_rows(width)] * 3 + [whole((width,))],
        [square_out] * 3 + [table_out, gain_out],
        (last_own, last_other, self_key, self_value, self_query, gain_attn), scalars=(info,),
    )
    return (
        layer_out,
        input_grad,
        memory_grad,
        grad_gain_attn,
        grad_self_query,
        grad_self_key,
        grad_self_value,
        grad_self_out,
        grad_table,
        grad_gain_cross,
        grad_cross_query,
        grad_cross_key,
        grad_cross_value,
        grad_cross_out,
        grad_gain_ffn,
        grad_gate_w,
        grad_up_w,
        grad_down_w,
    )


def solution(mesh):
    rows = P(("wide", "narrow"), None)
    vector, matrix = P("wide"), P("wide", None)
    return jax.shard_map(
        shards,
        mesh=mesh,
        in_specs=(rows,) * 3 + (P(),) * 18,
        out_specs=(rows,) * 3
        + (vector,)
        + (matrix,) * 5
        + (vector,)
        + (matrix,) * 4
        + (vector,)
        + (matrix,) * 3,
        check_vma=False,
    )
```

```python
import functools
import math

import jax
import jax.numpy as jnp
import numpy as np
from jax import lax
from jax.experimental import pallas as pl
from jax.experimental.pallas import tpu as pltpu
from jax.sharding import PartitionSpec as P

HEADS = 12
HEAD_DIM = 64
BUCKETS = 32
MAX_DIST = 128
ANSWERS = 8
GROUPS = 16
PAIR = 2 * HEAD_DIM
PAIRS = HEADS // 2
REACH = 256
QUERY_BLOCK = 128
WINDOW = REACH + QUERY_BLOCK
CROSS_BLOCK = 256
LANES = 128
HEADER = 8
TOGETHER = 2
PLANS = dict(
    projections=(14, 5.0),
    queries=(8, 3.0),
    self_forward=(20, 12.0),
    cross_forward=(16, 10.5),
    feed_forward=(24, 15.0),
    gate_up_gradient=(14, 6.0),
    down_gradient=(16, 4.4),
    cross_backward=(20, 12.0),
    square_gradients=(16, 2.0),
    memory_backward=(14, 3.6),
    self_backward_first=(20, 30.0),
    self_backward=(20, 7.0),
    query_gradient=(8, 9.0),
    key_value_gradient=(14, 2.4),
    input_gradient=(16, 1.0),
    partial_sum=(12, 1.0),
    partial_sum_late=(12, 0.0),
    partial_sum_beside=(12, 20.0),
    gate_outputs=(6, 0.0),
    down_outputs=(6, 0.0),
    second_outputs=(6, 0.0),
    last_outputs=(6, 0.0),
)
COVER = 1.15e9

epsilon = 1e-06
neg_big = -1e30
f32 = jnp.float32
bf16 = jnp.bfloat16


def mm(left, right):
    return jnp.dot(left, right, preferred_element_type=f32)


def mm_t(left, right):
    return lax.dot_general(left, right, (((1,), (1,)), ((), ())), preferred_element_type=f32)


def rms(values, gain_row):
    factor = lax.rsqrt(jnp.mean(values * values, axis=-1, keepdims=True) + epsilon)
    return values * factor * gain_row


def rms_back(values, gain_row, grad):
    factor = lax.rsqrt(jnp.mean(values * values, axis=-1, keepdims=True) + epsilon)
    unit = values * factor
    scaled = grad * gain_row
    center = jnp.mean(scaled * unit, axis=-1, keepdims=True)
    return factor * (scaled - unit * center)


def bucket_of(distance):
    exact_count = BUCKETS // 2
    log_count = BUCKETS - exact_count
    near_part = jnp.minimum(jnp.maximum(distance, 0), exact_count)
    far_part = jnp.zeros_like(distance)
    for level_index in range(1, log_count):
        edge = math.ceil(exact_count * (MAX_DIST / exact_count) ** (level_index / log_count))
        far_part = far_part + (distance >= edge).astype(jnp.int32)
    return near_part + far_part


def gain_of(ref):
    return ref[...].astype(f32).reshape(1, ref.shape[0])


def iota(shape, axis):
    return lax.broadcasted_iota(jnp.int32, shape, axis)


def low_lanes(shape):
    return iota(shape, len(shape) - 1) < HEAD_DIM


def stack_heads(rows):
    low = low_lanes(rows.shape)
    zero = jnp.zeros_like(rows)
    return jnp.concatenate([jnp.where(low, rows, zero), jnp.where(low, zero, rows)], axis=0)


def stack_heads_t(columns):
    low = iota(columns.shape, 0) < HEAD_DIM
    zero = jnp.zeros_like(columns)
    return jnp.concatenate([jnp.where(low, columns, zero), jnp.where(low, zero, columns)], axis=1)


def join_heads(stacked):
    half = stacked.shape[0] // 2
    return jnp.where(low_lanes((half, PAIR)), stacked[:half], stacked[half:])


def offset_bucket():
    lane = iota((1, 4 * QUERY_BLOCK), 1)
    distance = jnp.where(lane < WINDOW, REACH - lane, REACH + 4 * QUERY_BLOCK - lane)
    chosen = iota((BUCKETS, 4 * QUERY_BLOCK), 0) == bucket_of(distance)
    return distance, chosen


def answer_ends(lengths, row):
    total, ends = lengths[0, row], []
    for index in range(1, ANSWERS):
        ends.append(total)
        total = total + lengths[index, row]
    return ends


def project_kernel(
    gain_ref, x_hbm, memory_hbm, wk_hbm, wv_hbm, wck_hbm, wcv_hbm,
    h_ref, k_ref, v_ref, tail_ref, memory_out,
    x_ref, memory_ref, wk_ref, wv_ref, wck_ref, wcv_ref, sems,
):
    copies = [
        pltpu.make_async_copy(source, target, sems.at[index])
        for index, (source, target) in enumerate(
            (
                (x_hbm, x_ref),
                (memory_hbm, memory_ref),
                (wck_hbm, wck_ref),
                (wcv_hbm, wcv_ref),
                (wk_hbm, wk_ref),
                (wv_hbm, wv_ref),
            )
        )
    ]
    for copy in copies:
        copy.start()
    copies[0].wait()
    h_ref[...] = rms(x_ref[...].astype(f32), gain_of(gain_ref)).astype(bf16)
    copies[1].wait()
    copies[2].wait()
    memory_out[0] = mm(memory_ref[...], wck_ref[...]).astype(bf16)
    copies[3].wait()
    memory_out[1] = mm(memory_ref[...], wcv_ref[...]).astype(bf16)
    tokens = h_ref.shape[0]
    copies[4].wait()
    k_ref[...] = mm(h_ref[...], wk_ref[...]).astype(bf16)
    tail_ref[0] = k_ref[tokens - REACH :, :]
    copies[5].wait()
    v_ref[...] = mm(h_ref[...], wv_ref[...]).astype(bf16)
    tail_ref[1] = v_ref[tokens - REACH :, :]


def query_kernel(h_ref, wq_hbm, table_ref, q_ref, bias_ref, wq_ref, sem):
    copy = pltpu.make_async_copy(wq_hbm, wq_ref, sem)
    copy.start()
    distance, chosen = offset_bucket()
    base = jnp.where(distance < 0, neg_big, mm(table_ref[...], chosen.astype(bf16)))
    for head in range(HEADS):
        spread = jnp.broadcast_to(base[head : head + 1], (QUERY_BLOCK, 4 * QUERY_BLOCK))
        skewed = pltpu.roll(spread, 0, 1, stride=1, stride_axis=0)
        bias_ref[head * QUERY_BLOCK : (head + 1) * QUERY_BLOCK, :] = skewed[:, :WINDOW]
    copy.wait()
    q_ref[...] = mm(h_ref[...], wq_ref[...]).astype(bf16)


def self_forward_kernel(
    info, lengths,
    q_ref, k_ref, v_ref, halo_ref, bias, x_ref, wo_ref, gain_ref, wq_ref,
    o_ref, inv_ref, e_ref, x1_ref, h2_ref, qc_ref,
    keys, values, reach,
):
    step = pl.program_id(0)
    tokens = q_ref.shape[0]

    @pl.when(step == 0)
    def _():
        place = info[2] * tokens + iota((tokens, LANES), 0)
        start = jnp.zeros_like(place)
        for end in answer_ends(lengths, info[3]):
            start = jnp.where(place >= end, end, start)
        reach[...] = place - start
        for p in range(TOGETHER):
            ones = slice((2 * p + 1) * PAIR, 2 * (p + 1) * PAIR)
            values[:, ones] = jnp.ones((values.shape[0], PAIR), bf16)
        x1_ref[...] = x_ref[...].astype(f32)

    keys[0:REACH] = halo_ref[0]
    keys[REACH:] = k_ref[...]
    pairs = [slice(p * PAIR, (p + 1) * PAIR) for p in range(TOGETHER)]
    valued = [slice(2 * p * PAIR, 2 * (p + 1) * PAIR) for p in range(TOGETHER)]
    for pair, both in zip(pairs, valued):
        own = slice(both.start, both.start + PAIR)
        values[0:REACH, own] = halo_ref[1, :, pair]
        values[REACH:, own] = v_ref[:, pair]

    distance = REACH + iota((QUERY_BLOCK, WINDOW), 0) - iota((QUERY_BLOCK, WINDOW), 1)
    distance = jnp.concatenate([distance, distance], axis=0)
    items = [(b, p) for p in range(TOGETHER) for b in range(tokens // QUERY_BLOCK)]
    rows = [slice(b * QUERY_BLOCK, (b + 1) * QUERY_BLOCK) for b, _ in items]
    windows = [slice(b * QUERY_BLOCK, b * QUERY_BLOCK + WINDOW) for b, _ in items]
    scores = [
        mm_t(stack_heads(q_ref[r, pairs[p]]), keys[w, pairs[p]])
        for (_, p), r, w in zip(items, rows, windows)
    ]
    weights = []
    for (block, p), r, found in zip(items, rows, scores):
        own_reach = reach[r, 0:1]
        own_reach = jnp.concatenate([own_reach, own_reach], axis=0)
        shifted = found + bias[2 * p * QUERY_BLOCK : 2 * (p + 1) * QUERY_BLOCK, :]
        masked = jnp.where(distance <= own_reach, shifted, neg_big)
        top = jnp.max(masked, axis=-1, keepdims=True)
        weights.append(jnp.exp(masked - top).astype(bf16))
        e_ref[p, block] = weights[-1]
    mixed = [mm(e, values[w, valued[p]]) for (_, p), e, w in zip(items, weights, windows)]
    for (_, p), r, found in zip(items, rows, mixed):
        inverse = 1.0 / found[:, PAIR:]
        o_ref[r, pairs[p]] = join_heads(found[:, :PAIR] * inverse).astype(bf16)
        inv_ref[r, pairs[p]] = join_heads(inverse)
    x1_ref[...] += mm(o_ref[...], wo_ref[...])

    @pl.when(step == pl.num_programs(0) - 1)
    def _():
        h2_ref[...] = rms(x1_ref[...], gain_of(gain_ref)).astype(bf16)
        qc_ref[...] = mm(h2_ref[...], wq_ref[...]).astype(bf16)


def cross_forward_kernel(together, chunks, info, lengths, groups, bounds, *refs):
    q_ref, x1_ref, wo_ref, gain_ref = refs[:4]
    kv_refs = refs[4 : 4 + chunks]
    o_ref, inv_ref, e_ref, x2_ref, h3_ref = refs[4 + chunks : 9 + chunks]
    keys, values, query_group, key_group = refs[9 + chunks :]
    step = pl.program_id(0)
    tokens = q_ref.shape[0]
    part = kv_refs[0].shape[1]

    @pl.when(step == 0)
    def _():
        place = info[2] * tokens + iota((tokens, LANES), 0)
        group = jnp.zeros_like(place) + groups[0, info[3]]
        for index, end in enumerate(answer_ends(lengths, info[3])):
            group = jnp.where(place >= end, groups[index + 1, info[3]], group)
        query_group[...] = group
        total, ends = bounds[info[0], 0], []
        for index in range(1, GROUPS):
            ends.append(total)
            total = total + bounds[info[0], index]
        for chunk in range(chunks):
            owner = lax.rem(info[4] + chunks - chunk, chunks)
            token = owner * part + iota((8, part), 1)
            found = jnp.zeros_like(token)
            for end in ends:
                found = found + (token >= end).astype(jnp.int32)
            key_group[:, chunk * part : (chunk + 1) * part] = found
        for p in range(together):
            ones = slice((2 * p + 1) * PAIR, 2 * (p + 1) * PAIR)
            values[:, ones] = jnp.ones((values.shape[0], PAIR), bf16)
        x2_ref[...] = x1_ref[...]

    pairs = [slice(p * PAIR, (p + 1) * PAIR) for p in range(together)]
    valued = [slice(2 * p * PAIR, 2 * (p + 1) * PAIR) for p in range(together)]
    for chunk in range(chunks):
        at = slice(chunk * part, (chunk + 1) * part)
        keys[at] = kv_refs[chunk][0]
        for pair, both in zip(pairs, valued):
            values[at, both.start : both.start + PAIR] = kv_refs[chunk][1, :, pair]
    items = [(b, p) for p in range(together) for b in range(tokens // CROSS_BLOCK)]
    rows = [slice(b * CROSS_BLOCK, (b + 1) * CROSS_BLOCK) for b, _ in items]
    scores = [
        mm_t(stack_heads(q_ref[r, pairs[p]]), keys[:, pairs[p]]) for (_, p), r in zip(items, rows)
    ]
    weights = []
    for (block, p), r, found in zip(items, rows, scores):
        own_group = query_group[r, 0:1]
        own_group = jnp.concatenate([own_group, own_group], axis=0)
        masked = jnp.where(own_group == key_group[0:1, :], found, neg_big)
        top = jnp.max(masked, axis=-1, keepdims=True)
        weights.append(jnp.exp(masked - top).astype(bf16))
        e_ref[p, block] = weights[-1]
    mixed = [mm(e, values[:, valued[p]]) for (_, p), e in zip(items, weights)]
    for (_, p), r, found in zip(items, rows, mixed):
        inverse = 1.0 / found[:, PAIR:]
        o_ref[r, pairs[p]] = join_heads(found[:, :PAIR] * inverse).astype(bf16)
        inv_ref[r, pairs[p]] = join_heads(inverse)
    x2_ref[...] += mm(o_ref[...], wo_ref[...])

    @pl.when(step == pl.num_programs(0) - 1)
    def _():
        h3_ref[...] = rms(x2_ref[...], gain_of(gain_ref)).astype(bf16)


def ffn_kernel(
    h_ref, c_ref, x2_ref, gain_ref, wg_ref, wu_ref, wd_ref,
    u_ref, dga_ref, dgb_ref, out_ref, dx_ref, e_ref,
    total, dh,
):
    step = pl.program_id(0)
    root = math.sqrt(2.0 / math.pi)
    gate = mm(h_ref[...], wg_ref[...])
    up = mm(h_ref[...], wu_ref[...])
    du = mm_t(c_ref[...], wd_ref[...])
    square = gate * gate
    bent = jnp.tanh(gate * (root + (0.044715 * root) * square))
    share = 0.5 + 0.5 * bent
    active = gate * share
    bend = (0.5 - 0.5 * bent) * (2.0 * root + (6 * 0.044715 * root) * square)
    slope = share + active * bend
    u_ref[...] = (active * up).astype(bf16)
    dgb_ref[...] = (du * active).astype(bf16)
    dga_ref[...] = (du * up * slope).astype(bf16)
    out_part = mm(u_ref[...], wd_ref[...])
    dh_part = mm_t(dga_ref[...], wg_ref[...]) + mm_t(dgb_ref[...], wu_ref[...])

    @pl.when(step == 0)
    def _():
        total[...] = x2_ref[...] + out_part
        dh[...] = dh_part

    @pl.when(step > 0)
    def _():
        total[...] += out_part
        dh[...] += dh_part

    @pl.when(step == pl.num_programs(0) - 1)
    def _():
        out_ref[...] = total[...].astype(bf16)
        back = rms_back(x2_ref[...], gain_of(gain_ref), dh[...])
        dx_ref[...] = c_ref[...].astype(f32) + back
        e_ref[...] = dx_ref[...].astype(bf16)


def cross_backward_kernel(together, chunks, *refs):
    e2_ref, wo_ref, o_ref, inv_ref, p_ref, q_ref, wq_ref, x1_ref, dx2_ref, gain_ref = refs[:10]
    kv_refs = refs[10 : 10 + chunks]
    dq_ref, dx_ref, e1_ref = refs[10 + chunks : 13 + chunks]
    dkv_refs = refs[13 + chunks : 13 + 2 * chunks]
    keys, values, dk, dv, dh = refs[13 + 2 * chunks :]
    step = pl.program_id(0)
    tokens = q_ref.shape[0]
    part = kv_refs[0].shape[1]

    for chunk in range(chunks):
        keys[chunk * part : (chunk + 1) * part] = kv_refs[chunk][0]
        values[chunk * part : (chunk + 1) * part] = kv_refs[chunk][1]
    grad = mm_t(e2_ref[...], wo_ref[...]).astype(bf16).astype(f32)
    grad = (grad * inv_ref[...]).astype(bf16)
    query_t = q_ref[...].T
    grad_t = grad.T
    pairs = [slice(p * PAIR, (p + 1) * PAIR) for p in range(together)]
    items = [(b, p) for p in range(together) for b in range(tokens // CROSS_BLOCK)]
    rows = [slice(b * CROSS_BLOCK, (b + 1) * CROSS_BLOCK) for b, _ in items]
    grad_probs = [
        mm_t(stack_heads(grad[r, pairs[p]]), values[:, pairs[p]]) for (_, p), r in zip(items, rows)
    ]
    for pair in range(together):
        dv[pairs[pair]] = sum(
            mm(stack_heads_t(grad_t[pairs[p], r]), p_ref[p, b])
            for (b, p), r in zip(items, rows)
            if p == pair
        )
    scored = []
    for (block, p), r, found in zip(items, rows, grad_probs):
        weighed = grad[r, pairs[p]].astype(f32) * o_ref[r, pairs[p]].astype(f32)
        center = jnp.sum(stack_heads(weighed), axis=-1, keepdims=True)
        scored.append((p_ref[p, block].astype(f32) * (found - center)).astype(bf16))
    for (_, p), r, found in zip(items, rows, scored):
        dq_ref[r, pairs[p]] = join_heads(mm(found, keys[:, pairs[p]])).astype(bf16)
    for pair in range(together):
        dk[pairs[pair]] = sum(
            mm(stack_heads_t(query_t[pairs[p], r]), found)
            for (_, p), r, found in zip(items, rows, scored)
            if p == pair
        )
    dk_rows = dk[...].T.astype(bf16)
    dv_rows = dv[...].T.astype(bf16)
    for chunk in range(chunks):
        dkv_refs[chunk][0] = dk_rows[chunk * part : (chunk + 1) * part]
        dkv_refs[chunk][1] = dv_rows[chunk * part : (chunk + 1) * part]
    dh_part = mm_t(dq_ref[...], wq_ref[...])

    @pl.when(step == 0)
    def _():
        dh[...] = dh_part

    @pl.when(step > 0)
    def _():
        dh[...] += dh_part

    @pl.when(step == pl.num_programs(0) - 1)
    def _():
        back = rms_back(x1_ref[...], gain_of(gain_ref), dh[...])
        dx_ref[...] = dx2_ref[...] + back
        e1_ref[...] = dx_ref[...].astype(bf16)


def self_backward_kernel(
    begin, e1_ref, wo_ref, o_ref, inv_ref, p_hbm, q_ref, k_ref, v_ref, halo_ref, *refs
):
    dq_ref, dk_ref, dv_ref, back_ref, table_ref = refs[-13:-8]
    keys, values, dk, dv, by_offset, offsets, p_ref, sem = refs[-8:]
    copy = pltpu.make_async_copy(p_hbm.at[pl.ds(begin, TOGETHER)], p_ref, sem)
    copy.start()
    tokens = q_ref.shape[0]
    keys[0:REACH] = halo_ref[0]
    keys[REACH:] = k_ref[...]
    values[0:REACH] = halo_ref[1]
    values[REACH:] = v_ref[...]
    grad = mm_t(e1_ref[...], wo_ref[...]).astype(bf16).astype(f32)
    grad = (grad * inv_ref[...]).astype(bf16)
    query_t = q_ref[...].T
    grad_t = grad.T
    dk[...] = jnp.zeros_like(dk)
    dv[...] = jnp.zeros_like(dv)
    offsets[...] = jnp.zeros_like(offsets)
    pairs = [slice(p * PAIR, (p + 1) * PAIR) for p in range(TOGETHER)]
    items = [(b, p) for p in range(TOGETHER) for b in range(tokens // QUERY_BLOCK)]
    rows = [slice(b * QUERY_BLOCK, (b + 1) * QUERY_BLOCK) for b, _ in items]
    windows = [slice(b * QUERY_BLOCK, b * QUERY_BLOCK + WINDOW) for b, _ in items]
    grad_probs = [
        mm_t(stack_heads(grad[r, pairs[p]]), values[w, pairs[p]])
        for (_, p), r, w in zip(items, rows, windows)
    ]
    centers = []
    for (_, p), r in zip(items, rows):
        weighed = grad[r, pairs[p]].astype(f32) * o_ref[r, pairs[p]].astype(f32)
        centers.append(jnp.sum(stack_heads(weighed), axis=-1, keepdims=True))
    copy.wait()
    for (block, p), r, w in zip(items, rows, windows):
        dv[pairs[p], w] += mm(stack_heads_t(grad_t[pairs[p], r]), p_ref[p, block])
    scored = []
    for (block, p), found, center in zip(items, grad_probs, centers):
        exact = p_ref[p, block].astype(f32) * (found - center)
        near = exact[:, QUERY_BLOCK:]
        by_offset[p] = near if block == 0 else by_offset[p] + near
        scored.append(exact.astype(bf16))
    for (_, p), r, w, found in zip(items, rows, windows, scored):
        dq_ref[r, pairs[p]] = join_heads(mm(found, keys[w, pairs[p]])).astype(bf16)
        dk[pairs[p], w] += mm(stack_heads_t(query_t[pairs[p], r]), found)
    dk_rows = dk[...].T
    dv_rows = dv[...].T
    back_ref[0] = dk_rows[:REACH].astype(bf16)
    back_ref[1] = dv_rows[:REACH].astype(bf16)
    dk_ref[...] = dk_rows[REACH:]
    dv_ref[...] = dv_rows[REACH:]

    row_index = iota((QUERY_BLOCK, 2 * QUERY_BLOCK), 0)
    for p in range(TOGETHER):
        for head in range(2):
            tile = by_offset[p, head * QUERY_BLOCK : (head + 1) * QUERY_BLOCK, :]
            for bit in range(QUERY_BLOCK.bit_length() - 1):
                moved = pltpu.roll(tile, 2 * QUERY_BLOCK - (1 << bit), 1)
                tile = jnp.where((row_index >> bit) & 1 == 1, moved, tile)
            at = 2 * (begin + p) + head
            offsets[at : at + 1, :] = jnp.sum(tile, axis=0, keepdims=True)

    lane = iota((1, 2 * QUERY_BLOCK), 1)
    far = BUCKETS - 1
    bucket = bucket_of(QUERY_BLOCK - lane)
    row = iota((BUCKETS, 2 * QUERY_BLOCK), 0)
    inside = (lane <= QUERY_BLOCK) & (bucket < far)
    sign = jnp.where(row == far, -1.0, jnp.where(row == bucket, 1.0, 0.0))
    table_ref[...] = lax.dot_general(
        jnp.where(inside, sign, 0.0), offsets[0:HEADS], (((1,), (1,)), ((), ())),
        precision=lax.Precision.HIGHEST, preferred_element_type=f32,
    )


def input_kernel(
    dq_ref, dkl_ref, dvl_ref, wq_ref, wk_ref, wv_ref, x_ref, dx1_ref, gain_ref, dx_ref
):
    dh = (
        mm_t(dq_ref[...], wq_ref[...])
        + mm_t(dkl_ref[...], wk_ref[...])
        + mm_t(dvl_ref[...], wv_ref[...])
    )
    back = rms_back(x_ref[...].astype(f32), gain_of(gain_ref), dh)
    dx_ref[...] = dx1_ref[...] + back


def put_tiles(out_ref, info, side, offset, found, shards):
    rows = found.shape[0] // shards
    first = HEADER + side * shards
    for shard in range(shards):
        for tile in range(found.shape[1] // LANES):
            piece = found[
                shard * rows : (shard + 1) * rows, tile * LANES : (tile + 1) * LANES
            ].astype(bf16)
            out_ref[
                info[first + shard], offset + tile * rows : offset + (tile + 1) * rows, :
            ] = piece


def gate_up_kernel(shards, info, h_ref, gk_ref, gs_ref, uk_ref, us_ref, keep_ref, send_ref, h_t):
    @pl.when(pl.program_id(0) == 0)
    def _():
        h_t[...] = h_ref[...].T

    half = keep_ref.shape[1] // 2
    put_tiles(keep_ref, info, 0, 0, mm(h_t[...], gk_ref[...]), shards)
    put_tiles(send_ref, info, 1, 0, mm(h_t[...], gs_ref[...]), shards)
    put_tiles(keep_ref, info, 0, half, mm(h_t[...], uk_ref[...]), shards)
    put_tiles(send_ref, info, 1, half, mm(h_t[...], us_ref[...]), shards)


def down_kernel(
    shards, info, u_ref, c_ref, left_ref, own_ref, other_ref, keep_ref, send_ref, u_t, found
):
    u_t[...] = u_ref[...].T
    rows = found.shape[0] // shards // 2
    columns = found.shape[1]
    tiles = columns // LANES
    for begin in range(0, c_ref.shape[1], columns):
        found[...] = mm(u_t[...], c_ref[:, begin : begin + columns])
        offset = begin // LANES * rows
        for shard in range(shards):
            for which, out_ref in enumerate((keep_ref, send_ref)):
                slot = info[HEADER + (2 + which) * shards + shard]
                start = pl.multiple_of((2 * shard + (info[1] ^ which)) * rows, rows)
                piece = found[pl.ds(start, rows), :].astype(bf16)
                for tile in range(tiles):
                    at = offset + tile * rows
                    lane = tile * LANES
                    out_ref[slot, at : at + rows, :] = piece[:, lane : lane + LANES]
    left = left_ref[...].T
    offset = c_ref.shape[1] // LANES * rows
    put_tiles(keep_ref, info, 2, offset, mm(left, own_ref[...]), shards)
    put_tiles(send_ref, info, 3, offset, mm(left, other_ref[...]), shards)


def square_kernel(shards, count, info, *refs):
    sides = refs[: 3 * count]
    keep_ref, send_ref = refs[3 * count :]
    rows = keep_ref.shape[1] // count
    for index in range(count):
        left_ref, own_ref, other_ref = sides[3 * index : 3 * index + 3]
        left = left_ref[...].T
        put_tiles(keep_ref, info, 0, index * rows, mm(left, own_ref[...]), shards)
        put_tiles(send_ref, info, 1, index * rows, mm(left, other_ref[...]), shards)


def memory_back_kernel(chunks, shards, info, memory_ref, wk_ref, wv_ref, *refs):
    parts = refs[:chunks]
    keep_ref, send_ref, dm_ref, found, grad, memory_t = refs[chunks + 2 :]
    columns = found.shape[1] // 2

    def add(which, weight_ref):
        total = parts[0][which].astype(f32)
        for other in parts[1:]:
            total = total + other[which].astype(f32)
        grad[...] = total.astype(bf16)
        share = mm_t(grad[...], weight_ref[...])
        dm_ref[...] = share if which == 0 else dm_ref[...] + share

    @pl.when(pl.program_id(0) == 0)
    def _():
        memory_t[...] = memory_ref[...].T
        add(0, wk_ref)

    @pl.when(pl.program_id(0) == 1)
    def _():
        add(1, wv_ref)

    found[...] = mm(memory_t[...], grad[...])
    for flip, out_ref in enumerate((keep_ref, send_ref)):
        start = pl.multiple_of((info[1] ^ flip) * columns, LANES)
        put_tiles(out_ref, info, flip, 0, found[:, pl.ds(start, columns)], shards)


def keys_values_kernel(
    shards, info, h_ref, dk_ref, dv_ref, ret_ref, keep_in, send_in,
    keep_ref, send_ref, dkl_ref, dvl_ref, found,
):
    head = h_ref.shape[0] - REACH
    rows = (keep_ref.shape[1] - keep_in.shape[1]) // 2
    keep_ref[:, 2 * rows :, :] = keep_in[...]
    send_ref[:, 2 * rows :, :] = send_in[...]
    columns = found.shape[1] // 2
    left = h_ref[...].T
    for which, own, low in ((0, dk_ref, dkl_ref), (1, dv_ref, dvl_ref)):
        low[:head, :] = own[:head, :].astype(bf16)
        low[head:, :] = (own[head:, :] + ret_ref[which].astype(f32)).astype(bf16)
        found[...] = mm(left, low[...])
        for flip, out_ref in enumerate((keep_ref, send_ref)):
            start = pl.multiple_of((info[1] ^ flip) * columns, LANES)
            half = found[:, pl.ds(start, columns)]
            put_tiles(out_ref, info, flip, which * rows, half, shards)


def query_gradient_kernel(
    shards, info, h_ref, own_ref, other_ref, *refs
):
    *tables, keep_ref, send_ref = refs
    left = h_ref[...].T
    rows = keep_ref.shape[1] - 16
    put_tiles(keep_ref, info, 0, 0, mm(left, own_ref[...]), shards)
    put_tiles(send_ref, info, 1, 0, mm(left, other_ref[...]), shards)
    count = BUCKETS // shards
    table = jnp.concatenate(
        [sum(ref[...] for ref in tables), jnp.zeros((BUCKETS, LANES - HEADS), f32)], axis=1
    )
    for index in range(shards):
        piece = table[index * count : (index + 1) * count]
        tile = jnp.concatenate([piece, jnp.zeros((16 - count, LANES), f32)], axis=0).astype(bf16)
        for which, out_ref in enumerate((keep_ref, send_ref)):
            out_ref[info[HEADER + which * shards + index], rows:] = tile


def sum_kernel(*refs):
    total = refs[0][...].astype(f32)
    for ref in refs[1:-1]:
        total = total + ref[...].astype(f32)
    refs[-1][...] = total.astype(bf16)


def halves(info, own_ref, other_ref):
    own, other = own_ref[...].astype(f32), other_ref[...].astype(f32)
    first = info[1] == 0
    return jnp.where(first, own, other), jnp.where(first, other, own)


def fill_square(out_ref, sides, offset):
    rows, columns = out_ref.shape
    count = columns // LANES // 2
    for side, found in enumerate(sides):
        for tile in range(count):
            start = (side * count + tile) * LANES
            out_ref[:, start : start + LANES] = found[
                offset + tile * rows : offset + (tile + 1) * rows
            ]


def put_gain(info, pairs, gain_ref, out_ref):
    rows, width = pairs[0][0].shape[0], gain_ref.shape[0]
    total = None
    for weight_ref, grad_ref in pairs:
        share = jnp.sum(weight_ref[...].astype(f32) * grad_ref[...], axis=1, keepdims=True)
        total = share if total is None else total + share
    here = iota((rows, width), 1) == info[0] * rows + iota((rows, width), 0)
    gain = jnp.sum(jnp.where(here, gain_of(gain_ref), 0.0), axis=1, keepdims=True)
    spread = jnp.where(iota((rows, LANES), 0) == iota((rows, LANES), 1), total / gain, 0.0)
    out_ref[...] = jnp.sum(spread, axis=0)[:rows]


def gate_unpack_kernel(
    info, own_ref, other_ref, wg_ref, wu_ref, gain_ref, gate_ref, up_ref, gg_ref
):
    rows, columns = gate_ref.shape
    count = columns // LANES // 2
    for side, found in enumerate(halves(info, own_ref, other_ref)):
        for tile in range(count):
            start = (side * count + tile) * LANES
            at = (tile // 2) * 4 * rows + (tile % 2) * rows
            gate_ref[:, start : start + LANES] = found[at : at + rows]
            up_ref[:, start : start + LANES] = found[at + 2 * rows : at + 3 * rows]
    put_gain(info, ((wg_ref, gate_ref), (wu_ref, up_ref)), gain_ref, gg_ref)


def down_unpack_kernel(info, own_ref, other_ref, down_ref, square_ref):
    half = down_ref.shape[0] // 2
    tiles = down_ref.shape[1] // LANES
    sides = halves(info, own_ref, other_ref)
    for side, found in enumerate(sides):
        for tile in range(tiles):
            down_ref[side * half : (side + 1) * half, tile * LANES : (tile + 1) * LANES] = found[
                tile * half : (tile + 1) * half
            ]
    fill_square(square_ref, sides, tiles * half)


def square_unpack_kernel(gained, info, own_ref, other_ref, *refs):
    weights, gain_ref = refs[: len(gained)], refs[len(gained)]
    out_refs, gg_ref = refs[len(gained) + 1 : -1], refs[-1]
    sides = halves(info, own_ref, other_ref)
    offset = 0
    for out_ref in out_refs:
        fill_square(out_ref, sides, offset)
        offset += out_ref.shape[0] * (out_ref.shape[1] // LANES // 2)
    put_gain(info, [(w, out_refs[at]) for w, at in zip(weights, gained)], gain_ref, gg_ref)


def last_unpack_kernel(info, own_ref, other_ref, *refs):
    table_ref = refs[7]
    square_unpack_kernel((0, 1, 2), info, own_ref, other_ref, *refs[:7], refs[8])
    rows, heads = table_ref.shape
    table_ref[...] = own_ref[own_ref.shape[0] - 16 :, :].astype(f32)[:rows, :heads]


def whole(shape):
    return pl.BlockSpec(shape, lambda *_: (0,) * len(shape))


def call(kernel, name, grid, ins, outs, args, scalars=(), scratch=(), alias=None, more=0):
    grant, time = PLANS[name]
    shapes = [
        pltpu.HBM(out[0], out[1]) if len(out) > 3 else jax.ShapeDtypeStruct(out[0], out[1])
        for out in outs
    ]
    return pl.pallas_call(
        kernel,
        out_shape=shapes,
        grid_spec=pltpu.PrefetchScalarGridSpec(
            num_scalar_prefetch=len(scalars),
            grid=grid,
            in_specs=list(ins),
            out_specs=[out[2] for out in outs],
            scratch_shapes=list(scratch),
        ),
        input_output_aliases=alias or {},
        compiler_params=pltpu.CompilerParams(
            dimension_semantics=("arbitrary",) * len(grid), vmem_limit_bytes=(grant + more) * 2**20
        ),
        cost_estimate=pl.CostEstimate(
            flops=int(time * COVER), bytes_accessed=1, transcendentals=0
        ),
        name=name,
    )(*scalars, *args)


def full(*arrays):
    return [whole(a.shape) for a in arrays]


def bit_orders(bits, last_first):
    low, high = list(range(min(bits, 2))), list(range(2, bits))
    first, second = (low + high[::-1], low[::-1] + high)
    if last_first:
        first, second = (high[::-1] + low, high + low[::-1])
    return [first, second]


def info_table(wide_size, narrow_size, order_pairs):
    bits = wide_size.bit_length() - 1
    rows = []
    for w in range(wide_size):
        for n in range(narrow_size):
            side = n % 2
            row = [w, side, side, w * (narrow_size // 2) + n // 2, n]
            row += [0] * (HEADER - len(row))
            for pair in order_pairs:
                for order in (pair[side], pair[1 - side]):
                    for shard in range(wide_size):
                        apart = shard ^ w
                        slot = [((apart >> bit) & 1) << (bits - 1 - k) for k, bit in enumerate(order)]
                        row.append(sum(slot))
            rows.append(row)
    return np.array(rows, np.int32)


def shards(
    inputs, memory, cotangent, answer_lengths, answer_groups, memory_lengths,
    gain_attn, self_query, self_key, self_value, self_out, bucket_bias_table,
    gain_cross, cross_query, cross_key_matrix, cross_value, cross_out,
    gain_ffn, hidden_gate, hidden_up, hidden_down,
):
    tokens, width = inputs.shape
    answer_lengths, answer_groups = answer_lengths.T, answer_groups.T
    part = memory.shape[0]
    hidden = hidden_gate.shape[1]
    wide_size = lax.axis_size("wide")
    narrow_size = lax.axis_size("narrow")
    wide_index = lax.axis_index("wide")
    narrow_index = lax.axis_index("narrow")
    bits = wide_size.bit_length() - 1
    orders = bit_orders(bits, False)
    orders_last_first = bit_orders(bits, True)
    info = jnp.asarray(info_table(wide_size, narrow_size, (orders, orders_last_first)))
    info = lax.dynamic_slice(
        info, (wide_index * narrow_size + narrow_index, 0), (1, info.shape[1])
    )
    info = info.reshape(-1)
    gains = (gain_attn, gain_cross, gain_ffn)
    turn = [info]

    both = ("wide", "narrow")

    def to_narrow(value, target):
        pairs = [(n, target(n)) for n in range(narrow_size) if target(n) is not None]
        return lax.ppermute(value, "narrow", pairs)

    def to_wide(value, place, order_pair):
        pairs = []
        for w in range(wide_size):
            for n in range(narrow_size):
                partner = w ^ (1 << order_pair[n % 2][place])
                pairs.append((w * narrow_size + n, partner * narrow_size + n))
        return lax.ppermute(value, both, pairs)

    def after(values, *needed):
        return lax.optimization_barrier((tuple(values), needed))[0]

    def now(*values):
        return after(values, *turn) if turn else values

    def run(kernel, name, grid, ins, outs, args, **more):
        found = call(kernel, name, grid, ins, outs, (*now(args[0]), *args[1:]), **more)
        turn[:] = found[:1]
        return found

    class Group:
        def __init__(self, keep, send, order_pair=orders):
            self.pieces, self.place, self.count = [keep], 0, wide_size
            self.order_pair = order_pair
            self.pending = to_narrow(send, lambda n: n ^ 1)

        def total(self, first, count, name="partial_sum"):
            pieces = (*self.pieces, self.pending)
            rows, lanes = pieces[0].shape[1:]
            parts = 2 if count * rows >= 4096 and rows % 32 == 0 else 1
            spec = lambda at: pl.BlockSpec(
                (count, rows // parts, lanes), lambda j: (at, j, 0)
            )
            shape = (count, rows, lanes)
            (found,) = run(
                sum_kernel, name, (parts,), [spec(first)] * len(pieces),
                [(shape, bf16, spec(0))], pieces,
            )
            self.pieces = list(pieces)
            return found

        def step(self, name="partial_sum"):
            self.count //= 2
            sent = self.total(1, self.count, name)
            self.pending = to_wide(sent, self.place, self.order_pair)
            self.place += 1

        def finish(self, name="partial_sum"):
            while self.place < bits:
                self.step()
            total = self.total(0, 1, name)
            step = 2
            while step < narrow_size:
                self.pieces, self.pending = [total], to_narrow(total, lambda n, s=step: n ^ s)
                total = self.total(0, 1)
                step *= 2
            return total[0], to_narrow(total, lambda n: n ^ 1)[0]

    lanes = TOGETHER * PAIR
    steps = (PAIRS // TOGETHER,)
    block = lambda rows: pl.BlockSpec((rows, lanes), lambda j, *_: (0, j))
    out_rows = pl.BlockSpec((lanes, width), lambda j, *_: (j, 0))

    model = (tokens, width)
    square = (width, width)
    in_hbm = pl.BlockSpec(memory_space=pltpu.HBM)
    normed, keys, values, tail, memory_own = run(
        project_kernel, "projections", (1,),
        [whole((width,))] + [in_hbm] * 6,
        [(model, bf16, whole(model))] * 3
        + [((2, REACH, width), bf16, whole((2, REACH, width)))]
        + [((2, part, width), bf16, whole((2, part, width)))],
        (gains[0],)
        + tuple(
            pltpu.with_memory_space_constraint(a, pltpu.HBM)
            for a in (inputs, memory, self_key, self_value, cross_key_matrix, cross_value)
        ),
        scratch=(pltpu.VMEM(model, bf16), pltpu.VMEM((part, width), bf16))
        + (pltpu.VMEM(square, bf16),) * 4
        + (pltpu.SemaphoreType.DMA((6,)),),
    )
    halo = to_narrow(tail, lambda n: n + 1 if n % 2 == 0 else None)
    memory_parts = [memory_own] + [
        to_narrow(memory_own, lambda n, s=shift: (n + s) % narrow_size)
        for shift in range(1, narrow_size)
    ]

    queries, bias = run(
        query_kernel, "queries", (1,),
        [whole(model), in_hbm, whole((HEADS, BUCKETS))],
        [
            (model, bf16, whole(model)),
            ((HEADS * QUERY_BLOCK, WINDOW), f32, whole((HEADS * QUERY_BLOCK, WINDOW))),
        ],
        (normed, pltpu.with_memory_space_constraint(self_query, pltpu.HBM), bucket_bias_table.T),
        scratch=(pltpu.VMEM(square, bf16), pltpu.SemaphoreType.DMA),
    )

    halo_block = pl.BlockSpec((2, REACH, lanes), lambda j, *_: (0, 0, j))
    blocks = tokens // QUERY_BLOCK
    self_probs = pl.BlockSpec(
        (TOGETHER, blocks, 2 * QUERY_BLOCK, WINDOW), lambda j, *_: (j, 0, 0, 0)
    )
    attended, inverse, probs, x1, normed_two, cross_rows = run(
        self_forward_kernel, "self_forward", steps,
        [block(tokens)] * 3 + [halo_block]
        + [pl.BlockSpec((2 * TOGETHER * QUERY_BLOCK, WINDOW), lambda j, *_: (j, 0))]
        + [whole(model), out_rows]
        + full(gains[1], cross_query),
        [
            (model, bf16, block(tokens)),
            (model, f32, block(tokens)),
            ((PAIRS, blocks, 2 * QUERY_BLOCK, WINDOW), bf16, self_probs, "hbm"),
            (model, f32, whole(model)),
            (model, bf16, whole(model)),
            (model, bf16, whole(model)),
        ],
        (queries, keys, values, halo, bias, inputs, self_out, gains[1], cross_query),
        scalars=(info, answer_lengths),
        scratch=(
            pltpu.VMEM((tokens + REACH, lanes), bf16),
            pltpu.VMEM((tokens + REACH, 2 * lanes), bf16),
            pltpu.VMEM((tokens, LANES), jnp.int32),
        ),
    )

    memory_tokens = part * narrow_size
    together = TOGETHER + 1 if memory_tokens <= 2 * CROSS_BLOCK else TOGETHER
    lanes_c = together * PAIR
    block_c = lambda rows: pl.BlockSpec((rows, lanes_c), lambda j, *_: (0, j))
    rows_c = pl.BlockSpec((lanes_c, width), lambda j, *_: (j, 0))
    memory_block = pl.BlockSpec((2, part, lanes_c), lambda j, *_: (0, 0, j))
    cross_blocks = tokens // CROSS_BLOCK
    cross_probs = pl.BlockSpec(
        (together, cross_blocks, 2 * CROSS_BLOCK, memory_tokens), lambda j, *_: (j, 0, 0, 0)
    )
    attended_two, inverse_two, probs_two, x2, normed_three = run(
        functools.partial(cross_forward_kernel, together, narrow_size), "cross_forward", (PAIRS // together,),
        [block_c(tokens), whole(model), rows_c, whole((width,))] + [memory_block] * narrow_size,
        [
            (model, bf16, block_c(tokens)),
            (model, f32, block_c(tokens), "hbm"),
            ((PAIRS, cross_blocks, 2 * CROSS_BLOCK, memory_tokens), bf16, cross_probs, "hbm"),
            (model, f32, whole(model)),
            (model, bf16, whole(model)),
        ],
        (cross_rows, x1, cross_out, gains[2], *memory_parts),
        scalars=(info, answer_lengths, answer_groups, memory_lengths),
        more=memory_tokens // 32 - 8,
        scratch=(
            pltpu.VMEM((memory_tokens, lanes_c), bf16),
            pltpu.VMEM((memory_tokens, 2 * lanes_c), bf16),
            pltpu.VMEM((tokens, LANES), jnp.int32),
            pltpu.VMEM((8, memory_tokens), jnp.int32),
        ),
    )

    probs, inverse_two, probs_two = (
        pltpu.with_memory_space_constraint(a, pltpu.HBM) for a in (probs, inverse_two, probs_two)
    )

    tile = 512
    wide_tile = pl.BlockSpec((width, tile), lambda j, *_: (0, j))
    token_tile = pl.BlockSpec((tokens, tile), lambda j, *_: (0, j))
    hidden_shape = (tokens, hidden)
    unit, grad_gate, grad_up, layer_out, dx2, e2 = run(
        ffn_kernel, "feed_forward", (hidden // tile,),
        [whole(model)] * 3
        + [whole((width,)), wide_tile, wide_tile]
        + [pl.BlockSpec((tile, width), lambda j, *_: (j, 0))],
        [(hidden_shape, bf16, token_tile)] * 3
        + [
            (model, bf16, whole(model)),
            (model, f32, whole(model)),
            (model, bf16, whole(model)),
        ],
        (normed_three, cotangent, x2, gains[2], hidden_gate, hidden_up, hidden_down),
        scratch=(pltpu.VMEM(model, f32), pltpu.VMEM(model, f32)),
    )

    square_rows = width // wide_size * (width // 2 // LANES)
    gate_rows = width // wide_size * (hidden // 2 // LANES)
    down_rows = hidden // wide_size // 2 * (width // LANES)
    step_rows = gate_rows // 2
    gate_side = lambda flip: pl.BlockSpec(
        (tokens, 256), lambda j, info: (0, (info[1] ^ flip) * (hidden // 512) + j)
    )
    half_side = lambda flip: pl.BlockSpec(
        (tokens, width // 2), lambda j, info: (0, info[1] ^ flip)
    )
    anywhere = pl.BlockSpec(memory_space=pl.ANY)

    gate_shape = (wide_size, 2 * gate_rows, LANES)
    step_spec = pl.BlockSpec((wide_size, step_rows, LANES), lambda j, *_: (0, j, 0))
    keep, send = run(
        functools.partial(gate_up_kernel, wide_size), "gate_up_gradient", (hidden // 512,),
        [whole(model), gate_side(0), gate_side(1), gate_side(0), gate_side(1)],
        [(gate_shape, bf16, step_spec)] * 2,
        (normed_three, grad_gate, grad_gate, grad_up, grad_up),
        scalars=(info,),
        scratch=(pltpu.VMEM((width, tokens), bf16),),
    )
    gate_group = Group(keep, send)
    down_shape = (wide_size, down_rows + square_rows, LANES)
    keep, send = run(
        functools.partial(down_kernel, wide_size), "down_gradient", (1,),
        [whole(hidden_shape), whole(model), whole(model), half_side(0), half_side(1)],
        [(down_shape, bf16, whole(down_shape))] * 2,
        (unit, cotangent, attended_two, e2, e2),
        scalars=(info,),
        scratch=(
            pltpu.VMEM((hidden, tokens), bf16),
            pltpu.VMEM((hidden, width // 2), f32),
        ),
    )
    down_group = Group(keep, send, orders_last_first)
    gate_group.step()

    grad_cross_rows, dx1, e1, *memory_grads = run(
        functools.partial(cross_backward_kernel, together, narrow_size), "cross_backward", (PAIRS // together,),
        [whole(model), rows_c, block_c(tokens), block_c(tokens), cross_probs, block_c(tokens)]
        + [block_c(width), whole(model), whole(model), whole((width,))]
        + [memory_block] * narrow_size,
        [
            (model, bf16, block_c(tokens)),
            (model, f32, whole(model)),
            (model, bf16, whole(model)),
        ]
        + [((2, part, width), bf16, memory_block)] * narrow_size,
        (e2, cross_out, attended_two, inverse_two, probs_two, cross_rows, cross_query, x1, dx2)
        + (gains[1], *memory_parts),
        scratch=(
            pltpu.VMEM((memory_tokens, lanes_c), bf16),
            pltpu.VMEM((memory_tokens, lanes_c), bf16),
            pltpu.VMEM((lanes_c, memory_tokens), f32),
            pltpu.VMEM((lanes_c, memory_tokens), f32),
            pltpu.VMEM(model, f32),
        ),
        more=memory_tokens // 32 - 8,
    )
    memory_shares = [memory_grads[0]] + [
        to_narrow(memory_grads[shift], lambda n, s=shift: (n - s) % narrow_size)
        for shift in range(1, narrow_size)
    ]
    down_group.step()
    second_shape = (wide_size, 4 * square_rows, LANES)
    couple = ((normed_two, grad_cross_rows), (attended, e1))
    second_spec = pl.BlockSpec((wide_size, 2 * square_rows, LANES), lambda j, *_: (0, 0, 0))
    keep, send = run(
        functools.partial(square_kernel, wide_size, 2), "square_gradients", (1,),
        [whole(model), half_side(0), half_side(1)] * 2,
        [(second_shape, bf16, second_spec)] * 2,
        [side_of for left, right in couple for side_of in (left, right, right)],
        scalars=(info,),
    )
    memory_spec = pl.BlockSpec((wide_size, square_rows, LANES), lambda j, *_: (0, 2 + j, 0))
    keep, send, memory_grad = run(
        functools.partial(memory_back_kernel, narrow_size, wide_size), "memory_backward", (2,),
        full(memory, cross_key_matrix, cross_value, *memory_shares) + [anywhere] * 2,
        [(second_shape, bf16, memory_spec)] * 2
        + [((part, width), f32, whole((part, width)))],
        (memory, cross_key_matrix, cross_value, *memory_shares, keep, send),
        scalars=(info,),
        scratch=(
            pltpu.VMEM((width, width), f32),
            pltpu.VMEM((part, width), bf16),
            pltpu.VMEM((width, part), bf16),
        ),
        alias={4 + narrow_size: 0, 5 + narrow_size: 1},
    )
    second_group = Group(keep, send)
    gate_group.step()

    tables, carried, parts_of = [], [], PAIRS // TOGETHER
    for index in range(parts_of):
        at = lambda rows, i=index: pl.BlockSpec((rows, lanes), lambda *_: (0, i))
        halo_at = pl.BlockSpec((2, REACH, lanes), lambda *_, i=index: (0, 0, i))
        out_at = pl.BlockSpec((lanes, width), lambda *_, i=index: (i, 0))
        if index == 1:
            second_group.step()
        if index == 2:
            gate_group.step()
            down_group.step()
        *carried, table = run(
            functools.partial(self_backward_kernel, index * TOGETHER),
            "self_backward" if index else "self_backward_first", (1,),
            [whole(model), out_at, at(tokens), at(tokens), in_hbm]
            + [at(tokens)] * 3 + [halo_at] + [anywhere] * len(carried),
            [
                (model, bf16, at(tokens)),
                (model, f32, at(tokens)),
                (model, f32, at(tokens)),
                ((2, REACH, width), bf16, halo_at),
                ((BUCKETS, HEADS), f32, whole((BUCKETS, HEADS))),
            ],
            (e1, self_out, attended, inverse, probs, queries, keys, values, halo, *carried),
            scratch=(
                pltpu.VMEM((tokens + REACH, lanes), bf16),
                pltpu.VMEM((tokens + REACH, lanes), bf16),
                pltpu.VMEM((lanes, tokens + REACH), f32),
                pltpu.VMEM((lanes, tokens + REACH), f32),
                pltpu.VMEM((TOGETHER, 2 * QUERY_BLOCK, 2 * QUERY_BLOCK), f32),
                pltpu.VMEM((16, 2 * QUERY_BLOCK), f32),
                pltpu.VMEM((TOGETHER, blocks, 2 * QUERY_BLOCK, WINDOW), bf16),
                pltpu.SemaphoreType.DMA,
            ),
            alias={9 + i: i for i in range(4)} if index else None,
        )
        tables.append(table)
    grad_queries, grad_keys, grad_values, back = carried
    returned = to_narrow(back, lambda n: n - 1 if n % 2 == 1 else None)
    second_group.step()
    query_shape = (wide_size, square_rows + 16, LANES)
    last_shape = (wide_size, 3 * square_rows + 16, LANES)
    query_keep, query_send = run(
        functools.partial(query_gradient_kernel, wide_size), "query_gradient", (1,),
        [whole(model), half_side(0), half_side(1)] + [whole((BUCKETS, HEADS))] * parts_of,
        [(query_shape, bf16, whole(query_shape))] * 2,
        (normed, grad_queries, grad_queries, *tables),
        scalars=(info,),
    )
    keep, send, keys_low, values_low = run(
        functools.partial(keys_values_kernel, wide_size), "key_value_gradient", (1,),
        full(normed, grad_keys, grad_values, returned, query_keep, query_send),
        [(last_shape, bf16, whole(last_shape))] * 2 + [(model, bf16, whole(model))] * 2,
        (normed, grad_keys, grad_values, returned, query_keep, query_send),
        scalars=(info,),
        scratch=(pltpu.VMEM(square, f32),),
    )
    last_group = Group(keep, send)
    down_group.step("partial_sum_beside")
    gate_group.step()
    second_group.step()
    last_group.step()
    (input_grad,) = run(
        input_kernel, "input_gradient", (1,),
        full(grad_queries, keys_low, values_low)
        + full(self_query, self_key, self_value, inputs, dx1, gains[0]),
        [(model, f32, whole(model))],
        (grad_queries, keys_low, values_low)
        + (self_query, self_key, self_value, inputs, dx1, gains[0]),
    )

    square_out = ((width // wide_size, width), f32, whole((width // wide_size, width)))
    gate_out = ((width // wide_size, hidden), f32, whole((width // wide_size, hidden)))
    down_out = ((hidden // wide_size, width), f32, whole((hidden // wide_size, width)))
    size = width // wide_size
    gain_out = ((size,), f32, whole((size,)))
    own_rows = lambda columns: pl.BlockSpec((size, columns), lambda j, info: (info[0], 0))
    gate_own, gate_other = gate_group.finish()
    last_group.step()
    grad_gate_w, grad_up_w, grad_gain_ffn = run(
        gate_unpack_kernel, "gate_outputs", (1,),
        full(gate_own, gate_other) + [own_rows(hidden)] * 2 + [whole((width,))],
        [gate_out] * 2 + [gain_out],
        (gate_own, gate_other, hidden_gate, hidden_up, gain_ffn), scalars=(info,),
    )
    last_group.step("partial_sum_late")
    down_group.step("partial_sum_late")
    second_group.step("partial_sum_late")
    down_own, down_other = down_group.finish("partial_sum_late")
    second_own, second_other = second_group.finish("partial_sum_late")
    grad_down_w, grad_cross_out = run(
        down_unpack_kernel, "down_outputs", (1,), full(down_own, down_other),
        [down_out, square_out], (down_own, down_other), scalars=(info,),
    )
    last_group.step("partial_sum_late")
    (
        grad_cross_query, grad_self_out, grad_cross_key, grad_cross_value, grad_gain_cross,
    ) = run(
        functools.partial(square_unpack_kernel, (0,)), "second_outputs", (1,),
        full(second_own, second_other) + [own_rows(width), whole((width,))],
        [square_out] * 4 + [gain_out],
        (second_own, second_other, cross_query, gain_cross), scalars=(info,),
    )
    last_own, last_other = last_group.finish("partial_sum_late")
    table_out = ((BUCKETS // wide_size, HEADS), f32, whole((BUCKETS // wide_size, HEADS)))
    grad_self_key, grad_self_value, grad_self_query, grad_table, grad_gain_attn = run(
        last_unpack_kernel, "last_outputs", (1,),
        full(last_own, last_other) + [own_rows(width)] * 3 + [whole((width,))],
        [square_out] * 3 + [table_out, gain_out],
        (last_own, last_other, self_key, self_value, self_query, gain_attn), scalars=(info,),
    )
    return (
        layer_out,
        input_grad,
        memory_grad,
        grad_gain_attn,
        grad_self_query,
        grad_self_key,
        grad_self_value,
        grad_self_out,
        grad_table,
        grad_gain_cross,
        grad_cross_query,
        grad_cross_key,
        grad_cross_value,
        grad_cross_out,
        grad_gain_ffn,
        grad_gate_w,
        grad_up_w,
        grad_down_w,
    )


def solution(mesh):
    rows = P(("wide", "narrow"), None)
    vector, matrix = P("wide"), P("wide", None)
    return jax.shard_map(
        shards,
        mesh=mesh,
        in_specs=(rows,) * 3 + (P(),) * 18,
        out_specs=(rows,) * 3
        + (vector,)
        + (matrix,) * 5
        + (vector,)
        + (matrix,) * 4
        + (vector,)
        + (matrix,) * 3,
        check_vma=False,
    )
```

```python
import functools
import math

import jax
import jax.numpy as jnp
import numpy as np
from jax import lax
from jax.experimental import pallas as pl
from jax.experimental.pallas import tpu as pltpu
from jax.sharding import PartitionSpec as P

HEADS = 12
HEAD_DIM = 64
BUCKETS = 32
MAX_DIST = 128
ANSWERS = 8
GROUPS = 16
PAIR = 2 * HEAD_DIM
PAIRS = HEADS // 2
REACH = 256
QUERY_BLOCK = 128
WINDOW = REACH + QUERY_BLOCK
CROSS_BLOCK = 256
LANES = 128
HEADER = 8
TOGETHER = 2
PLANS = dict(
    projections=(14, 5.0),
    queries=(8, 3.0),
    self_forward=(20, 12.0),
    cross_forward=(16, 10.5),
    feed_forward=(34, 15.0),
    gate_up_gradient=(14, 6.0),
    down_gradient=(16, 4.4),
    cross_backward=(20, 12.0),
    square_gradients=(16, 2.0),
    memory_backward=(14, 3.6),
    self_backward_first=(20, 30.0),
    self_backward=(20, 7.0),
    query_gradient=(8, 9.0),
    key_value_gradient=(14, 2.4),
    input_gradient=(16, 3.6),
    partial_sum=(12, 1.0),
    partial_sum_late=(12, 0.0),
    partial_sum_beside=(12, 20.0),
    gate_outputs=(6, 0.0),
    down_outputs=(6, 0.0),
    second_outputs=(6, 0.0),
    last_outputs=(6, 0.0),
)
COVER = 1.15e9

epsilon = 1e-06
neg_big = -1e30
f32 = jnp.float32
bf16 = jnp.bfloat16


def mm(left, right):
    return jnp.dot(left, right, preferred_element_type=f32)


def mm_t(left, right):
    return lax.dot_general(left, right, (((1,), (1,)), ((), ())), preferred_element_type=f32)


def rms(values, gain_row):
    factor = lax.rsqrt(jnp.mean(values * values, axis=-1, keepdims=True) + epsilon)
    return values * factor * gain_row


def rms_back(values, gain_row, grad):
    factor = lax.rsqrt(jnp.mean(values * values, axis=-1, keepdims=True) + epsilon)
    unit = values * factor
    scaled = grad * gain_row
    center = jnp.mean(scaled * unit, axis=-1, keepdims=True)
    return factor * (scaled - unit * center)


def bucket_of(distance):
    exact_count = BUCKETS // 2
    log_count = BUCKETS - exact_count
    near_part = jnp.minimum(jnp.maximum(distance, 0), exact_count)
    far_part = jnp.zeros_like(distance)
    for level_index in range(1, log_count):
        edge = math.ceil(exact_count * (MAX_DIST / exact_count) ** (level_index / log_count))
        far_part = far_part + (distance >= edge).astype(jnp.int32)
    return near_part + far_part


def gain_of(ref):
    return ref[...].astype(f32).reshape(1, ref.shape[0])


def iota(shape, axis):
    return lax.broadcasted_iota(jnp.int32, shape, axis)


def low_lanes(shape):
    return iota(shape, len(shape) - 1) < HEAD_DIM


def stack_heads(rows):
    low = low_lanes(rows.shape)
    zero = jnp.zeros_like(rows)
    return jnp.concatenate([jnp.where(low, rows, zero), jnp.where(low, zero, rows)], axis=0)


def stack_heads_t(columns):
    low = iota(columns.shape, 0) < HEAD_DIM
    zero = jnp.zeros_like(columns)
    return jnp.concatenate([jnp.where(low, columns, zero), jnp.where(low, zero, columns)], axis=1)


def join_heads(stacked):
    half = stacked.shape[0] // 2
    return jnp.where(low_lanes((half, PAIR)), stacked[:half], stacked[half:])


def offset_bucket():
    lane = iota((1, 4 * QUERY_BLOCK), 1)
    distance = jnp.where(lane < WINDOW, REACH - lane, REACH + 4 * QUERY_BLOCK - lane)
    chosen = iota((BUCKETS, 4 * QUERY_BLOCK), 0) == bucket_of(distance)
    return distance, chosen


def answer_ends(lengths, row):
    total, ends = lengths[0, row], []
    for index in range(1, ANSWERS):
        ends.append(total)
        total = total + lengths[index, row]
    return ends


def project_kernel(
    gain_ref, x_hbm, memory_hbm, wk_hbm, wv_hbm, wck_hbm, wcv_hbm,
    h_ref, k_ref, v_ref, tail_ref, memory_out,
    x_ref, memory_ref, wk_ref, wv_ref, wck_ref, wcv_ref, sems,
):
    copies = [
        pltpu.make_async_copy(source, target, sems.at[index])
        for index, (source, target) in enumerate(
            (
                (x_hbm, x_ref),
                (memory_hbm, memory_ref),
                (wck_hbm, wck_ref),
                (wcv_hbm, wcv_ref),
                (wk_hbm, wk_ref),
                (wv_hbm, wv_ref),
            )
        )
    ]
    for copy in copies:
        copy.start()
    copies[0].wait()
    h_ref[...] = rms(x_ref[...].astype(f32), gain_of(gain_ref)).astype(bf16)
    copies[1].wait()
    copies[2].wait()
    memory_out[0] = mm(memory_ref[...], wck_ref[...]).astype(bf16)
    copies[3].wait()
    memory_out[1] = mm(memory_ref[...], wcv_ref[...]).astype(bf16)
    tokens = h_ref.shape[0]
    copies[4].wait()
    k_ref[...] = mm(h_ref[...], wk_ref[...]).astype(bf16)
    tail_ref[0] = k_ref[tokens - REACH :, :]
    copies[5].wait()
    v_ref[...] = mm(h_ref[...], wv_ref[...]).astype(bf16)
    tail_ref[1] = v_ref[tokens - REACH :, :]


def query_kernel(h_ref, wq_hbm, table_ref, q_ref, bias_ref, wq_ref, sem):
    copy = pltpu.make_async_copy(wq_hbm, wq_ref, sem)
    copy.start()
    distance, chosen = offset_bucket()
    base = jnp.where(distance < 0, neg_big, mm(table_ref[...], chosen.astype(bf16)))
    for head in range(HEADS):
        spread = jnp.broadcast_to(base[head : head + 1], (QUERY_BLOCK, 4 * QUERY_BLOCK))
        skewed = pltpu.roll(spread, 0, 1, stride=1, stride_axis=0)
        bias_ref[head * QUERY_BLOCK : (head + 1) * QUERY_BLOCK, :] = skewed[:, :WINDOW]
    copy.wait()
    q_ref[...] = mm(h_ref[...], wq_ref[...]).astype(bf16)


def self_forward_kernel(
    info, lengths,
    q_ref, k_ref, v_ref, halo_ref, bias, x_ref, wo_ref, gain_ref, wq_ref,
    o_ref, inv_ref, e_ref, x1_ref, h2_ref, qc_ref,
    keys, values, reach,
):
    step = pl.program_id(0)
    tokens = q_ref.shape[0]

    @pl.when(step == 0)
    def _():
        place = info[2] * tokens + iota((tokens, LANES), 0)
        start = jnp.zeros_like(place)
        for end in answer_ends(lengths, info[3]):
            start = jnp.where(place >= end, end, start)
        reach[...] = place - start
        for p in range(TOGETHER):
            ones = slice((2 * p + 1) * PAIR, 2 * (p + 1) * PAIR)
            values[:, ones] = jnp.ones((values.shape[0], PAIR), bf16)
        x1_ref[...] = x_ref[...].astype(f32)

    keys[0:REACH] = halo_ref[0]
    keys[REACH:] = k_ref[...]
    pairs = [slice(p * PAIR, (p + 1) * PAIR) for p in range(TOGETHER)]
    valued = [slice(2 * p * PAIR, 2 * (p + 1) * PAIR) for p in range(TOGETHER)]
    for pair, both in zip(pairs, valued):
        own = slice(both.start, both.start + PAIR)
        values[0:REACH, own] = halo_ref[1, :, pair]
        values[REACH:, own] = v_ref[:, pair]

    distance = REACH + iota((QUERY_BLOCK, WINDOW), 0) - iota((QUERY_BLOCK, WINDOW), 1)
    distance = jnp.concatenate([distance, distance], axis=0)
    items = [(b, p) for p in range(TOGETHER) for b in range(tokens // QUERY_BLOCK)]
    rows = [slice(b * QUERY_BLOCK, (b + 1) * QUERY_BLOCK) for b, _ in items]
    windows = [slice(b * QUERY_BLOCK, b * QUERY_BLOCK + WINDOW) for b, _ in items]
    scores = [
        mm_t(stack_heads(q_ref[r, pairs[p]]), keys[w, pairs[p]])
        for (_, p), r, w in zip(items, rows, windows)
    ]
    weights = []
    for (block, p), r, found in zip(items, rows, scores):
        own_reach = reach[r, 0:1]
        own_reach = jnp.concatenate([own_reach, own_reach], axis=0)
        shifted = found + bias[2 * p * QUERY_BLOCK : 2 * (p + 1) * QUERY_BLOCK, :]
        masked = jnp.where(distance <= own_reach, shifted, neg_big)
        top = jnp.max(masked, axis=-1, keepdims=True)
        weights.append(jnp.exp(masked - top).astype(bf16))
        e_ref[p, block] = weights[-1]
    mixed = [mm(e, values[w, valued[p]]) for (_, p), e, w in zip(items, weights, windows)]
    for (_, p), r, found in zip(items, rows, mixed):
        inverse = 1.0 / found[:, PAIR:]
        o_ref[r, pairs[p]] = join_heads(found[:, :PAIR] * inverse).astype(bf16)
        inv_ref[r, pairs[p]] = join_heads(inverse)
    x1_ref[...] += mm(o_ref[...], wo_ref[...])

    @pl.when(step == pl.num_programs(0) - 1)
    def _():
        h2_ref[...] = rms(x1_ref[...], gain_of(gain_ref)).astype(bf16)
        qc_ref[...] = mm(h2_ref[...], wq_ref[...]).astype(bf16)


def cross_forward_kernel(together, chunks, info, lengths, groups, bounds, *refs):
    q_ref, x1_ref, wo_ref, gain_ref = refs[:4]
    kv_refs = refs[4 : 4 + chunks]
    o_ref, inv_ref, e_ref, x2_ref, h3_ref = refs[4 + chunks : 9 + chunks]
    keys, values, query_group, key_group = refs[9 + chunks :]
    step = pl.program_id(0)
    tokens = q_ref.shape[0]
    part = kv_refs[0].shape[1]

    @pl.when(step == 0)
    def _():
        place = info[2] * tokens + iota((tokens, LANES), 0)
        group = jnp.zeros_like(place) + groups[0, info[3]]
        for index, end in enumerate(answer_ends(lengths, info[3])):
            group = jnp.where(place >= end, groups[index + 1, info[3]], group)
        query_group[...] = group
        total, ends = bounds[info[0], 0], []
        for index in range(1, GROUPS):
            ends.append(total)
            total = total + bounds[info[0], index]
        for chunk in range(chunks):
            owner = lax.rem(info[4] + chunks - chunk, chunks)
            token = owner * part + iota((8, part), 1)
            found = jnp.zeros_like(token)
            for end in ends:
                found = found + (token >= end).astype(jnp.int32)
            key_group[:, chunk * part : (chunk + 1) * part] = found
        for p in range(together):
            ones = slice((2 * p + 1) * PAIR, 2 * (p + 1) * PAIR)
            values[:, ones] = jnp.ones((values.shape[0], PAIR), bf16)
        x2_ref[...] = x1_ref[...]

    pairs = [slice(p * PAIR, (p + 1) * PAIR) for p in range(together)]
    valued = [slice(2 * p * PAIR, 2 * (p + 1) * PAIR) for p in range(together)]
    for chunk in range(chunks):
        at = slice(chunk * part, (chunk + 1) * part)
        keys[at] = kv_refs[chunk][0]
        for pair, both in zip(pairs, valued):
            values[at, both.start : both.start + PAIR] = kv_refs[chunk][1, :, pair]
    items = [(b, p) for p in range(together) for b in range(tokens // CROSS_BLOCK)]
    rows = [slice(b * CROSS_BLOCK, (b + 1) * CROSS_BLOCK) for b, _ in items]
    scores = [
        mm_t(stack_heads(q_ref[r, pairs[p]]), keys[:, pairs[p]]) for (_, p), r in zip(items, rows)
    ]
    weights = []
    for (block, p), r, found in zip(items, rows, scores):
        own_group = query_group[r, 0:1]
        own_group = jnp.concatenate([own_group, own_group], axis=0)
        masked = jnp.where(own_group == key_group[0:1, :], found, neg_big)
        top = jnp.max(masked, axis=-1, keepdims=True)
        weights.append(jnp.exp(masked - top).astype(bf16))
        e_ref[p, block] = weights[-1]
    mixed = [mm(e, values[:, valued[p]]) for (_, p), e in zip(items, weights)]
    for (_, p), r, found in zip(items, rows, mixed):
        inverse = 1.0 / found[:, PAIR:]
        o_ref[r, pairs[p]] = join_heads(found[:, :PAIR] * inverse).astype(bf16)
        inv_ref[r, pairs[p]] = join_heads(inverse)
    x2_ref[...] += mm(o_ref[...], wo_ref[...])

    @pl.when(step == pl.num_programs(0) - 1)
    def _():
        h3_ref[...] = rms(x2_ref[...], gain_of(gain_ref)).astype(bf16)


def ffn_kernel(
    h_ref, c_ref, x2_ref, gain_ref, wg_ref, wu_ref, wd_ref,
    u_ref, dga_ref, dgb_ref, out_ref, dx_ref, e_ref,
    total, dh,
):
    step = pl.program_id(0)
    root = math.sqrt(2.0 / math.pi)
    gate = mm(h_ref[...], wg_ref[...])
    up = mm(h_ref[...], wu_ref[...])
    du = mm_t(c_ref[...], wd_ref[...])
    square = gate * gate
    bent = jnp.tanh(gate * (root + (0.044715 * root) * square))
    share = 0.5 + 0.5 * bent
    active = gate * share
    bend = (0.5 - 0.5 * bent) * (2.0 * root + (6 * 0.044715 * root) * square)
    slope = share + active * bend
    u_ref[...] = (active * up).astype(bf16)
    dgb_ref[...] = (du * active).astype(bf16)
    dga_ref[...] = (du * up * slope).astype(bf16)
    out_part = mm(u_ref[...], wd_ref[...])
    dh_part = mm_t(dga_ref[...], wg_ref[...]) + mm_t(dgb_ref[...], wu_ref[...])

    @pl.when(step == 0)
    def _():
        total[...] = x2_ref[...] + out_part
        dh[...] = dh_part

    @pl.when(step > 0)
    def _():
        total[...] += out_part
        dh[...] += dh_part

    @pl.when(step == pl.num_programs(0) - 1)
    def _():
        out_ref[...] = total[...].astype(bf16)
        back = rms_back(x2_ref[...], gain_of(gain_ref), dh[...])
        dx_ref[...] = c_ref[...].astype(f32) + back
        e_ref[...] = dx_ref[...].astype(bf16)


def cross_backward_kernel(together, chunks, *refs):
    e2_ref, wo_ref, o_ref, inv_ref, p_ref, q_ref, wq_ref, x1_ref, dx2_ref, gain_ref = refs[:10]
    kv_refs = refs[10 : 10 + chunks]
    dq_ref, dx_ref, e1_ref = refs[10 + chunks : 13 + chunks]
    dkv_refs = refs[13 + chunks : 13 + 2 * chunks]
    keys, values, dk, dv, dh = refs[13 + 2 * chunks :]
    step = pl.program_id(0)
    tokens = q_ref.shape[0]
    part = kv_refs[0].shape[1]

    for chunk in range(chunks):
        keys[chunk * part : (chunk + 1) * part] = kv_refs[chunk][0]
        values[chunk * part : (chunk + 1) * part] = kv_refs[chunk][1]
    grad = mm_t(e2_ref[...], wo_ref[...]).astype(bf16).astype(f32)
    grad = (grad * inv_ref[...]).astype(bf16)
    query_t = q_ref[...].T
    grad_t = grad.T
    pairs = [slice(p * PAIR, (p + 1) * PAIR) for p in range(together)]
    items = [(b, p) for p in range(together) for b in range(tokens // CROSS_BLOCK)]
    rows = [slice(b * CROSS_BLOCK, (b + 1) * CROSS_BLOCK) for b, _ in items]
    grad_probs = [
        mm_t(stack_heads(grad[r, pairs[p]]), values[:, pairs[p]]) for (_, p), r in zip(items, rows)
    ]
    for pair in range(together):
        dv[pairs[pair]] = sum(
            mm(stack_heads_t(grad_t[pairs[p], r]), p_ref[p, b])
            for (b, p), r in zip(items, rows)
            if p == pair
        )
    scored = []
    for (block, p), r, found in zip(items, rows, grad_probs):
        weighed = grad[r, pairs[p]].astype(f32) * o_ref[r, pairs[p]].astype(f32)
        center = jnp.sum(stack_heads(weighed), axis=-1, keepdims=True)
        scored.append((p_ref[p, block].astype(f32) * (found - center)).astype(bf16))
    for (_, p), r, found in zip(items, rows, scored):
        dq_ref[r, pairs[p]] = join_heads(mm(found, keys[:, pairs[p]])).astype(bf16)
    for pair in range(together):
        dk[pairs[pair]] = sum(
            mm(stack_heads_t(query_t[pairs[p], r]), found)
            for (_, p), r, found in zip(items, rows, scored)
            if p == pair
        )
    dk_rows = dk[...].T.astype(bf16)
    dv_rows = dv[...].T.astype(bf16)
    for chunk in range(chunks):
        dkv_refs[chunk][0] = dk_rows[chunk * part : (chunk + 1) * part]
        dkv_refs[chunk][1] = dv_rows[chunk * part : (chunk + 1) * part]
    dh_part = mm_t(dq_ref[...], wq_ref[...])

    @pl.when(step == 0)
    def _():
        dh[...] = dh_part

    @pl.when(step > 0)
    def _():
        dh[...] += dh_part

    @pl.when(step == pl.num_programs(0) - 1)
    def _():
        back = rms_back(x1_ref[...], gain_of(gain_ref), dh[...])
        dx_ref[...] = dx2_ref[...] + back
        e1_ref[...] = dx_ref[...].astype(bf16)


def self_backward_kernel(
    begin, e1_ref, wo_ref, o_ref, inv_ref, p_hbm, q_ref, k_ref, v_ref, halo_ref, *refs
):
    dq_ref, dk_ref, dv_ref, back_ref, table_ref = refs[-13:-8]
    keys, values, dk, dv, by_offset, offsets, p_ref, sem = refs[-8:]
    copy = pltpu.make_async_copy(p_hbm.at[pl.ds(begin, TOGETHER)], p_ref, sem)
    copy.start()
    tokens = q_ref.shape[0]
    keys[0:REACH] = halo_ref[0]
    keys[REACH:] = k_ref[...]
    values[0:REACH] = halo_ref[1]
    values[REACH:] = v_ref[...]
    grad = mm_t(e1_ref[...], wo_ref[...]).astype(bf16).astype(f32)
    grad = (grad * inv_ref[...]).astype(bf16)
    query_t = q_ref[...].T
    grad_t = grad.T
    dk[...] = jnp.zeros_like(dk)
    dv[...] = jnp.zeros_like(dv)
    offsets[...] = jnp.zeros_like(offsets)
    pairs = [slice(p * PAIR, (p + 1) * PAIR) for p in range(TOGETHER)]
    items = [(b, p) for p in range(TOGETHER) for b in range(tokens // QUERY_BLOCK)]
    rows = [slice(b * QUERY_BLOCK, (b + 1) * QUERY_BLOCK) for b, _ in items]
    windows = [slice(b * QUERY_BLOCK, b * QUERY_BLOCK + WINDOW) for b, _ in items]
    grad_probs = [
        mm_t(stack_heads(grad[r, pairs[p]]), values[w, pairs[p]])
        for (_, p), r, w in zip(items, rows, windows)
    ]
    centers = []
    for (_, p), r in zip(items, rows):
        weighed = grad[r, pairs[p]].astype(f32) * o_ref[r, pairs[p]].astype(f32)
        centers.append(jnp.sum(stack_heads(weighed), axis=-1, keepdims=True))
    copy.wait()
    for (block, p), r, w in zip(items, rows, windows):
        dv[pairs[p], w] += mm(stack_heads_t(grad_t[pairs[p], r]), p_ref[p, block])
    scored = []
    for (block, p), found, center in zip(items, grad_probs, centers):
        exact = p_ref[p, block].astype(f32) * (found - center)
        near = exact[:, QUERY_BLOCK:]
        by_offset[p] = near if block == 0 else by_offset[p] + near
        scored.append(exact.astype(bf16))
    for (_, p), r, w, found in zip(items, rows, windows, scored):
        dq_ref[r, pairs[p]] = join_heads(mm(found, keys[w, pairs[p]])).astype(bf16)
        dk[pairs[p], w] += mm(stack_heads_t(query_t[pairs[p], r]), found)
    dk_rows = dk[...].T
    dv_rows = dv[...].T
    back_ref[0] = dk_rows[:REACH].astype(bf16)
    back_ref[1] = dv_rows[:REACH].astype(bf16)
    dk_ref[...] = dk_rows[REACH:]
    dv_ref[...] = dv_rows[REACH:]

    row_index = iota((QUERY_BLOCK, 2 * QUERY_BLOCK), 0)
    for p in range(TOGETHER):
        for head in range(2):
            tile = by_offset[p, head * QUERY_BLOCK : (head + 1) * QUERY_BLOCK, :]
            for bit in range(QUERY_BLOCK.bit_length() - 1):
                moved = pltpu.roll(tile, 2 * QUERY_BLOCK - (1 << bit), 1)
                tile = jnp.where((row_index >> bit) & 1 == 1, moved, tile)
            at = 2 * (begin + p) + head
            offsets[at : at + 1, :] = jnp.sum(tile, axis=0, keepdims=True)

    lane = iota((1, 2 * QUERY_BLOCK), 1)
    far = BUCKETS - 1
    bucket = bucket_of(QUERY_BLOCK - lane)
    row = iota((BUCKETS, 2 * QUERY_BLOCK), 0)
    inside = (lane <= QUERY_BLOCK) & (bucket < far)
    sign = jnp.where(row == far, -1.0, jnp.where(row == bucket, 1.0, 0.0))
    table_ref[...] = lax.dot_general(
        jnp.where(inside, sign, 0.0), offsets[0:HEADS], (((1,), (1,)), ((), ())),
        precision=lax.Precision.HIGHEST, preferred_element_type=f32,
    )


def input_kernel(
    dq_ref, dkl_ref, dvl_ref, wq_ref, wk_ref, wv_ref, x_ref, dx1_ref, gain_ref, dx_ref
):
    dh = (
        mm_t(dq_ref[...], wq_ref[...])
        + mm_t(dkl_ref[...], wk_ref[...])
        + mm_t(dvl_ref[...], wv_ref[...])
    )
    back = rms_back(x_ref[...].astype(f32), gain_of(gain_ref), dh)
    dx_ref[...] = dx1_ref[...] + back


def put_tiles(out_ref, info, side, offset, found, shards):
    rows = found.shape[0] // shards
    first = HEADER + side * shards
    for shard in range(shards):
        for tile in range(found.shape[1] // LANES):
            piece = found[
                shard * rows : (shard + 1) * rows, tile * LANES : (tile + 1) * LANES
            ].astype(bf16)
            out_ref[
                info[first + shard], offset + tile * rows : offset + (tile + 1) * rows, :
            ] = piece


def gate_up_kernel(shards, info, h_ref, gk_ref, gs_ref, uk_ref, us_ref, keep_ref, send_ref, h_t):
    @pl.when(pl.program_id(0) == 0)
    def _():
        h_t[...] = h_ref[...].T

    half = keep_ref.shape[1] // 2
    put_tiles(keep_ref, info, 0, 0, mm(h_t[...], gk_ref[...]), shards)
    put_tiles(send_ref, info, 1, 0, mm(h_t[...], gs_ref[...]), shards)
    put_tiles(keep_ref, info, 0, half, mm(h_t[...], uk_ref[...]), shards)
    put_tiles(send_ref, info, 1, half, mm(h_t[...], us_ref[...]), shards)


def down_kernel(
    shards, info, u_ref, c_ref, left_ref, own_ref, other_ref, keep_ref, send_ref, u_t, found
):
    u_t[...] = u_ref[...].T
    rows = found.shape[0] // shards // 2
    columns = found.shape[1]
    tiles = columns // LANES
    for begin in range(0, c_ref.shape[1], columns):
        found[...] = mm(u_t[...], c_ref[:, begin : begin + columns])
        offset = begin // LANES * rows
        for shard in range(shards):
            for which, out_ref in enumerate((keep_ref, send_ref)):
                slot = info[HEADER + (2 + which) * shards + shard]
                start = pl.multiple_of((2 * shard + (info[1] ^ which)) * rows, rows)
                piece = found[pl.ds(start, rows), :].astype(bf16)
                for tile in range(tiles):
                    at = offset + tile * rows
                    lane = tile * LANES
                    out_ref[slot, at : at + rows, :] = piece[:, lane : lane + LANES]
    left = left_ref[...].T
    offset = c_ref.shape[1] // LANES * rows
    put_tiles(keep_ref, info, 2, offset, mm(left, own_ref[...]), shards)
    put_tiles(send_ref, info, 3, offset, mm(left, other_ref[...]), shards)


def square_kernel(shards, count, info, *refs):
    sides = refs[: 3 * count]
    keep_ref, send_ref = refs[3 * count :]
    rows = keep_ref.shape[1] // count
    for index in range(count):
        left_ref, own_ref, other_ref = sides[3 * index : 3 * index + 3]
        left = left_ref[...].T
        put_tiles(keep_ref, info, 0, index * rows, mm(left, own_ref[...]), shards)
        put_tiles(send_ref, info, 1, index * rows, mm(left, other_ref[...]), shards)


def memory_back_kernel(chunks, shards, info, memory_ref, wk_ref, wv_ref, *refs):
    parts = refs[:chunks]
    keep_ref, send_ref, dm_ref, found, grad, memory_t = refs[chunks + 2 :]
    columns = found.shape[1] // 2

    def add(which, weight_ref):
        total = parts[0][which].astype(f32)
        for other in parts[1:]:
            total = total + other[which].astype(f32)
        grad[...] = total.astype(bf16)
        share = mm_t(grad[...], weight_ref[...])
        dm_ref[...] = share if which == 0 else dm_ref[...] + share

    @pl.when(pl.program_id(0) == 0)
    def _():
        memory_t[...] = memory_ref[...].T
        add(0, wk_ref)

    @pl.when(pl.program_id(0) == 1)
    def _():
        add(1, wv_ref)

    found[...] = mm(memory_t[...], grad[...])
    for flip, out_ref in enumerate((keep_ref, send_ref)):
        start = pl.multiple_of((info[1] ^ flip) * columns, LANES)
        put_tiles(out_ref, info, flip, 0, found[:, pl.ds(start, columns)], shards)


def keys_values_kernel(
    shards, info, h_ref, dk_ref, dv_ref, ret_ref, keep_in, send_in,
    keep_ref, send_ref, dkl_ref, dvl_ref, found,
):
    head = h_ref.shape[0] - REACH
    rows = (keep_ref.shape[1] - keep_in.shape[1]) // 2
    keep_ref[:, 2 * rows :, :] = keep_in[...]
    send_ref[:, 2 * rows :, :] = send_in[...]
    columns = found.shape[1] // 2
    left = h_ref[...].T
    for which, own, low in ((0, dk_ref, dkl_ref), (1, dv_ref, dvl_ref)):
        low[:head, :] = own[:head, :].astype(bf16)
        low[head:, :] = (own[head:, :] + ret_ref[which].astype(f32)).astype(bf16)
        found[...] = mm(left, low[...])
        for flip, out_ref in enumerate((keep_ref, send_ref)):
            start = pl.multiple_of((info[1] ^ flip) * columns, LANES)
            half = found[:, pl.ds(start, columns)]
            put_tiles(out_ref, info, flip, which * rows, half, shards)


def query_gradient_kernel(
    shards, info, h_ref, own_ref, other_ref, *refs
):
    *tables, keep_ref, send_ref = refs
    left = h_ref[...].T
    rows = keep_ref.shape[1] - 16
    put_tiles(keep_ref, info, 0, 0, mm(left, own_ref[...]), shards)
    put_tiles(send_ref, info, 1, 0, mm(left, other_ref[...]), shards)
    count = BUCKETS // shards
    table = jnp.concatenate(
        [sum(ref[...] for ref in tables), jnp.zeros((BUCKETS, LANES - HEADS), f32)], axis=1
    )
    for index in range(shards):
        piece = table[index * count : (index + 1) * count]
        tile = jnp.concatenate([piece, jnp.zeros((16 - count, LANES), f32)], axis=0).astype(bf16)
        for which, out_ref in enumerate((keep_ref, send_ref)):
            out_ref[info[HEADER + which * shards + index], rows:] = tile


def sum_kernel(*refs):
    total = refs[0][...].astype(f32)
    for ref in refs[1:-1]:
        total = total + ref[...].astype(f32)
    refs[-1][...] = total.astype(bf16)


def halves(info, own_ref, other_ref):
    own, other = own_ref[...].astype(f32), other_ref[...].astype(f32)
    first = info[1] == 0
    return jnp.where(first, own, other), jnp.where(first, other, own)


def fill_square(out_ref, sides, offset):
    rows, columns = out_ref.shape
    count = columns // LANES // 2
    for side, found in enumerate(sides):
        for tile in range(count):
            start = (side * count + tile) * LANES
            out_ref[:, start : start + LANES] = found[
                offset + tile * rows : offset + (tile + 1) * rows
            ]


def put_gain(info, pairs, gain_ref, out_ref):
    rows, width = pairs[0][0].shape[0], gain_ref.shape[0]
    total = None
    for weight_ref, grad_ref in pairs:
        share = jnp.sum(weight_ref[...].astype(f32) * grad_ref[...], axis=1, keepdims=True)
        total = share if total is None else total + share
    here = iota((rows, width), 1) == info[0] * rows + iota((rows, width), 0)
    gain = jnp.sum(jnp.where(here, gain_of(gain_ref), 0.0), axis=1, keepdims=True)
    spread = jnp.where(iota((rows, LANES), 0) == iota((rows, LANES), 1), total / gain, 0.0)
    out_ref[...] = jnp.sum(spread, axis=0)[:rows]


def gate_unpack_kernel(
    info, own_ref, other_ref, wg_ref, wu_ref, gain_ref, gate_ref, up_ref, gg_ref
):
    rows, columns = gate_ref.shape
    count = columns // LANES // 2
    for side, found in enumerate(halves(info, own_ref, other_ref)):
        for tile in range(count):
            start = (side * count + tile) * LANES
            at = (tile // 2) * 4 * rows + (tile % 2) * rows
            gate_ref[:, start : start + LANES] = found[at : at + rows]
            up_ref[:, start : start + LANES] = found[at + 2 * rows : at + 3 * rows]
    put_gain(info, ((wg_ref, gate_ref), (wu_ref, up_ref)), gain_ref, gg_ref)


def down_unpack_kernel(info, own_ref, other_ref, down_ref, square_ref):
    half = down_ref.shape[0] // 2
    tiles = down_ref.shape[1] // LANES
    sides = halves(info, own_ref, other_ref)
    for side, found in enumerate(sides):
        for tile in range(tiles):
            down_ref[side * half : (side + 1) * half, tile * LANES : (tile + 1) * LANES] = found[
                tile * half : (tile + 1) * half
            ]
    fill_square(square_ref, sides, tiles * half)


def square_unpack_kernel(gained, info, own_ref, other_ref, *refs):
    weights, gain_ref = refs[: len(gained)], refs[len(gained)]
    out_refs, gg_ref = refs[len(gained) + 1 : -1], refs[-1]
    sides = halves(info, own_ref, other_ref)
    offset = 0
    for out_ref in out_refs:
        fill_square(out_ref, sides, offset)
        offset += out_ref.shape[0] * (out_ref.shape[1] // LANES // 2)
    put_gain(info, [(w, out_refs[at]) for w, at in zip(weights, gained)], gain_ref, gg_ref)


def last_unpack_kernel(info, own_ref, other_ref, *refs):
    table_ref = refs[7]
    square_unpack_kernel((0, 1, 2), info, own_ref, other_ref, *refs[:7], refs[8])
    rows, heads = table_ref.shape
    table_ref[...] = own_ref[own_ref.shape[0] - 16 :, :].astype(f32)[:rows, :heads]


def whole(shape):
    return pl.BlockSpec(shape, lambda *_: (0,) * len(shape))


def call(kernel, name, grid, ins, outs, args, scalars=(), scratch=(), alias=None, more=0):
    grant, time = PLANS[name]
    shapes = [
        pltpu.HBM(out[0], out[1]) if len(out) > 3 else jax.ShapeDtypeStruct(out[0], out[1])
        for out in outs
    ]
    return pl.pallas_call(
        kernel,
        out_shape=shapes,
        grid_spec=pltpu.PrefetchScalarGridSpec(
            num_scalar_prefetch=len(scalars),
            grid=grid,
            in_specs=list(ins),
            out_specs=[out[2] for out in outs],
            scratch_shapes=list(scratch),
        ),
        input_output_aliases=alias or {},
        compiler_params=pltpu.CompilerParams(
            dimension_semantics=("arbitrary",) * len(grid), vmem_limit_bytes=(grant + more) * 2**20
        ),
        cost_estimate=pl.CostEstimate(
            flops=int(time * COVER), bytes_accessed=1, transcendentals=0
        ),
        name=name,
    )(*scalars, *args)


def full(*arrays):
    return [whole(a.shape) for a in arrays]


def bit_orders(bits, last_first):
    low, high = list(range(min(bits, 2))), list(range(2, bits))
    first, second = (low + high[::-1], low[::-1] + high)
    if last_first:
        first, second = (high[::-1] + low, high + low[::-1])
    return [first, second]


def info_table(wide_size, narrow_size, order_pairs):
    bits = wide_size.bit_length() - 1
    rows = []
    for w in range(wide_size):
        for n in range(narrow_size):
            side = n % 2
            row = [w, side, side, w * (narrow_size // 2) + n // 2, n]
            row += [0] * (HEADER - len(row))
            for pair in order_pairs:
                for order in (pair[side], pair[1 - side]):
                    for shard in range(wide_size):
                        apart = shard ^ w
                        slot = [((apart >> bit) & 1) << (bits - 1 - k) for k, bit in enumerate(order)]
                        row.append(sum(slot))
            rows.append(row)
    return np.array(rows, np.int32)


def shards(
    inputs, memory, cotangent, answer_lengths, answer_groups, memory_lengths,
    gain_attn, self_query, self_key, self_value, self_out, bucket_bias_table,
    gain_cross, cross_query, cross_key_matrix, cross_value, cross_out,
    gain_ffn, hidden_gate, hidden_up, hidden_down,
):
    tokens, width = inputs.shape
    answer_lengths, answer_groups = answer_lengths.T, answer_groups.T
    part = memory.shape[0]
    hidden = hidden_gate.shape[1]
    wide_size = lax.axis_size("wide")
    narrow_size = lax.axis_size("narrow")
    wide_index = lax.axis_index("wide")
    narrow_index = lax.axis_index("narrow")
    bits = wide_size.bit_length() - 1
    orders = bit_orders(bits, False)
    orders_last_first = bit_orders(bits, True)
    info = jnp.asarray(info_table(wide_size, narrow_size, (orders, orders_last_first)))
    info = lax.dynamic_slice(
        info, (wide_index * narrow_size + narrow_index, 0), (1, info.shape[1])
    )
    info = info.reshape(-1)
    gains = (gain_attn, gain_cross, gain_ffn)
    turn = [info]

    both = ("wide", "narrow")

    def to_narrow(value, target):
        pairs = [(n, target(n)) for n in range(narrow_size) if target(n) is not None]
        return lax.ppermute(value, "narrow", pairs)

    def to_wide(value, place, order_pair):
        pairs = []
        for w in range(wide_size):
            for n in range(narrow_size):
                partner = w ^ (1 << order_pair[n % 2][place])
                pairs.append((w * narrow_size + n, partner * narrow_size + n))
        return lax.ppermute(value, both, pairs)

    def after(values, *needed):
        return lax.optimization_barrier((tuple(values), needed))[0]

    def now(*values):
        return after(values, *turn) if turn else values

    def run(kernel, name, grid, ins, outs, args, **more):
        found = call(kernel, name, grid, ins, outs, (*now(args[0]), *args[1:]), **more)
        turn[:] = found[:1]
        return found

    class Group:
        def __init__(self, keep, send, order_pair=orders):
            self.pieces, self.place, self.count = [keep], 0, wide_size
            self.order_pair = order_pair
            self.pending = to_narrow(send, lambda n: n ^ 1)

        def total(self, first, count, name="partial_sum"):
            pieces = (*self.pieces, self.pending)
            rows, lanes = pieces[0].shape[1:]
            parts = 2 if count * rows >= 4096 and rows % 32 == 0 else 1
            spec = lambda at: pl.BlockSpec(
                (count, rows // parts, lanes), lambda j: (at, j, 0)
            )
            shape = (count, rows, lanes)
            (found,) = run(
                sum_kernel, name, (parts,), [spec(first)] * len(pieces),
                [(shape, bf16, spec(0))], pieces,
            )
            self.pieces = list(pieces)
            return found

        def step(self, name="partial_sum"):
            self.count //= 2
            sent = self.total(1, self.count, name)
            self.pending = to_wide(sent, self.place, self.order_pair)
            self.place += 1

        def finish(self, name="partial_sum"):
            while self.place < bits:
                self.step()
            total = self.total(0, 1, name)
            step = 2
            while step < narrow_size:
                self.pieces, self.pending = [total], to_narrow(total, lambda n, s=step: n ^ s)
                total = self.total(0, 1)
                step *= 2
            return total[0], to_narrow(total, lambda n: n ^ 1)[0]

    lanes = TOGETHER * PAIR
    steps = (PAIRS // TOGETHER,)
    block = lambda rows: pl.BlockSpec((rows, lanes), lambda j, *_: (0, j))
    out_rows = pl.BlockSpec((lanes, width), lambda j, *_: (j, 0))

    model = (tokens, width)
    square = (width, width)
    in_hbm = pl.BlockSpec(memory_space=pltpu.HBM)
    normed, keys, values, tail, memory_own = run(
        project_kernel, "projections", (1,),
        [whole((width,))] + [in_hbm] * 6,
        [(model, bf16, whole(model))] * 3
        + [((2, REACH, width), bf16, whole((2, REACH, width)))]
        + [((2, part, width), bf16, whole((2, part, width)))],
        (gains[0],)
        + tuple(
            pltpu.with_memory_space_constraint(a, pltpu.HBM)
            for a in (inputs, memory, self_key, self_value, cross_key_matrix, cross_value)
        ),
        scratch=(pltpu.VMEM(model, bf16), pltpu.VMEM((part, width), bf16))
        + (pltpu.VMEM(square, bf16),) * 4
        + (pltpu.SemaphoreType.DMA((6,)),),
    )
    halo = to_narrow(tail, lambda n: n + 1 if n % 2 == 0 else None)
    memory_parts = [memory_own] + [
        to_narrow(memory_own, lambda n, s=shift: (n + s) % narrow_size)
        for shift in range(1, narrow_size)
    ]

    queries, bias = run(
        query_kernel, "queries", (1,),
        [whole(model), in_hbm, whole((HEADS, BUCKETS))],
        [
            (model, bf16, whole(model)),
            ((HEADS * QUERY_BLOCK, WINDOW), f32, whole((HEADS * QUERY_BLOCK, WINDOW))),
        ],
        (normed, pltpu.with_memory_space_constraint(self_query, pltpu.HBM), bucket_bias_table.T),
        scratch=(pltpu.VMEM(square, bf16), pltpu.SemaphoreType.DMA),
    )

    halo_block = pl.BlockSpec((2, REACH, lanes), lambda j, *_: (0, 0, j))
    blocks = tokens // QUERY_BLOCK
    self_probs = pl.BlockSpec(
        (TOGETHER, blocks, 2 * QUERY_BLOCK, WINDOW), lambda j, *_: (j, 0, 0, 0)
    )
    attended, inverse, probs, x1, normed_two, cross_rows = run(
        self_forward_kernel, "self_forward", steps,
        [block(tokens)] * 3 + [halo_block]
        + [pl.BlockSpec((2 * TOGETHER * QUERY_BLOCK, WINDOW), lambda j, *_: (j, 0))]
        + [whole(model), out_rows]
        + full(gains[1], cross_query),
        [
            (model, bf16, block(tokens)),
            (model, f32, block(tokens)),
            ((PAIRS, blocks, 2 * QUERY_BLOCK, WINDOW), bf16, self_probs, "hbm"),
            (model, f32, whole(model)),
            (model, bf16, whole(model)),
            (model, bf16, whole(model)),
        ],
        (queries, keys, values, halo, bias, inputs, self_out, gains[1], cross_query),
        scalars=(info, answer_lengths),
        scratch=(
            pltpu.VMEM((tokens + REACH, lanes), bf16),
            pltpu.VMEM((tokens + REACH, 2 * lanes), bf16),
            pltpu.VMEM((tokens, LANES), jnp.int32),
        ),
    )

    memory_tokens = part * narrow_size
    together = TOGETHER + 1 if memory_tokens <= 2 * CROSS_BLOCK else TOGETHER
    lanes_c = together * PAIR
    block_c = lambda rows: pl.BlockSpec((rows, lanes_c), lambda j, *_: (0, j))
    rows_c = pl.BlockSpec((lanes_c, width), lambda j, *_: (j, 0))
    memory_block = pl.BlockSpec((2, part, lanes_c), lambda j, *_: (0, 0, j))
    cross_blocks = tokens // CROSS_BLOCK
    cross_probs = pl.BlockSpec(
        (together, cross_blocks, 2 * CROSS_BLOCK, memory_tokens), lambda j, *_: (j, 0, 0, 0)
    )
    attended_two, inverse_two, probs_two, x2, normed_three = run(
        functools.partial(cross_forward_kernel, together, narrow_size), "cross_forward", (PAIRS // together,),
        [block_c(tokens), whole(model), rows_c, whole((width,))] + [memory_block] * narrow_size,
        [
            (model, bf16, block_c(tokens)),
            (model, f32, block_c(tokens), "hbm"),
            ((PAIRS, cross_blocks, 2 * CROSS_BLOCK, memory_tokens), bf16, cross_probs, "hbm"),
            (model, f32, whole(model)),
            (model, bf16, whole(model)),
        ],
        (cross_rows, x1, cross_out, gains[2], *memory_parts),
        scalars=(info, answer_lengths, answer_groups, memory_lengths),
        more=memory_tokens // 32 - 8,
        scratch=(
            pltpu.VMEM((memory_tokens, lanes_c), bf16),
            pltpu.VMEM((memory_tokens, 2 * lanes_c), bf16),
            pltpu.VMEM((tokens, LANES), jnp.int32),
            pltpu.VMEM((8, memory_tokens), jnp.int32),
        ),
    )

    probs, inverse_two, probs_two = (
        pltpu.with_memory_space_constraint(a, pltpu.HBM) for a in (probs, inverse_two, probs_two)
    )

    tile = 1024
    wide_tile = pl.BlockSpec((width, tile), lambda j, *_: (0, j))
    token_tile = pl.BlockSpec((tokens, tile), lambda j, *_: (0, j))
    hidden_shape = (tokens, hidden)
    unit, grad_gate, grad_up, layer_out, dx2, e2 = run(
        ffn_kernel, "feed_forward", (hidden // tile,),
        [whole(model)] * 3
        + [whole((width,)), wide_tile, wide_tile]
        + [pl.BlockSpec((tile, width), lambda j, *_: (j, 0))],
        [(hidden_shape, bf16, token_tile)] * 3
        + [
            (model, bf16, whole(model)),
            (model, f32, whole(model)),
            (model, bf16, whole(model)),
        ],
        (normed_three, cotangent, x2, gains[2], hidden_gate, hidden_up, hidden_down),
        scratch=(pltpu.VMEM(model, f32), pltpu.VMEM(model, f32)),
    )

    square_rows = width // wide_size * (width // 2 // LANES)
    gate_rows = width // wide_size * (hidden // 2 // LANES)
    down_rows = hidden // wide_size // 2 * (width // LANES)
    step_rows = gate_rows // 2
    gate_side = lambda flip: pl.BlockSpec(
        (tokens, 256), lambda j, info: (0, (info[1] ^ flip) * (hidden // 512) + j)
    )
    half_side = lambda flip: pl.BlockSpec(
        (tokens, width // 2), lambda j, info: (0, info[1] ^ flip)
    )
    anywhere = pl.BlockSpec(memory_space=pl.ANY)

    gate_shape = (wide_size, 2 * gate_rows, LANES)
    step_spec = pl.BlockSpec((wide_size, step_rows, LANES), lambda j, *_: (0, j, 0))
    keep, send = run(
        functools.partial(gate_up_kernel, wide_size), "gate_up_gradient", (hidden // 512,),
        [whole(model), gate_side(0), gate_side(1), gate_side(0), gate_side(1)],
        [(gate_shape, bf16, step_spec)] * 2,
        (normed_three, grad_gate, grad_gate, grad_up, grad_up),
        scalars=(info,),
        scratch=(pltpu.VMEM((width, tokens), bf16),),
    )
    gate_group = Group(keep, send)
    down_shape = (wide_size, down_rows + square_rows, LANES)
    keep, send = run(
        functools.partial(down_kernel, wide_size), "down_gradient", (1,),
        [whole(hidden_shape), whole(model), whole(model), half_side(0), half_side(1)],
        [(down_shape, bf16, whole(down_shape))] * 2,
        (unit, cotangent, attended_two, e2, e2),
        scalars=(info,),
        scratch=(
            pltpu.VMEM((hidden, tokens), bf16),
            pltpu.VMEM((hidden, width // 2), f32),
        ),
    )
    down_group = Group(keep, send, orders_last_first)
    gate_group.step()

    grad_cross_rows, dx1, e1, *memory_grads = run(
        functools.partial(cross_backward_kernel, together, narrow_size), "cross_backward", (PAIRS // together,),
        [whole(model), rows_c, block_c(tokens), block_c(tokens), cross_probs, block_c(tokens)]
        + [block_c(width), whole(model), whole(model), whole((width,))]
        + [memory_block] * narrow_size,
        [
            (model, bf16, block_c(tokens)),
            (model, f32, whole(model)),
            (model, bf16, whole(model)),
        ]
        + [((2, part, width), bf16, memory_block)] * narrow_size,
        (e2, cross_out, attended_two, inverse_two, probs_two, cross_rows, cross_query, x1, dx2)
        + (gains[1], *memory_parts),
        scratch=(
            pltpu.VMEM((memory_tokens, lanes_c), bf16),
            pltpu.VMEM((memory_tokens, lanes_c), bf16),
            pltpu.VMEM((lanes_c, memory_tokens), f32),
            pltpu.VMEM((lanes_c, memory_tokens), f32),
            pltpu.VMEM(model, f32),
        ),
        more=memory_tokens // 32 - 8,
    )
    memory_shares = [memory_grads[0]] + [
        to_narrow(memory_grads[shift], lambda n, s=shift: (n - s) % narrow_size)
        for shift in range(1, narrow_size)
    ]
    down_group.step()
    second_shape = (wide_size, 4 * square_rows, LANES)
    couple = ((normed_two, grad_cross_rows), (attended, e1))
    second_spec = pl.BlockSpec((wide_size, 2 * square_rows, LANES), lambda j, *_: (0, 0, 0))
    keep, send = run(
        functools.partial(square_kernel, wide_size, 2), "square_gradients", (1,),
        [whole(model), half_side(0), half_side(1)] * 2,
        [(second_shape, bf16, second_spec)] * 2,
        [side_of for left, right in couple for side_of in (left, right, right)],
        scalars=(info,),
    )
    memory_spec = pl.BlockSpec((wide_size, square_rows, LANES), lambda j, *_: (0, 2 + j, 0))
    keep, send, memory_grad = run(
        functools.partial(memory_back_kernel, narrow_size, wide_size), "memory_backward", (2,),
        full(memory, cross_key_matrix, cross_value, *memory_shares) + [anywhere] * 2,
        [(second_shape, bf16, memory_spec)] * 2
        + [((part, width), f32, whole((part, width)))],
        (memory, cross_key_matrix, cross_value, *memory_shares, keep, send),
        scalars=(info,),
        scratch=(
            pltpu.VMEM((width, width), f32),
            pltpu.VMEM((part, width), bf16),
            pltpu.VMEM((width, part), bf16),
        ),
        alias={4 + narrow_size: 0, 5 + narrow_size: 1},
    )
    second_group = Group(keep, send)
    gate_group.step()

    tables, carried, parts_of = [], [], PAIRS // TOGETHER
    for index in range(parts_of):
        at = lambda rows, i=index: pl.BlockSpec((rows, lanes), lambda *_: (0, i))
        halo_at = pl.BlockSpec((2, REACH, lanes), lambda *_, i=index: (0, 0, i))
        out_at = pl.BlockSpec((lanes, width), lambda *_, i=index: (i, 0))
        if index == 1:
            second_group.step()
        if index == 2:
            gate_group.step()
            down_group.step()
        *carried, table = run(
            functools.partial(self_backward_kernel, index * TOGETHER),
            "self_backward" if index else "self_backward_first", (1,),
            [whole(model), out_at, at(tokens), at(tokens), in_hbm]
            + [at(tokens)] * 3 + [halo_at] + [anywhere] * len(carried),
            [
                (model, bf16, at(tokens)),
                (model, f32, at(tokens)),
                (model, f32, at(tokens)),
                ((2, REACH, width), bf16, halo_at),
                ((BUCKETS, HEADS), f32, whole((BUCKETS, HEADS))),
            ],
            (e1, self_out, attended, inverse, probs, queries, keys, values, halo, *carried),
            scratch=(
                pltpu.VMEM((tokens + REACH, lanes), bf16),
                pltpu.VMEM((tokens + REACH, lanes), bf16),
                pltpu.VMEM((lanes, tokens + REACH), f32),
                pltpu.VMEM((lanes, tokens + REACH), f32),
                pltpu.VMEM((TOGETHER, 2 * QUERY_BLOCK, 2 * QUERY_BLOCK), f32),
                pltpu.VMEM((16, 2 * QUERY_BLOCK), f32),
                pltpu.VMEM((TOGETHER, blocks, 2 * QUERY_BLOCK, WINDOW), bf16),
                pltpu.SemaphoreType.DMA,
            ),
            alias={9 + i: i for i in range(4)} if index else None,
        )
        tables.append(table)
    grad_queries, grad_keys, grad_values, back = carried
    returned = to_narrow(back, lambda n: n - 1 if n % 2 == 1 else None)
    second_group.step()
    query_shape = (wide_size, square_rows + 16, LANES)
    last_shape = (wide_size, 3 * square_rows + 16, LANES)
    query_keep, query_send = run(
        functools.partial(query_gradient_kernel, wide_size), "query_gradient", (1,),
        [whole(model), half_side(0), half_side(1)] + [whole((BUCKETS, HEADS))] * parts_of,
        [(query_shape, bf16, whole(query_shape))] * 2,
        (normed, grad_queries, grad_queries, *tables),
        scalars=(info,),
    )
    keep, send, keys_low, values_low = run(
        functools.partial(keys_values_kernel, wide_size), "key_value_gradient", (1,),
        full(normed, grad_keys, grad_values, returned, query_keep, query_send),
        [(last_shape, bf16, whole(last_shape))] * 2 + [(model, bf16, whole(model))] * 2,
        (normed, grad_keys, grad_values, returned, query_keep, query_send),
        scalars=(info,),
        scratch=(pltpu.VMEM(square, f32),),
    )
    last_group = Group(keep, send)
    down_group.step("partial_sum_beside")
    gate_group.step()
    second_group.step()
    last_group.step()
    (input_grad,) = run(
        input_kernel, "input_gradient", (1,),
        full(grad_queries, keys_low, values_low)
        + full(self_query, self_key, self_value, inputs, dx1, gains[0]),
        [(model, f32, whole(model))],
        (grad_queries, keys_low, values_low)
        + (self_query, self_key, self_value, inputs, dx1, gains[0]),
    )

    square_out = ((width // wide_size, width), f32, whole((width // wide_size, width)))
    gate_out = ((width // wide_size, hidden), f32, whole((width // wide_size, hidden)))
    down_out = ((hidden // wide_size, width), f32, whole((hidden // wide_size, width)))
    size = width // wide_size
    gain_out = ((size,), f32, whole((size,)))
    own_rows = lambda columns: pl.BlockSpec((size, columns), lambda j, info: (info[0], 0))
    gate_own, gate_other = gate_group.finish()
    last_group.step()
    grad_gate_w, grad_up_w, grad_gain_ffn = run(
        gate_unpack_kernel, "gate_outputs", (1,),
        full(gate_own, gate_other) + [own_rows(hidden)] * 2 + [whole((width,))],
        [gate_out] * 2 + [gain_out],
        (gate_own, gate_other, hidden_gate, hidden_up, gain_ffn), scalars=(info,),
    )
    last_group.step("partial_sum_late")
    down_group.step("partial_sum_late")
    second_group.step("partial_sum_late")
    down_own, down_other = down_group.finish("partial_sum_late")
    second_own, second_other = second_group.finish("partial_sum_late")
    grad_down_w, grad_cross_out = run(
        down_unpack_kernel, "down_outputs", (1,), full(down_own, down_other),
        [down_out, square_out], (down_own, down_other), scalars=(info,),
    )
    last_group.step("partial_sum_late")
    (
        grad_cross_query, grad_self_out, grad_cross_key, grad_cross_value, grad_gain_cross,
    ) = run(
        functools.partial(square_unpack_kernel, (0,)), "second_outputs", (1,),
        full(second_own, second_other) + [own_rows(width), whole((width,))],
        [square_out] * 4 + [gain_out],
        (second_own, second_other, cross_query, gain_cross), scalars=(info,),
    )
    last_own, last_other = last_group.finish("partial_sum_late")
    table_out = ((BUCKETS // wide_size, HEADS), f32, whole((BUCKETS // wide_size, HEADS)))
    grad_self_key, grad_self_value, grad_self_query, grad_table, grad_gain_attn = run(
        last_unpack_kernel, "last_outputs", (1,),
        full(last_own, last_other) + [own_rows(width)] * 3 + [whole((width,))],
        [square_out] * 3 + [table_out, gain_out],
        (last_own, last_other, self_key, self_value, self_query, gain_attn), scalars=(info,),
    )
    return (
        layer_out,
        input_grad,
        memory_grad,
        grad_gain_attn,
        grad_self_query,
        grad_self_key,
        grad_self_value,
        grad_self_out,
        grad_table,
        grad_gain_cross,
        grad_cross_query,
        grad_cross_key,
        grad_cross_value,
        grad_cross_out,
        grad_gain_ffn,
        grad_gate_w,
        grad_up_w,
        grad_down_w,
    )


def solution(mesh):
    rows = P(("wide", "narrow"), None)
    vector, matrix = P("wide"), P("wide", None)
    return jax.shard_map(
        shards,
        mesh=mesh,
        in_specs=(rows,) * 3 + (P(),) * 18,
        out_specs=(rows,) * 3
        + (vector,)
        + (matrix,) * 5
        + (vector,)
        + (matrix,) * 4
        + (vector,)
        + (matrix,) * 3,
        check_vma=False,
    )
```
